512 devices in a mesh: row: 32 (over y, x, core), col: 16 (over z).
Axes of the slice: x: 4, y: 4, z: 16, core: 2. Of those that a mesh axis runs over, the one named last changes fastest.
Arguments:
- noise: bfloat16 [16384, 128], P('row'), may hold values from -6 to 6
- w_first: bfloat16 [128, 512], replicated, may hold values from -0.5 to 0.5
- w_second: bfloat16 [512, 1024], replicated, may hold values from -0.25 to 0.25
- history: bfloat16 [16384, 1024], P('col'), may hold values from -4 to 4
Outputs:
- grad_first: float32 [128, 512], replicated
- grad_second: float32 [512, 1024], P(None, 'col')
The draws below stay inside these ranges and needn't reach their ends.
All inputs are finite; a program needn't handle non-finite values.
Results may differ from the reference program's by a relative error of at most 0.00085.
Values sent between devices are 32-bit elements; how exact they have to be, the bound alone decides.
A program may use at most 64 MiB of HBM per device.

```python
import math
import jax
import jax.numpy as jnp
from jax import lax

G = 1024
HID = 512
ZD = 128
SWEEPS = 3
NG = 16384
NH = 16384


def block_scale(own_key, shape, shards, least, top_value):
    def one(dim, shards_of):
        draws = jax.random.uniform(jax.random.fold_in(jax.random.fold_in(own_key, 6), dim), (shards_of,), jnp.float32, least / len(shards), top_value / len(shards))
        return jnp.repeat(jnp.exp(draws), shape[dim] // shards_of).reshape((-1,) + (1,) * (len(shape) - dim - 1))

    factor_of = one(*shards[0])
    for cut in shards[1:]:
        factor_of = factor_of * one(*cut)
    return factor_of


def scatter_about(rng, dims, scale, reach, shards=(), kind=jnp.bfloat16):
    level = block_scale(rng, dims, shards, -0.22, 0.18) if shards else 1.0
    drawn = jax.random.normal(rng, dims, jnp.float32) * scale * level
    return jnp.minimum(jnp.maximum(drawn, -reach), reach).astype(kind)


def setup_inputs(seed: int = 0) -> dict:
    splits = jax.random.split(jax.random.key(seed), 5)
    noise = scatter_about(splits[0], (NG, ZD), 1.0, 6.0, ((0, 32),))
    w_first = scatter_about(splits[1], (ZD, HID), ZD ** -0.5, 0.5)
    w_second = scatter_about(splits[2], (HID, G), HID ** -0.5, 0.25)
    history = scatter_about(splits[3], (NH, G), 0.5, 4.0, ((0, 16),))
    return dict(noise=noise, w_first=w_first, w_second=w_second, history=history)


EPSILON = 0.01

def reference(noise, w_first, w_second, history):
    preact = jnp.dot(noise, w_first, preferred_element_type=jnp.float32)
    hidden = jax.nn.silu(preact).astype(jnp.bfloat16)
    surface = jnp.dot(hidden, w_second, preferred_element_type=jnp.float32).astype(jnp.bfloat16)
    surf_f = surface.astype(jnp.float32)
    hist_f = history.astype(jnp.float32)
    surf_sq = lax.optimization_barrier(jnp.sum(surf_f * surf_f, axis=1))
    hist_sq = lax.optimization_barrier(jnp.sum(hist_f * hist_f, axis=1))
    block = min(1024, NG)
    surf_blocks = surface.reshape(NG // block, block, G)
    sq_blocks = surf_sq.reshape(NG // block, block)

    def cost_block(pair):
        rows, squares = pair
        inner = lax.dot_general(rows, history, (((1,), (1,)), ((), ())), preferred_element_type=jnp.float32)
        return (squares[:, None] + hist_sq[None, :] - 2.0 * inner) / G
    cost = lax.map(cost_block, (surf_blocks, sq_blocks)).reshape(NG, NH)
    f_pot = jnp.zeros((NG,), jnp.float32)
    g_pot = jnp.zeros((NH,), jnp.float32)
    for sweep_no in range(SWEEPS):
        g_pot = -EPSILON * (-math.log(NG) + jax.nn.logsumexp((f_pot[:, None] - cost) / EPSILON, axis=0))
        f_pot = -EPSILON * (-math.log(NH) + jax.nn.logsumexp((g_pot[None, :] - cost) / EPSILON, axis=1))
    weights = (jnp.exp((f_pot[:, None] + g_pot[None, :] - cost) / EPSILON) / NH).astype(jnp.bfloat16)
    barycentre = jnp.dot(weights, history, preferred_element_type=jnp.float32)
    d_surface = ((surf_f - barycentre) * (1.0 / math.sqrt(NG))).astype(jnp.bfloat16)
    d_hidden = lax.dot_general(d_surface, w_second, (((1,), (1,)), ((), ())), preferred_element_type=jnp.float32)
    sigma = jax.nn.sigmoid(preact)
    d_preact = (d_hidden * sigma * (1.0 + preact * (1.0 - sigma))).astype(jnp.bfloat16)
    grad_first = lax.dot_general(noise, d_preact, (((0,), (0,)), ((), ())), preferred_element_type=jnp.float32)
    grad_second = lax.dot_general(hidden, d_surface, (((0,), (0,)), ((), ())), preferred_element_type=jnp.float32)
    return (grad_first, grad_second)
```

```python
import functools
import math
from types import SimpleNamespace

import jax
import jax.numpy as jnp
from jax import lax
from jax.experimental import pallas as pl
from jax.experimental.pallas import tpu as pltpu
from jax.sharding import PartitionSpec as P

SWEEPS = 3
EPSILON = 0.01
MESH = pl.DeviceIdType.MESH
F32 = jnp.float32
BF16 = jnp.bfloat16
LANES = 128
CHUNK = 32


def kernel(geometry, names, noise, w_first, w_second, history, out_first, out_second, *scratch):
    ny, nx, nz = geometry
    chips = ny * nx
    n_row, n_col = 2 * chips, nz
    s = SimpleNamespace(**dict(zip(names, scratch)))
    sem = scratch[-1]
    gen, zdim = noise.shape
    hist, width = history.shape
    hid = w_first.shape[1]
    half = hid // 2
    quarter = half // 2
    gen_total, hist_total = gen * n_row, hist * n_col
    scale = 1.0 / math.sqrt(gen_total)

    me = lax.axis_index("row")
    z = lax.axis_index("col")
    core = lax.rem(me, 2)
    other = 1 - core
    chip = me // 2
    x = lax.rem(chip, nx)
    y = chip // nx
    odd = lax.rem(z, 2) == 1

    barrier = pltpu.get_barrier_semaphore()

    def greet_row(k, c):
        pl.semaphore_signal(barrier, inc=1, device_id=(lax.rem(me + k, n_row), z), device_id_type=MESH)
        return c

    def greet_col(k, c):
        pl.semaphore_signal(barrier, inc=1, device_id=(me, lax.rem(z + k, n_col)), device_id_type=MESH)
        return c

    lax.fori_loop(1, n_row, greet_row, 0)
    lax.fori_loop(1, n_col, greet_col, 0)

    def start(src, dst, number, device):
        pltpu.make_async_remote_copy(
            src_ref=src, dst_ref=dst, send_sem=sem.at[2 * number], recv_sem=sem.at[2 * number + 1],
            device_id=device, device_id_type=MESH,
        ).start()

    def wait_bytes(like, index):
        pltpu.make_async_copy(like, like, sem.at[index]).wait()

    pending = []

    def arrived(number, *like):
        for part in like:
            wait_bytes(part, 2 * number + 1)
        pending.append((number, like))

    def to_row(src, dst, number):
        def step(k, c):
            start(src, dst.at[k - 1], number, (lax.rem(me + k, n_row), z))
            return c
        lax.fori_loop(1, n_row, step, 0)

    def to_col(src, dst, number):
        def step(k, c):
            start(src, dst.at[k - 1], number, (me, lax.rem(z + k, n_col)))
            return c
        lax.fori_loop(1, n_col, step, 0)

    def at(offset, size, unit):
        return pl.ds(pl.multiple_of(offset, unit), size)

    def each(count, body):
        lax.fori_loop(0, count, lambda k, c: (body(k), c)[1], 0)

    def wide(v, copies):
        return jnp.concatenate([v] * copies, axis=1)

    def eye():
        return lax.broadcasted_iota(jnp.int32, (LANES, LANES), 0) == lax.broadcasted_iota(
            jnp.int32, (LANES, LANES), 1)

    def rows_from_line(line, dst):
        for k in range(dst.shape[0]):
            dst[k:k + 1, :] = line[:, k * LANES:(k + 1) * LANES]

    def line_from_rows(rows):
        return jnp.concatenate([rows[k:k + 1, :] for k in range(rows.shape[0])], axis=1)

    def rows_from_column(column, dst):
        for k in range(dst.shape[0]):
            block = column[k * LANES:(k + 1) * LANES, :]
            dst[k:k + 1, :] = jnp.sum(jnp.where(eye(), block, 0.0), axis=0, keepdims=True)

    def column_from_rows(rows, column):
        for k in range(rows.shape[0]):
            block = jnp.where(eye(), jnp.broadcast_to(rows[k:k + 1, :], (LANES, LANES)), 0.0)
            column[k * LANES:(k + 1) * LANES, :] = jnp.broadcast_to(
                jnp.sum(block, axis=1, keepdims=True), (LANES, LANES))

    def dot(a, b):
        return jnp.dot(a, b, preferred_element_type=F32)

    def dot_t(a, b):
        return lax.dot_general(a, b, (((1,), (1,)), ((), ())), preferred_element_type=F32)

    tile_h = min(256, hid)
    tile_g = min(256, width)
    tile_j = min(256, hist)

    s.noise_t[...] = jnp.transpose(noise[...].astype(F32)).astype(BF16)
    for n in range(hid // tile_h):
        cols = slice(n * tile_h, (n + 1) * tile_h)
        preact = dot(noise[...], w_first[:, cols])
        sigma = 1.0 / (1.0 + jnp.exp(-preact))
        hidden = preact * sigma
        s.hidden[:, cols] = hidden.astype(BF16)
        s.mult[:, cols] = sigma * (1.0 + preact * (1.0 - sigma))

    def surface_tile(n):
        cols = at(n * tile_g, tile_g, tile_g)
        s.surface[:, cols] = dot(s.hidden[...], w_second[:, cols]).astype(BF16)
    each(width // tile_g, surface_tile)

    def surf_squares(k):
        rows = at(k * CHUNK, CHUNK, CHUNK)
        v = s.surface[rows, :].astype(F32)
        total = jnp.sum(v * v, axis=1, keepdims=True)
        s.surf_sq[rows, :] = jnp.broadcast_to(total, (CHUNK, LANES))
    each(gen // CHUNK, surf_squares)

    def hist_squares(k):
        rows = at(k * LANES, LANES, LANES)
        v = history[rows, :].astype(F32)
        total = jnp.sum(v * v, axis=1, keepdims=True)
        block = jnp.where(eye(), jnp.broadcast_to(total, (LANES, LANES)), 0.0)
        s.hist_sq[:, rows] = jnp.sum(block, axis=0, keepdims=True)
    each(hist // LANES, hist_squares)

    def cost_tile(n):
        cols = at(n * tile_j, tile_j, tile_j)
        inner = dot_t(s.surface[...], history[cols, :])
        cost = (wide(s.surf_sq[...], tile_j // LANES) + s.hist_sq[:, cols] - 2.0 * inner) / width
        scores = -cost / EPSILON
        s.plan[:, cols] = scores
        top = jnp.max(scores, axis=0, keepdims=True)
        s.col_a[:, cols] = top
        s.col_b[:, cols] = jnp.sum(jnp.exp(scores - top), axis=0, keepdims=True)
    each(hist // tile_j, cost_tile)

    rows_from_line(s.col_a[...], s.m_pair.at[0])
    rows_from_line(s.col_b[...], s.m_pair.at[1])

    pl.semaphore_wait(barrier, n_row - 1 + n_col - 1)
    to_row(s.m_pair, s.m_pair_in, 0)

    def hist_w_tile(n):
        rows = at(n * 256, min(256, hist), min(256, hist))
        prod = dot_t(history[rows, :], w_second[...])
        hi = prod.astype(BF16)
        s.hist_w_hi[rows, :] = hi
        s.hist_w_lo[rows, :] = (prod - hi.astype(F32)).astype(BF16)
    each(hist // min(256, hist), hist_w_tile)

    arrived(0, s.m_pair_in)
    tops, sums = s.m_pair_in[:, 0], s.m_pair_in[:, 1]
    top = jnp.maximum(jnp.max(tops, axis=0), s.m_pair[0])
    total = jnp.sum(sums * jnp.exp(tops - top[None]), axis=0)
    total = total + s.m_pair[1] * jnp.exp(s.m_pair[0] - top)
    s.m_row[0] = math.log(gen_total) - (top + jnp.log(total))
    s.col_a[...] = line_from_rows(s.m_row[0])

    def first_rows(k):
        rows = at(k * CHUNK, CHUNK, CHUNK)
        scores = s.plan[rows, :] + s.col_a[...]
        top = jnp.max(scores, axis=1, keepdims=True)
        grown = jnp.exp(scores - top)
        s.plan[rows, :] = grown
        s.row_a[rows, :] = jnp.broadcast_to(top, (CHUNK, LANES))
        s.row_b[rows, :] = jnp.broadcast_to(jnp.sum(grown, axis=1, keepdims=True), (CHUNK, LANES))
    each(gen // CHUNK, first_rows)
    blocks = gen // LANES
    rows_from_column(s.row_a, s.m_col0.at[0])
    rows_from_column(s.row_b, s.m_col0.at[1])
    to_col(s.m_col0, s.m_col0_in, 1)

    def surf_w_tile(n):
        cols = at(n * tile_h, tile_h, tile_h)
        s.surf_w[:, cols] = dot_t(s.surface[...], w_second[cols, :])
    each(hid // tile_h, surf_w_tile)
    s.hidden_t[...] = jnp.transpose(s.hidden[...].astype(F32)).astype(BF16)

    arrived(1, s.m_col0_in)
    tops, sums = s.m_col0_in[:, 0], s.m_col0_in[:, 1]
    top = jnp.maximum(jnp.max(tops, axis=0), s.m_col0[0])
    total = jnp.sum(sums * jnp.exp(tops - top[None]), axis=0)
    total = total + s.m_col0[1] * jnp.exp(s.m_col0[0] - top)
    column_from_rows(jnp.exp(s.m_col0[0] - top) / total, s.row_a)

    def column_sums(scaled):
        def step(k, acc):
            rows = at(k * CHUNK, CHUNK, CHUNK)
            v = s.plan[rows, :] * wide(s.row_a[rows, :], hist // LANES)
            if scaled:
                s.plan[rows, :] = v
            return acc + jnp.sum(v.reshape(CHUNK // 8, 8, hist), axis=0)
        acc = lax.fori_loop(0, gen // CHUNK, step, jnp.zeros((8, hist), F32))
        return jnp.sum(acc, axis=0, keepdims=True)

    def row_sums(k):
        rows = at(k * CHUNK, CHUNK, CHUNK)
        v = jnp.sum(s.plan[rows, :] * s.col_a[...], axis=1, keepdims=True)
        s.row_b[rows, :] = jnp.broadcast_to(v, (CHUNK, LANES))

    for sweep in range(1, SWEEPS):
        number = 2 * sweep
        mine, theirs = s.m_row.at[sweep], s.m_row_in.at[sweep - 1]
        rows_from_line(column_sums(sweep == 1), mine)
        to_row(mine, theirs, number)
        if sweep == 1:
            pair = at(lax.div(z, 2) * LANES, LANES, LANES)
            prod = dot(s.hidden_t[...], s.surface[:, pair])
            turned = pltpu.roll(prod, 64, axis=1)
            s.term_a[...] = jnp.where(odd, turned, prod)
            s.term_b[...] = jnp.where(odd, prod, turned)
            low = lax.broadcasted_iota(jnp.int32, (8, LANES), 1) < 64

            def owner_term(o):
                oc, ox, oy = lax.rem(o, 2), lax.rem(o // 2, nx), o // (2 * nx)
                upper = oc * half + ox * (quarter // nx) + oy * 8
                lower = oc * half + quarter + oy * (quarter // ny) + ox * 8
                s.term[o] = jnp.where(
                    low, s.term_a[at(upper, 8, 8), :], s.term_b[at(lower, 8, 8), :])
            each(n_row, owner_term)

            def send_term(k, c):
                peer = lax.rem(me + k, n_row)
                start(s.term.at[peer], s.term_in.at[k - 1], 6, (peer, z))
                return c
            lax.fori_loop(1, n_row, send_term, 0)
        arrived(number, theirs)
        total = mine[...] + jnp.sum(theirs[...], axis=0)
        s.col_a[...] = line_from_rows((gen_total / hist_total) / total)

        each(gen // CHUNK, row_sums)
        mine, theirs = s.m_col.at[sweep - 1], s.m_col_in.at[sweep - 1]
        rows_from_column(s.row_b, mine)
        to_col(mine, theirs, number + 1)
        arrived(number + 1, theirs)
        total = mine[...] + jnp.sum(theirs[...], axis=0)
        column_from_rows(1.0 / total, s.row_a)

    def weight_rows(k):
        rows = at(k * CHUNK, CHUNK, CHUNK)
        v = s.plan[rows, :] * wide(s.row_a[rows, :], hist // LANES) * s.col_a[...]
        s.weights[rows, :] = v.astype(BF16)
    each(gen // CHUNK, weight_rows)

    def acc_tile(which):
        rows = at(which * half, half, half)

        def body(n):
            cols = at(n * tile_j, tile_j, tile_j)
            s.acc[rows, cols] = dot(s.hidden_t[rows, :], s.weights[:, cols])
        each(hist // tile_j, body)

    sibling = (me + 1 - 2 * core, z)
    acc_tile(other)
    start(s.acc.at[at(other * half, half, half), :], s.acc_in, 7, sibling)
    acc_tile(core)

    def first_tile(n):
        cols = at(n * tile_h, tile_h, tile_h)
        value = dot(s.weights[...], s.hist_w_hi[:, cols]) + dot(s.weights[...], s.hist_w_lo[:, cols])
        d_hidden = (s.surf_w[:, cols] * (1.0 / n_col) - value) * scale
        d_preact = d_hidden * s.mult[:, cols]
        hi = d_preact.astype(BF16)
        lo = (d_preact - hi.astype(F32)).astype(BF16)
        s.first[:, cols] = dot(s.noise_t[...], hi) + dot(s.noise_t[...], lo)
    each(hid // tile_h, first_tile)
    start(s.first.at[:, at(other * half, half, half)], s.first_in, 8, sibling)

    arrived(7, s.acc_in)

    def add_sibling(k):
        rows = at(core * half + k * CHUNK, CHUNK, CHUNK)
        s.acc[rows, :] = s.acc[rows, :] + s.acc_in[at(k * CHUNK, CHUNK, CHUNK), :]
    each(half // CHUNK, add_sibling)
    span_x, span_y = quarter // nx, quarter // ny
    base_u, base_l = core * half, core * half + quarter
    for k in range(1, nx):
        to = lax.rem(x + k, nx)
        start(s.acc.at[at(base_u + to * span_x, span_x, 8), :], s.x_in.at[k - 1], 9,
              ((y * nx + to) * 2 + core, z))
    for k in range(1, ny):
        to = lax.rem(y + k, ny)
        start(s.acc.at[at(base_l + to * span_y, span_y, 8), :], s.y_in.at[k - 1], 10,
              ((to * nx + x) * 2 + core, z))

    arrived(8, s.first_in)
    s.first_half[...] = s.first[:, at(core * half, half, half)] + s.first_in[...]
    piece = zdim // chips

    def send_first(k, c):
        to = lax.rem(chip + k, chips)
        start(s.first_half.at[at(to * piece, piece, 8), :], s.first_chip_in.at[k - 1], 11,
              (to * 2 + core, z))
        return c
    lax.fori_loop(1, chips, send_first, 0)
    arrived(11, s.first_chip_in)
    s.first_piece[0] = s.first_half[at(chip * piece, piece, 8), :] + jnp.sum(s.first_chip_in[...], axis=0)
    to_col(s.first_piece.at[0], s.first_z_in, 12)

    arrived(9, s.x_in)
    arrived(10, s.y_in)
    rows_u, rows_l = at(base_u + x * span_x, span_x, 8), at(base_l + y * span_y, span_y, 8)
    s.acc[rows_u, :] = s.acc[rows_u, :] + jnp.sum(s.x_in[...], axis=0)
    s.acc[rows_l, :] = s.acc[rows_l, :] + jnp.sum(s.y_in[...], axis=0)
    for k in range(1, ny):
        to = lax.rem(y + k, ny)
        start(s.acc.at[at(base_u + x * span_x + to * 8, 8, 8), :], s.y_in2.at[k - 1], 13,
              ((to * nx + x) * 2 + core, z))
    for k in range(1, nx):
        to = lax.rem(x + k, nx)
        start(s.acc.at[at(base_l + y * span_y + to * 8, 8, 8), :], s.x_in2.at[k - 1], 14,
              ((y * nx + to) * 2 + core, z))
    arrived(13, s.y_in2)
    arrived(14, s.x_in2)
    mine_u, mine_l = base_u + x * span_x + y * 8, base_l + y * span_y + x * 8
    s.reduced[0:8, :] = s.acc[at(mine_u, 8, 8), :] + jnp.sum(s.y_in2[...], axis=0)
    s.reduced[8:16, :] = s.acc[at(mine_l, 8, 8), :] + jnp.sum(s.x_in2[...], axis=0)

    hi = s.reduced[...].astype(BF16)
    lo = (s.reduced[...] - hi.astype(F32)).astype(BF16)
    both = jnp.concatenate([hi, lo], axis=0)

    def mix_tile(n):
        cols = at(n * tile_g, tile_g, tile_g)
        prod = dot(both, history[:, cols])
        s.mix[:, cols] = prod[0:16] + prod[16:32]
    each(width // tile_g, mix_tile)
    low = lax.broadcasted_iota(jnp.int32, (8, LANES), 1) < 64
    for k in range(nz):
        lanes = slice((k // 2) * LANES, (k // 2 + 1) * LANES)
        upper, lower = s.mix[0:8, lanes], s.mix[8:16, lanes]
        if k % 2 == 0:
            s.slices[k] = jnp.where(low, upper, pltpu.roll(lower, 64, axis=1))
        else:
            s.slices[k] = jnp.where(low, pltpu.roll(upper, 64, axis=1), lower)

    def send_slice(k, c):
        to = lax.rem(z + k, n_col)
        start(s.slices.at[to], s.slices_in.at[k - 1], 15, (me, to))
        return c
    lax.fori_loop(1, n_col, send_slice, 0)

    arrived(12, s.first_z_in)
    s.first_all[core, chip] = s.first_piece[0] + jnp.sum(s.first_z_in[...], axis=0)

    def spread(array, number):
        def step(k, c):
            start(array.at[core, chip], array.at[core, chip], number, (lax.rem(chip + k, chips) * 2 + core, z))
            return c
        lax.fori_loop(1, chips, step, 0)
    spread(s.first_all, 16)

    arrived(6, s.term_in)
    term = s.term[me] + jnp.sum(s.term_in[...], axis=0)
    arrived(15, s.slices_in)
    mixed = s.slices[z] + jnp.sum(s.slices_in[...], axis=0)
    s.second_all[core, chip] = (term - mixed) * scale
    spread(s.second_all, 17)

    arrived(16, s.first_all.at[0, pl.ds(0, chips - 1)])
    start(s.first_all.at[core], s.first_all.at[core], 18, sibling)
    arrived(17, s.second_all.at[0, pl.ds(0, chips - 1)])
    start(s.second_all.at[core], s.second_all.at[core], 19, sibling)
    arrived(18, s.first_all.at[0])
    arrived(19, s.second_all.at[0])

    def place_chip(k):
        for c in range(2):
            out_first[at(k * piece, piece, 8), c * half:(c + 1) * half] = s.first_all[c, k]
            cx, cy = lax.rem(k, nx), k // nx
            v = s.second_all[c, k]
            out_second[at(c * half + cx * span_x + cy * 8, 8, 8), :] = v[:, 0:64]
            out_second[at(c * half + quarter + cy * span_y + cx * 8, 8, 8), :] = pltpu.roll(v, 64, axis=1)[:, 0:64]
    each(chips, place_chip)

    for number, like in pending:
        for part in like:
            wait_bytes(part, 2 * number)


def shards(geometry, noise, w_first, w_second, history):
    ny, nx, nz = geometry
    chips = ny * nx
    n_row = 2 * chips
    gen, zdim = noise.shape
    hist, width = history.shape
    hid = w_first.shape[1]
    half, quarter = hid // 2, hid // 4
    piece = zdim // chips
    jr, ir = hist // LANES, gen // LANES
    shapes = dict(
        hidden=((gen, hid), BF16), hidden_t=((hid, gen), BF16), noise_t=((zdim, gen), BF16),
        surface=((gen, width), BF16), mult=((gen, hid), F32), surf_w=((gen, hid), F32),
        hist_w_hi=((hist, hid), BF16), hist_w_lo=((hist, hid), BF16),
        plan=((gen, hist), F32), weights=((gen, hist), BF16),
        surf_sq=((gen, LANES), F32), hist_sq=((1, hist), F32),
        row_a=((gen, LANES), F32), row_b=((gen, LANES), F32), col_a=((1, hist), F32), col_b=((1, hist), F32),
        row_col=((8, LANES), F32), row_sum=((8, LANES), F32),
        m_pair=((2, jr, LANES), F32), m_pair_in=((n_row - 1, 2, jr, LANES), F32),
        m_col0=((2, ir, LANES), F32), m_col0_in=((nz - 1, 2, ir, LANES), F32),
        m_row=((SWEEPS, jr, LANES), F32), m_row_in=((SWEEPS - 1, n_row - 1, jr, LANES), F32),
        m_col=((SWEEPS - 1, ir, LANES), F32), m_col_in=((SWEEPS - 1, nz - 1, ir, LANES), F32),
        acc=((hid, hist), F32), acc_in=((half, hist), F32),
        x_in=((nx - 1, quarter // nx, hist), F32), y_in=((ny - 1, quarter // ny, hist), F32),
        x_in2=((nx - 1, 8, hist), F32), y_in2=((ny - 1, 8, hist), F32), reduced=((16, hist), F32),
        first=((zdim, hid), F32), first_in=((zdim, half), F32), first_half=((zdim, half), F32),
        first_chip_in=((chips - 1, piece, half), F32), first_piece=((1, piece, half), F32),
        first_z_in=((nz - 1, piece, half), F32), first_all=((2, chips, piece, half), F32),
        term_a=((hid, LANES), F32), term_b=((hid, LANES), F32),
        term=((n_row, 8, LANES), F32), term_in=((n_row - 1, 8, LANES), F32),
        mix=((16, width), F32), slices=((nz, 8, LANES), F32), slices_in=((nz - 1, 8, LANES), F32),
        second_all=((2, chips, 8, LANES), F32),
    )
    scratch = [pltpu.VMEM(*shape) for shape in shapes.values()] + [pltpu.SemaphoreType.DMA((40,))]
    slice_width = width // nz
    return pl.pallas_call(
        functools.partial(kernel, geometry, tuple(shapes)),
        out_shape=(
            jax.ShapeDtypeStruct((zdim, hid), F32),
            jax.ShapeDtypeStruct((hid, slice_width), F32),
        ),
        in_specs=[pl.BlockSpec(memory_space=pltpu.VMEM)] * 4,
        out_specs=(pl.BlockSpec(memory_space=pltpu.VMEM),) * 2,
        scratch_shapes=scratch,
        compiler_params=pltpu.CompilerParams(
            collective_id=0, has_side_effects=True, vmem_limit_bytes=56 * 1024 * 1024
        ),
        name="transport",
    )(noise, w_first, w_second, history)


def solution(mesh):
    chips = mesh.shape["row"] // 2
    nx = math.isqrt(chips)
    geometry = (chips // nx, nx, mesh.shape["col"])
    placed = (P("row", None), P(), P(), P("col", None))
    return jax.shard_map(
        functools.partial(shards, geometry), mesh=mesh, in_specs=placed,
        out_specs=(P(), P(None, "col")), check_vma=False,
    )
```

```python
import functools
import math
from types import SimpleNamespace

import jax
import jax.numpy as jnp
from jax import lax
from jax.experimental import pallas as pl
from jax.experimental.pallas import tpu as pltpu
from jax.sharding import PartitionSpec as P

SWEEPS = 3
EPSILON = 0.01
MESH = pl.DeviceIdType.MESH
F32 = jnp.float32
BF16 = jnp.bfloat16
LANES = 128


def kernel(geometry, names, noise, w_first, w_second, history, out_first, out_second, *scratch):
    ny, nx, nz = geometry
    chips = ny * nx
    n_row, n_col = 2 * chips, nz
    s = SimpleNamespace(**dict(zip(names, scratch)))
    sem = scratch[-1]
    gen, zdim = noise.shape
    hist, width = history.shape
    hid = w_first.shape[1]
    half = hid // 2
    quarter = half // 2
    gen_total, hist_total = gen * n_row, hist * n_col
    scale = 1.0 / math.sqrt(gen_total)

    me = lax.axis_index("row")
    z = lax.axis_index("col")
    core = lax.rem(me, 2)
    other = 1 - core
    chip = me // 2
    x = lax.rem(chip, nx)
    y = chip // nx
    odd = lax.rem(z, 2) == 1

    barrier = pltpu.get_barrier_semaphore()

    def greet_row(k, c):
        pl.semaphore_signal(barrier, inc=1, device_id=(lax.rem(me + k, n_row), z), device_id_type=MESH)
        return c

    def greet_col(k, c):
        pl.semaphore_signal(barrier, inc=1, device_id=(me, lax.rem(z + k, n_col)), device_id_type=MESH)
        return c

    lax.fori_loop(1, n_row, greet_row, 0)
    lax.fori_loop(1, n_col, greet_col, 0)

    def start(src, dst, number, device):
        pltpu.make_async_remote_copy(
            src_ref=src, dst_ref=dst, send_sem=sem.at[2 * number], recv_sem=sem.at[2 * number + 1],
            device_id=device, device_id_type=MESH,
        ).start()

    def wait_bytes(like, index):
        pltpu.make_async_copy(like, like, sem.at[index]).wait()

    flying, landed = {}, {}

    def expect(number, like):
        flying[number] = like

    def arrived(number):
        landed[number] = flying.pop(number)
        wait_bytes(landed[number], 2 * number + 1)

    def finish():
        for number in tuple(flying):
            arrived(number)
        for number, like in landed.items():
            wait_bytes(like, 2 * number)

    def to_row(src, dst, number):
        def step(k, c):
            start(src, dst.at[k - 1], number, (lax.rem(me + k, n_row), z))
            return c
        lax.fori_loop(1, n_row, step, 0)
        expect(number, dst)

    def to_col(src, dst, number):
        def step(k, c):
            start(src, dst.at[k - 1], number, (me, lax.rem(z + k, n_col)))
            return c
        lax.fori_loop(1, n_col, step, 0)
        expect(number, dst)

    def at(offset, size, unit):
        return pl.ds(offset if isinstance(offset, int) else pl.multiple_of(offset, unit), size)

    def each(count, body):
        lax.fori_loop(0, count, lambda k, c: (body(k), c)[1], 0)

    tiles = [slice(k * LANES, (k + 1) * LANES) for k in range(max(hist, width) // LANES)]
    plan_tiles = tiles[:hist // LANES]
    blocks = gen // LANES

    def block(k):
        return at(k * LANES, LANES, LANES)

    def fold(v):
        return jnp.sum(v.reshape(LANES // 8, 8, LANES), axis=0)

    def rows_from_column(column, dst, total):
        for k in range(dst.shape[0]):
            turned = jnp.transpose(column[tiles[k], :])
            dst[k:k + 1, :] = jnp.sum(turned, axis=0, keepdims=True) if total else turned[0:1, :]

    def column_from_rows(rows, column):
        for k in range(rows.shape[0]):
            column[tiles[k], :] = jnp.transpose(jnp.broadcast_to(rows[k:k + 1, :], (LANES, LANES)))

    def dot(a, b):
        return jnp.dot(a, b, preferred_element_type=F32)

    def dot_t(a, b):
        return lax.dot_general(a, b, (((1,), (1,)), ((), ())), preferred_element_type=F32)

    tile_h = min(256, hid)
    tile_g = min(256, width)
    tile_j = min(256, hist)

    for n in range(hid // tile_h):
        cols = slice(n * tile_h, (n + 1) * tile_h)
        preact = dot(noise[...], w_first[:, cols])
        s.mult[:, cols] = preact
        s.hidden[:, cols] = (preact / (1.0 + jnp.exp(-preact))).astype(BF16)

    def surface_tile(n):
        cols = at(n * tile_g, tile_g, tile_g)
        s.surface[:, cols] = dot(s.hidden[...], w_second[:, cols]).astype(BF16)
    each(width // tile_g, surface_tile)

    def squares(ref, rows):
        total = jnp.zeros((LANES, LANES), F32)
        for cols in tiles[:width // LANES]:
            v = ref[rows, cols].astype(F32)
            total = total + v * v
        return total

    def surf_squares(k):
        s.surf_sq[block(k), :] = squares(s.surface, block(k))
    each(blocks, surf_squares)
    s.surf_sq[...] = jnp.broadcast_to(jnp.sum(s.surf_sq[...], axis=1, keepdims=True), (gen, LANES))

    def hist_squares(k):
        s.hist_sq[:, block(k)] = jnp.sum(jnp.transpose(squares(history, block(k))), axis=0, keepdims=True)
    each(hist // LANES, hist_squares)

    def inner_tile(n):
        cols = at(n * tile_j, tile_j, tile_j)
        s.plan[:, cols] = dot_t(s.surface[...], history[cols, :])
    each(hist // tile_j, inner_tile)

    def score_block(k, tops):
        rows, out = block(k), []
        own = s.surf_sq[rows, :]
        for cols, top in zip(plan_tiles, tops):
            cost = (own + s.hist_sq[:, cols] - 2.0 * s.plan[rows, cols]) * (1.0 / width)
            scores = cost * (-1.0 / EPSILON)
            s.plan[rows, cols] = scores
            out.append(jnp.maximum(top, jnp.max(scores.reshape(LANES // 8, 8, LANES), axis=0)))
        return tuple(out)
    tops = lax.fori_loop(0, blocks, score_block, tuple(jnp.full((8, LANES), -jnp.inf, F32) for _ in plan_tiles))
    for k, top in enumerate(tops):
        s.m_pair[0, k:k + 1, :] = jnp.max(top, axis=0, keepdims=True)

    def score_sums(k, sums):
        rows, out = block(k), []
        for n, (cols, total) in enumerate(zip(plan_tiles, sums)):
            out.append(total + fold(jnp.exp(s.plan[rows, cols] - s.m_pair[0, n:n + 1, :])))
        return tuple(out)
    zeros = tuple(jnp.zeros((8, LANES), F32) for _ in plan_tiles)
    for k, total in enumerate(lax.fori_loop(0, blocks, score_sums, zeros)):
        s.m_pair[1, k:k + 1, :] = jnp.sum(total, axis=0, keepdims=True)

    pl.semaphore_wait(barrier, n_row - 1 + n_col - 1)
    to_row(s.m_pair, s.m_pair_in, 0)

    def hist_w_tile(n):
        rows = at(n * 256, min(256, hist), min(256, hist))
        prod = dot_t(history[rows, :], w_second[...])
        hi = prod.astype(BF16)
        s.hist_w_hi[rows, :] = hi
        s.hist_w_lo[rows, :] = (prod - hi.astype(F32)).astype(BF16)
    each(hist // min(256, hist), hist_w_tile)

    arrived(0)
    tops, sums = s.m_pair_in[:, 0], s.m_pair_in[:, 1]
    top = jnp.maximum(jnp.max(tops, axis=0), s.m_pair[0])
    total = jnp.sum(sums * jnp.exp(tops - top[None]), axis=0)
    total = total + s.m_pair[1] * jnp.exp(s.m_pair[0] - top)
    s.m_row[0] = math.log(gen_total) - (top + jnp.log(total))

    def row_tops(k):
        rows = block(k)
        top = s.plan[rows, plan_tiles[0]] + s.m_row[0, 0:1, :]
        for n, cols in enumerate(plan_tiles[1:], 1):
            top = jnp.maximum(top, s.plan[rows, cols] + s.m_row[0, n:n + 1, :])
        s.row_a[rows, :] = top
    each(blocks, row_tops)
    s.row_a[...] = jnp.broadcast_to(jnp.max(s.row_a[...], axis=1, keepdims=True), (gen, LANES))

    def first_rows(k):
        rows = block(k)
        top, total = s.row_a[rows, :], jnp.zeros((LANES, LANES), F32)
        for n, cols in enumerate(plan_tiles):
            grown = jnp.exp(s.plan[rows, cols] + s.m_row[0, n:n + 1, :] - top)
            s.plan[rows, cols] = grown
            total = total + grown
        s.row_b[rows, :] = total
    each(blocks, first_rows)
    rows_from_column(s.row_a, s.m_col0.at[0], False)
    rows_from_column(s.row_b, s.m_col0.at[1], True)
    to_col(s.m_col0, s.m_col0_in, 1)

    def surf_w_tile(n):
        cols = at(n * tile_h, tile_h, tile_h)
        s.surf_w[:, cols] = dot_t(s.surface[...], w_second[cols, :])
    each(hid // tile_h, surf_w_tile)
    s.hidden_t[...] = jnp.transpose(s.hidden[...].astype(F32)).astype(BF16)

    pair = at(lax.div(z, 2) * LANES, LANES, LANES)
    prod = dot(s.hidden_t[...], s.surface[:, pair])
    turned = pltpu.roll(prod, 64, axis=1)
    s.term_a[...] = jnp.where(odd, turned, prod)
    s.term_b[...] = jnp.where(odd, prod, turned)
    low = lax.broadcasted_iota(jnp.int32, (8, LANES), 1) < 64

    def owner_term(o):
        oc, ox, oy = lax.rem(o, 2), lax.rem(o // 2, nx), o // (2 * nx)
        upper = oc * half + ox * (quarter // nx) + oy * 8
        lower = oc * half + quarter + oy * (quarter // ny) + ox * 8
        s.term[o] = jnp.where(low, s.term_a[at(upper, 8, 8), :], s.term_b[at(lower, 8, 8), :])
    each(n_row, owner_term)

    def send_term(k, c):
        peer = lax.rem(me + k, n_row)
        start(s.term.at[peer], s.term_in.at[k - 1], 6, (peer, z))
        return c
    lax.fori_loop(1, n_row, send_term, 0)
    expect(6, s.term_in)

    arrived(1)
    tops, sums = s.m_col0_in[:, 0], s.m_col0_in[:, 1]
    top = jnp.maximum(jnp.max(tops, axis=0), s.m_col0[0])
    total = jnp.sum(sums * jnp.exp(tops - top[None]), axis=0)
    total = total + s.m_col0[1] * jnp.exp(s.m_col0[0] - top)
    column_from_rows(jnp.exp(s.m_col0[0] - top) / total, s.row_a)

    def column_sums(scaled, dst):
        def step(k, sums):
            rows, out = block(k), []
            own = s.row_a[rows, :]
            for cols, total in zip(plan_tiles, sums):
                v = s.plan[rows, cols] * own
                if scaled:
                    s.plan[rows, cols] = v
                out.append(total + fold(v))
            return tuple(out)
        for k, total in enumerate(lax.fori_loop(0, blocks, step, zeros)):
            dst[k:k + 1, :] = jnp.sum(total, axis=0, keepdims=True)

    def row_sums(k):
        rows = block(k)
        total = jnp.zeros((LANES, LANES), F32)
        for n, cols in enumerate(plan_tiles):
            total = total + s.plan[rows, cols] * s.col_b[n:n + 1, :]
        s.row_b[rows, :] = total

    for sweep in range(1, SWEEPS):
        number = 2 * sweep
        mine, theirs = s.m_row.at[sweep], s.m_row_in.at[sweep - 1]
        column_sums(sweep == 1, mine)
        to_row(mine, theirs, number)
        if sweep == 1:
            preact = s.mult[...]
            sigma = 1.0 / (1.0 + jnp.exp(-preact))
            s.mult[...] = sigma * (1.0 + preact * (1.0 - sigma))
            s.noise_t[...] = jnp.transpose(noise[...].astype(F32)).astype(BF16)
        arrived(number)
        total = mine[...] + jnp.sum(theirs[...], axis=0)
        s.col_b[...] = (gen_total / hist_total) / total

        each(blocks, row_sums)
        mine, theirs = s.m_col.at[sweep - 1], s.m_col_in.at[sweep - 1]
        rows_from_column(s.row_b, mine, True)
        to_col(mine, theirs, number + 1)
        arrived(number + 1)
        total = mine[...] + jnp.sum(theirs[...], axis=0)
        column_from_rows(1.0 / total, s.row_a)

    def weight_rows(k):
        rows = block(k)
        own = s.row_a[rows, :]
        for n, cols in enumerate(plan_tiles):
            s.weights[rows, cols] = (s.plan[rows, cols] * own * s.col_b[n:n + 1, :]).astype(BF16)
    each(blocks, weight_rows)

    def acc_tile(which):
        rows = at(which * half, half, half)

        def body(n):
            cols = at(n * tile_j, tile_j, tile_j)
            s.acc[rows, cols] = dot(s.hidden_t[rows, :], s.weights[:, cols])
        each(hist // tile_j, body)

    span_x, span_y = quarter // nx, quarter // ny
    base_u, base_l = core * half, core * half + quarter
    sibling = (me + 1 - 2 * core, z)
    acc_tile(other)
    order = [pair for k in range(1, nx) for pair in ((True, k), (False, k))] + [(True, 0), (False, 0)]

    def block_rows(upper, k):
        return lax.rem(x + k, nx) * span_x if upper else quarter + lax.rem(y + k, ny) * span_y

    for n, (upper, k) in enumerate(order):
        rows = block_rows(upper, k)
        start(s.acc.at[at(other * half + rows, span_x, 8), :], s.acc_in.at[at(rows, span_x, 8), :], 20 + n, sibling)
        expect(20 + n, s.acc_in.at[at(n * span_x, span_x, 8), :])
    acc_tile(core)

    def pass_on(n):
        upper, k = order[n]
        rows = block_rows(upper, k)
        arrived(20 + n)
        mine = at(core * half + rows, span_x, 8)
        s.acc[mine, :] = s.acc[mine, :] + s.acc_in[at(rows, span_x, 8), :]
        if k and upper:
            start(s.acc.at[mine, :], s.x_in.at[k - 1], 9, ((y * nx + lax.rem(x + k, nx)) * 2 + core, z))
        elif k:
            start(s.acc.at[mine, :], s.y_in.at[k - 1], 10, ((lax.rem(y + k, ny) * nx + x) * 2 + core, z))

    def first_tile(n):
        cols = at(n * tile_h, tile_h, tile_h)
        value = dot(s.weights[...], s.hist_w_hi[:, cols]) + dot(s.weights[...], s.hist_w_lo[:, cols])
        d_hidden = (s.surf_w[:, cols] * (1.0 / n_col) - value) * scale
        d_preact = d_hidden * s.mult[:, cols]
        hi = d_preact.astype(BF16)
        lo = (d_preact - hi.astype(F32)).astype(BF16)
        s.first[:, cols] = dot(s.noise_t[...], hi) + dot(s.noise_t[...], lo)

    for n in range(2):
        pass_on(2 * n)
        pass_on(2 * n + 1)
        first_tile(n)
    start(s.first.at[:, at(other * half, half, half)], s.first_in, 8, sibling)
    expect(8, s.first_in)
    for n in range(4, len(order)):
        pass_on(n)
    expect(9, s.x_in)
    expect(10, s.y_in)

    arrived(8)
    s.first_half[...] = s.first[:, at(core * half, half, half)] + s.first_in[...]
    piece = zdim // chips

    def send_first(k, c):
        to = lax.rem(chip + k, chips)
        start(s.first_half.at[at(to * piece, piece, 8), :], s.first_chip_in.at[k - 1], 11,
              (to * 2 + core, z))
        return c
    lax.fori_loop(1, chips, send_first, 0)
    expect(11, s.first_chip_in)
    arrived(11)
    s.first_piece[0] = s.first_half[at(chip * piece, piece, 8), :] + jnp.sum(s.first_chip_in[...], axis=0)
    to_col(s.first_piece.at[0], s.first_z_in, 12)

    arrived(9)
    arrived(10)
    rows_u, rows_l = at(base_u + x * span_x, span_x, 8), at(base_l + y * span_y, span_y, 8)
    s.acc[rows_u, :] = s.acc[rows_u, :] + jnp.sum(s.x_in[...], axis=0)
    s.acc[rows_l, :] = s.acc[rows_l, :] + jnp.sum(s.y_in[...], axis=0)
    for k in range(1, ny):
        to = lax.rem(y + k, ny)
        start(s.acc.at[at(base_u + x * span_x + to * 8, 8, 8), :], s.y_in2.at[k - 1], 13,
              ((to * nx + x) * 2 + core, z))
    for k in range(1, nx):
        to = lax.rem(x + k, nx)
        start(s.acc.at[at(base_l + y * span_y + to * 8, 8, 8), :], s.x_in2.at[k - 1], 14,
              ((y * nx + to) * 2 + core, z))
    expect(13, s.y_in2)
    expect(14, s.x_in2)
    arrived(13)
    arrived(14)
    mine_u, mine_l = base_u + x * span_x + y * 8, base_l + y * span_y + x * 8
    s.reduced[0:8, :] = s.acc[at(mine_u, 8, 8), :] + jnp.sum(s.y_in2[...], axis=0)
    s.reduced[8:16, :] = s.acc[at(mine_l, 8, 8), :] + jnp.sum(s.x_in2[...], axis=0)

    hi = s.reduced[...].astype(BF16)
    lo = (s.reduced[...] - hi.astype(F32)).astype(BF16)
    both = jnp.concatenate([hi, lo], axis=0)

    def mix_tile(n):
        cols = at(n * tile_g, tile_g, tile_g)
        prod = dot(both, history[:, cols])
        s.mix[:, cols] = prod[0:16] + prod[16:32]
    each(width // tile_g, mix_tile)
    low = lax.broadcasted_iota(jnp.int32, (8, LANES), 1) < 64
    for k in range(nz):
        lanes = slice((k // 2) * LANES, (k // 2 + 1) * LANES)
        upper, lower = s.mix[0:8, lanes], s.mix[8:16, lanes]
        if k % 2 == 0:
            s.slices[k] = jnp.where(low, upper, pltpu.roll(lower, 64, axis=1))
        else:
            s.slices[k] = jnp.where(low, pltpu.roll(upper, 64, axis=1), lower)

    def send_slice(k, c):
        to = lax.rem(z + k, n_col)
        start(s.slices.at[to], s.slices_in.at[k - 1], 15, (me, to))
        return c
    lax.fori_loop(1, n_col, send_slice, 0)
    expect(15, s.slices_in)

    arrived(12)
    s.first_all[core, chip] = s.first_piece[0] + jnp.sum(s.first_z_in[...], axis=0)

    def spread(array, number):
        def step(k, c):
            start(array.at[core, chip], array.at[core, chip], number, (lax.rem(chip + k, chips) * 2 + core, z))
            return c
        lax.fori_loop(1, chips, step, 0)
        expect(number, array.at[0, pl.ds(0, chips - 1)])
    spread(s.first_all, 16)

    arrived(6)
    term = s.term[me] + jnp.sum(s.term_in[...], axis=0)
    arrived(15)
    mixed = s.slices[z] + jnp.sum(s.slices_in[...], axis=0)
    s.second_all[me] = (term - mixed) * scale

    def send_second(k, c):
        start(s.second_all.at[me], s.second_all.at[me], 17, (lax.rem(me + k, n_row), z))
        return c
    lax.fori_loop(1, n_row, send_second, 0)
    expect(17, s.second_all.at[pl.ds(0, n_row - 1)])

    arrived(16)
    start(s.first_all.at[core], s.first_all.at[core], 18, sibling)
    expect(18, s.first_all.at[0])
    arrived(18)
    out_first[...] = s.first_all[...]
    arrived(17)
    out_second[...] = s.second_all[...]
    finish()


def place(geometry, first, second, out_first, out_second, wide):
    ny, nx, nz = geometry
    half, piece = out_first.shape[1] // 2, first.shape[2]
    quarter = half // 2
    for y in range(ny):
        for x in range(nx):
            chip = y * nx + x
            for c in range(2):
                out_first[chip * piece:(chip + 1) * piece, c * half:(c + 1) * half] = first[c, chip]
                upper = c * half + x * (quarter // nx) + y * 8
                lower = c * half + quarter + y * (quarter // ny) + x * 8
                v = second[2 * chip + c]
                wide[upper:upper + 8, :] = v
                wide[lower:lower + 8, :] = pltpu.roll(v, 64, axis=1)
    for k in range(wide.shape[0] // LANES):
        out_second[:, k * LANES:(k + 1) * LANES] = jnp.transpose(wide[k * LANES:(k + 1) * LANES, :])[0:64, :]


def shards(geometry, noise, w_first, w_second, history):
    ny, nx, nz = geometry
    chips = ny * nx
    n_row = 2 * chips
    gen, zdim = noise.shape
    hist, width = history.shape
    hid = w_first.shape[1]
    half, quarter = hid // 2, hid // 4
    piece = zdim // chips
    jr, ir = hist // LANES, gen // LANES
    shapes = dict(
        hidden=((gen, hid), BF16), hidden_t=((hid, gen), BF16), noise_t=((zdim, gen), BF16),
        surface=((gen, width), BF16), mult=((gen, hid), F32), surf_w=((gen, hid), F32),
        hist_w_hi=((hist, hid), BF16), hist_w_lo=((hist, hid), BF16),
        plan=((gen, hist), F32), weights=((gen, hist), BF16),
        surf_sq=((gen, LANES), F32), hist_sq=((1, hist), F32),
        row_a=((gen, LANES), F32), row_b=((gen, LANES), F32), col_b=((jr, LANES), F32),
        m_pair=((2, jr, LANES), F32), m_pair_in=((n_row - 1, 2, jr, LANES), F32),
        m_col0=((2, ir, LANES), F32), m_col0_in=((nz - 1, 2, ir, LANES), F32),
        m_row=((SWEEPS, jr, LANES), F32), m_row_in=((SWEEPS - 1, n_row - 1, jr, LANES), F32),
        m_col=((SWEEPS - 1, ir, LANES), F32), m_col_in=((SWEEPS - 1, nz - 1, ir, LANES), F32),
        acc=((hid, hist), F32), acc_in=((half, hist), F32),
        x_in=((nx - 1, quarter // nx, hist), F32), y_in=((ny - 1, quarter // ny, hist), F32),
        x_in2=((nx - 1, 8, hist), F32), y_in2=((ny - 1, 8, hist), F32), reduced=((16, hist), F32),
        first=((zdim, hid), F32), first_in=((zdim, half), F32), first_half=((zdim, half), F32),
        first_chip_in=((chips - 1, piece, half), F32), first_piece=((1, piece, half), F32),
        first_z_in=((nz - 1, piece, half), F32), first_all=((2, chips, piece, half), F32),
        term_a=((hid, LANES), F32), term_b=((hid, LANES), F32),
        term=((n_row, 8, LANES), F32), term_in=((n_row - 1, 8, LANES), F32),
        mix=((16, width), F32), slices=((nz, 8, LANES), F32), slices_in=((nz - 1, 8, LANES), F32),
        second_all=((n_row, 8, LANES), F32),
    )
    scratch = [pltpu.VMEM(*shape) for shape in shapes.values()] + [pltpu.SemaphoreType.DMA((56,))]
    vmem = pl.BlockSpec(memory_space=pltpu.VMEM)
    first, second = pl.pallas_call(
        functools.partial(kernel, geometry, tuple(shapes)),
        out_shape=(
            jax.ShapeDtypeStruct((2, chips, piece, half), F32),
            jax.ShapeDtypeStruct((n_row, 8, LANES), F32),
        ),
        in_specs=[vmem] * 4,
        out_specs=(vmem, vmem),
        scratch_shapes=scratch,
        compiler_params=pltpu.CompilerParams(
            collective_id=0, has_side_effects=True, vmem_limit_bytes=56 * 1024 * 1024
        ),
        name="transport",
    )(noise, w_first, w_second, history)
    grad_first, turned = pl.pallas_call(
        functools.partial(place, geometry),
        out_shape=(
            jax.ShapeDtypeStruct((zdim, hid), F32),
            jax.ShapeDtypeStruct((width // nz, hid), F32),
        ),
        in_specs=[vmem] * 2,
        out_specs=(vmem, vmem),
        scratch_shapes=[pltpu.VMEM((hid, LANES), F32)],
        name="place",
    )(first, second)
    return grad_first, turned.T


def solution(mesh):
    chips = mesh.shape["row"] // 2
    nx = math.isqrt(chips)
    geometry = (chips // nx, nx, mesh.shape["col"])
    placed = (P("row", None), P(), P(), P("col", None))
    return jax.shard_map(
        functools.partial(shards, geometry), mesh=mesh, in_specs=placed,
        out_specs=(P(), P(None, "col")), check_vma=False,
    )
```

```python
import functools
import math
from types import SimpleNamespace

import jax
import jax.numpy as jnp
from jax import lax
from jax.experimental import pallas as pl
from jax.experimental.pallas import tpu as pltpu
from jax.sharding import PartitionSpec as P

SWEEPS = 3
EPSILON = 0.01
MESH = pl.DeviceIdType.MESH
F32 = jnp.float32
BF16 = jnp.bfloat16
LANES = 128


def kernel(geometry, names, noise, w_first, w_second_hbm, history_hbm, out_first, out_second, *scratch):
    ny, nx, nz = geometry
    chips = ny * nx
    n_row, n_col = 2 * chips, nz
    s = SimpleNamespace(**dict(zip(names, scratch)))
    sem = scratch[-1]
    w_second, history = s.w_second, s.history
    load_w = pltpu.make_async_copy(w_second_hbm, w_second, sem.at[78])
    load_h = pltpu.make_async_copy(history_hbm, history, sem.at[79])
    load_w.start()
    load_h.start()
    gen, zdim = noise.shape
    hist, width = history.shape
    hid = w_first.shape[1]
    half = hid // 2
    quarter = half // 2
    gen_total, hist_total = gen * n_row, hist * n_col
    scale = 1.0 / math.sqrt(gen_total)

    me = lax.axis_index("row")
    z = lax.axis_index("col")
    core = lax.rem(me, 2)
    other = 1 - core
    chip = me // 2
    x = lax.rem(chip, nx)
    y = chip // nx
    odd = lax.rem(z, 2) == 1

    barrier = pltpu.get_barrier_semaphore()

    def far(a, n):
        return lax.rem(n // 2 + n * n - a * (a + 1) // 2, n)

    def over_chips(send):
        def step(j, c):
            to_y, to_x = lax.rem(y + far(j // nx, ny), ny), lax.rem(x + far(lax.rem(j, nx), nx), nx)
            send(to_y * nx + to_x, j)
            return c
        lax.fori_loop(0, chips - 1, step, 0)

    def over_row(send):
        def step(j, c):
            k = j // 2
            to_y, to_x = lax.rem(y + far(k // nx, ny), ny), lax.rem(x + far(lax.rem(k, nx), nx), nx)
            send((to_y * nx + to_x) * 2 + lax.rem(core + 1 + j, 2), j)
            return c
        lax.fori_loop(0, n_row - 1, step, 0)

    def over_col(send):
        def step(j, c):
            send(lax.rem(z + n_col // 2 + (j + 1) // 2 * (1 - 2 * lax.rem(j, 2)), n_col), j)
            return c
        lax.fori_loop(0, n_col - 1, step, 0)

    over_col(lambda to, j: pl.semaphore_signal(barrier, inc=1, device_id=(me, to), device_id_type=MESH))
    over_row(lambda to, j: pl.semaphore_signal(barrier, inc=1, device_id=(to, z), device_id_type=MESH))

    def start(src, dst, number, device):
        pltpu.make_async_remote_copy(
            src_ref=src, dst_ref=dst, send_sem=sem.at[2 * number], recv_sem=sem.at[2 * number + 1],
            device_id=device, device_id_type=MESH,
        ).start()

    def wait_bytes(like, index):
        pltpu.make_async_copy(like, like, sem.at[index]).wait()

    flying, landed = {}, {}

    def expect(number, like):
        flying[number] = like

    def arrived(number):
        landed[number] = flying.pop(number)
        wait_bytes(landed[number], 2 * number + 1)

    def finish():
        for number in tuple(flying):
            arrived(number)
        for number, like in landed.items():
            wait_bytes(like, 2 * number)

    def to_row(src, dst, number):
        over_row(lambda to, j: start(src, dst.at[j], number, (to, z)))
        expect(number, dst)

    def to_col(src, dst, number):
        over_col(lambda to, j: start(src, dst.at[j], number, (me, to)))
        expect(number, dst)

    def at(offset, size, unit):
        return pl.ds(offset if isinstance(offset, int) else pl.multiple_of(offset, unit), size)

    def each(count, body):
        lax.fori_loop(0, count, lambda k, c: (body(k), c)[1], 0)

    tiles = [slice(k * LANES, (k + 1) * LANES) for k in range(max(hist, width) // LANES)]
    plan_tiles = tiles[:hist // LANES]
    blocks = gen // LANES

    def block(k):
        return at(k * LANES, LANES, LANES)

    def fold(v):
        return jnp.sum(v.reshape(LANES // 8, 8, LANES), axis=0)

    def rows_from_column(column, dst, total):
        for k in range(dst.shape[0]):
            turned = jnp.transpose(column[tiles[k], :])
            dst[k:k + 1, :] = jnp.sum(turned, axis=0, keepdims=True) if total else turned[0:1, :]

    def column_from_rows(rows, column):
        for k in range(rows.shape[0]):
            column[tiles[k], :] = jnp.transpose(jnp.broadcast_to(rows[k:k + 1, :], (LANES, LANES)))

    def dot(a, b):
        return jnp.dot(a, b, preferred_element_type=F32)

    def dot_t(a, b):
        return lax.dot_general(a, b, (((1,), (1,)), ((), ())), preferred_element_type=F32)

    tile_h = min(256, hid)
    tile_g = min(256, width)
    tile_j = min(256, hist)

    for n in range(hid // tile_h):
        cols = slice(n * tile_h, (n + 1) * tile_h)
        preact = dot(noise[...], w_first[:, cols])
        s.mult[:, cols] = preact
        s.hidden[:, cols] = (preact / (1.0 + jnp.exp(-preact))).astype(BF16)

    load_w.wait()

    def surface_tile(n):
        cols = at(n * tile_g, tile_g, tile_g)
        s.surface[:, cols] = dot(s.hidden[...], w_second[:, cols]).astype(BF16)
    each(width // tile_g, surface_tile)

    def squares(ref, rows):
        total = jnp.zeros((LANES, LANES), F32)
        for cols in tiles[:width // LANES]:
            v = ref[rows, cols].astype(F32)
            total = total + v * v
        return total

    def surf_squares(k):
        s.surf_sq[block(k), :] = squares(s.surface, block(k))
    each(blocks, surf_squares)
    s.surf_sq[...] = jnp.broadcast_to(jnp.sum(s.surf_sq[...], axis=1, keepdims=True), (gen, LANES))

    load_h.wait()

    def inner_tile(n):
        cols = at(n * tile_j, tile_j, tile_j)
        s.plan[:, cols] = dot_t(s.surface[...], history[cols, :])
    each(hist // tile_j, inner_tile)

    def score_block(k, tops):
        rows, out = block(k), []
        own = s.surf_sq[rows, :]
        for cols, top in zip(plan_tiles, tops):
            cost = (own - 2.0 * s.plan[rows, cols]) * (1.0 / width)
            scores = cost * (-1.0 / EPSILON)
            s.plan[rows, cols] = scores
            out.append(jnp.maximum(top, jnp.max(scores.reshape(LANES // 8, 8, LANES), axis=0)))
        return tuple(out)
    tops = lax.fori_loop(0, blocks, score_block, tuple(jnp.full((8, LANES), -jnp.inf, F32) for _ in plan_tiles))
    for k, top in enumerate(tops):
        s.m_pair[0, k:k + 1, :] = jnp.max(top, axis=0, keepdims=True)

    def score_sums(k, sums):
        rows, out = block(k), []
        for n, (cols, total) in enumerate(zip(plan_tiles, sums)):
            out.append(total + fold(jnp.exp(s.plan[rows, cols] - s.m_pair[0, n:n + 1, :])))
        return tuple(out)
    zeros = tuple(jnp.zeros((8, LANES), F32) for _ in plan_tiles)
    for k, total in enumerate(lax.fori_loop(0, blocks, score_sums, zeros)):
        s.m_pair[1, k:k + 1, :] = jnp.sum(total, axis=0, keepdims=True)

    pl.semaphore_wait(barrier, n_row - 1 + n_col - 1)
    to_row(s.m_pair, s.m_pair_in, 0)

    def hist_w_tile(n):
        rows = at(n * 256, min(256, hist), min(256, hist))
        prod = dot_t(history[rows, :], w_second[...])
        hi = prod.astype(BF16)
        s.hist_w_hi[rows, :] = hi
        s.hist_w_lo[rows, :] = (prod - hi.astype(F32)).astype(BF16)
    each(hist // min(256, hist), hist_w_tile)

    def hist_squares(k):
        s.hist_sq[pl.ds(k, 1), :] = jnp.sum(jnp.transpose(squares(history, block(k))), axis=0, keepdims=True)
    each(hist // LANES, hist_squares)
    hist_cost = s.hist_sq[...] * (1.0 / width) * (1.0 / EPSILON)

    arrived(0)
    tops, sums = s.m_pair_in[:, 0], s.m_pair_in[:, 1]
    top = jnp.maximum(jnp.max(tops, axis=0), s.m_pair[0])
    total = jnp.sum(sums * jnp.exp(tops - top[None]), axis=0)
    total = total + s.m_pair[1] * jnp.exp(s.m_pair[0] - top)
    g_first = math.log(gen_total) - (top + jnp.log(total) - hist_cost)
    s.m_row[0] = g_first - hist_cost

    def row_tops(k):
        rows = block(k)
        top = s.plan[rows, plan_tiles[0]] + s.m_row[0, 0:1, :]
        for n, cols in enumerate(plan_tiles[1:], 1):
            top = jnp.maximum(top, s.plan[rows, cols] + s.m_row[0, n:n + 1, :])
        s.row_a[rows, :] = top
    each(blocks, row_tops)
    s.row_a[...] = jnp.broadcast_to(jnp.max(s.row_a[...], axis=1, keepdims=True), (gen, LANES))

    def first_rows(k):
        rows = block(k)
        top, total = s.row_a[rows, :], jnp.zeros((LANES, LANES), F32)
        for n, cols in enumerate(plan_tiles):
            grown = jnp.exp(s.plan[rows, cols] + s.m_row[0, n:n + 1, :] - top)
            s.plan[rows, cols] = grown
            total = total + grown
        s.row_b[rows, :] = total
    each(blocks, first_rows)
    rows_from_column(s.row_a, s.m_col0.at[0], False)
    rows_from_column(s.row_b, s.m_col0.at[1], True)
    to_col(s.m_col0, s.m_col0_in, 1)

    def surf_w_tile(n):
        cols = at(n * tile_h, tile_h, tile_h)
        s.surf_w[:, cols] = dot_t(s.surface[...], w_second[cols, :])
    each(hid // tile_h, surf_w_tile)
    s.hidden_t[...] = jnp.transpose(s.hidden[...].astype(F32)).astype(BF16)

    pair = at(lax.div(z, 2) * LANES, LANES, LANES)
    prod = dot(s.hidden_t[...], s.surface[:, pair])
    turned = pltpu.roll(prod, 64, axis=1)
    s.term_a[...] = jnp.where(odd, turned, prod)
    s.term_b[...] = jnp.where(odd, prod, turned)
    low = lax.broadcasted_iota(jnp.int32, (8, LANES), 1) < 64

    def owner_term(o):
        oc, ox, oy = lax.rem(o, 2), lax.rem(o // 2, nx), o // (2 * nx)
        upper = oc * half + oy * (quarter // ny) + ox * 8
        lower = oc * half + quarter + ox * (quarter // nx) + oy * 8
        s.term[o] = jnp.where(low, s.term_a[at(upper, 8, 8), :], s.term_b[at(lower, 8, 8), :])
    each(n_row, owner_term)

    over_row(lambda to, j: start(s.term.at[to], s.term_in.at[j], 6, (to, z)))
    expect(6, s.term_in)

    arrived(1)
    tops, sums = s.m_col0_in[:, 0], s.m_col0_in[:, 1]
    top = jnp.maximum(jnp.max(tops, axis=0), s.m_col0[0])
    total = jnp.sum(sums * jnp.exp(tops - top[None]), axis=0)
    total = total + s.m_col0[1] * jnp.exp(s.m_col0[0] - top)
    column_from_rows(jnp.exp(s.m_col0[0] - top) / total, s.row_a)

    def column_sums(scaled, dst):
        def step(k, sums):
            rows, out = block(k), []
            own = s.row_a[rows, :]
            for cols, total in zip(plan_tiles, sums):
                v = s.plan[rows, cols] * own
                if scaled:
                    s.plan[rows, cols] = v
                out.append(total + fold(v))
            return tuple(out)
        for k, total in enumerate(lax.fori_loop(0, blocks, step, zeros)):
            dst[k:k + 1, :] = jnp.sum(total, axis=0, keepdims=True)

    def row_sums(k):
        rows = block(k)
        total = jnp.zeros((LANES, LANES), F32)
        for n, cols in enumerate(plan_tiles):
            total = total + s.plan[rows, cols] * s.col_b[n:n + 1, :]
        s.row_b[rows, :] = total

    for sweep in range(1, SWEEPS):
        number = 2 * sweep
        mine, theirs = s.m_row.at[sweep], s.m_row_in.at[sweep - 1]
        column_sums(sweep == 1, mine)
        to_row(mine, theirs, number)
        if sweep == 1:
            preact = s.mult[...]
            sigma = 1.0 / (1.0 + jnp.exp(-preact))
            s.mult[...] = sigma * (1.0 + preact * (1.0 - sigma))
            s.noise_t[...] = jnp.transpose(noise[...].astype(F32)).astype(BF16)
        arrived(number)
        total = mine[...] + jnp.sum(theirs[...], axis=0)
        s.col_b[...] = (gen_total / hist_total) / total

        each(blocks, row_sums)
        mine, theirs = s.m_col.at[sweep - 1], s.m_col_in.at[sweep - 1]
        rows_from_column(s.row_b, mine, True)
        to_col(mine, theirs, number + 1)
        arrived(number + 1)
        total = mine[...] + jnp.sum(theirs[...], axis=0)
        column_from_rows(1.0 / total, s.row_a)

    def weight_rows(k):
        rows = block(k)
        own = s.row_a[rows, :]
        for n, cols in enumerate(plan_tiles):
            s.weights[rows, cols] = (s.plan[rows, cols] * own * s.col_b[n:n + 1, :]).astype(BF16)
    each(blocks, weight_rows)

    def acc_tile(which):
        rows = at(which * half, half, half)

        def body(n):
            cols = at(n * tile_j, tile_j, tile_j)
            s.acc[rows, cols] = dot(s.hidden_t[rows, :], s.weights[:, cols])
        each(hist // tile_j, body)

    span_x, span_y = quarter // nx, quarter // ny
    base_u, base_l = core * half, core * half + quarter
    sibling = (me + 1 - 2 * core, z)
    acc_tile(other)
    order = [pair for k in range(1, nx) for pair in ((True, k), (False, k))] + [(True, 0), (False, 0)]

    def block_rows(upper, k):
        return lax.rem(y + k, ny) * span_y if upper else quarter + lax.rem(x + k, nx) * span_x

    for n, (upper, k) in enumerate(order):
        rows = block_rows(upper, k)
        start(s.acc.at[at(other * half + rows, span_x, 8), :], s.acc_in.at[at(rows, span_x, 8), :], 20 + n, sibling)
        expect(20 + n, s.acc_in.at[at(n * span_x, span_x, 8), :])
    acc_tile(core)

    def chip_at(upper, k, first):
        if upper == first:
            return (y * nx + lax.rem(x + k, nx)) * 2 + core, lax.rem(x + k, nx) * 8
        return (lax.rem(y + k, ny) * nx + x) * 2 + core, lax.rem(y + k, ny) * 8

    def pass_on(n):
        upper, k = order[n]
        rows = block_rows(upper, k)
        arrived(20 + n)
        mine = at(core * half + rows, span_x, 8)
        s.acc[mine, :] = s.acc[mine, :] + s.acc_in[at(rows, span_x, 8), :]
        into = s.x_in if upper else s.y_in
        for j in range(1, nx):
            device, offset = chip_at(upper, j, True)
            start(s.acc.at[at(core * half + rows + offset, 8, 8), :], into.at[k, j - 1], 30 + n, (device, z))
        expect(30 + n, into.at[k])

    def pass_second(n):
        upper, k = order[n]
        arrived(30 + n)
        rows = at(core * half + block_rows(upper, k) + chip_at(upper, 0, True)[1], 8, 8)
        total = s.acc[rows, :] + jnp.sum((s.x_in if upper else s.y_in)[k], axis=0)
        if k == 0:
            return total
        s.acc[rows, :] = total
        into = s.y_in2 if upper else s.x_in2
        start(s.acc.at[rows, :], into.at[k - 1], 13 if upper else 14, (chip_at(upper, k, False)[0], z))

    def first_tile(n):
        cols = at(n * tile_h, tile_h, tile_h)
        value = dot(s.weights[...], s.hist_w_hi[:, cols]) + dot(s.weights[...], s.hist_w_lo[:, cols])
        d_hidden = (s.surf_w[:, cols] * (1.0 / n_col) - value) * scale
        d_preact = d_hidden * s.mult[:, cols]
        hi = d_preact.astype(BF16)
        lo = (d_preact - hi.astype(F32)).astype(BF16)
        s.first[:, cols] = dot(s.noise_t[...], hi) + dot(s.noise_t[...], lo)

    for n in range(2):
        for k in range(4):
            pass_on(4 * n + k)
        first_tile(n)
    start(s.first.at[:, at(other * half, half, half)], s.first_in, 8, sibling)
    expect(8, s.first_in)
    pass_second(0)
    pass_second(1)

    arrived(8)
    s.first_half[...] = s.first[:, at(core * half, half, half)] + s.first_in[...]
    piece = zdim // chips
    over_chips(lambda to, j: start(
        s.first_half.at[at(to * piece, piece, 8), :], s.first_chip_in.at[j], 11, (to * 2 + core, z)))
    expect(11, s.first_chip_in)
    for n in range(2, len(order) - 2):
        pass_second(n)
    expect(13, s.y_in2)
    expect(14, s.x_in2)
    own_u, own_l = pass_second(len(order) - 2), pass_second(len(order) - 1)
    arrived(11)
    s.first_piece[0] = s.first_half[at(chip * piece, piece, 8), :] + jnp.sum(s.first_chip_in[...], axis=0)
    to_col(s.first_piece.at[0], s.first_z_in, 12)
    arrived(13)
    arrived(14)
    s.reduced[0:8, :] = own_u + jnp.sum(s.y_in2[...], axis=0)
    s.reduced[8:16, :] = own_l + jnp.sum(s.x_in2[...], axis=0)

    hi = s.reduced[...].astype(BF16)
    lo = (s.reduced[...] - hi.astype(F32)).astype(BF16)
    both = jnp.concatenate([hi, lo], axis=0)

    def mix_tile(n):
        cols = at(n * tile_g, tile_g, tile_g)
        prod = dot(both, history[:, cols])
        s.mix[:, cols] = prod[0:16] + prod[16:32]
    each(width // tile_g, mix_tile)
    low = lax.broadcasted_iota(jnp.int32, (8, LANES), 1) < 64
    for k in range(nz):
        lanes = slice((k // 2) * LANES, (k // 2 + 1) * LANES)
        upper, lower = s.mix[0:8, lanes], s.mix[8:16, lanes]
        if k % 2 == 0:
            s.slices[k] = jnp.where(low, upper, pltpu.roll(lower, 64, axis=1))
        else:
            s.slices[k] = jnp.where(low, pltpu.roll(upper, 64, axis=1), lower)

    over_col(lambda to, j: start(s.slices.at[to], s.slices_in.at[j], 15, (me, to)))
    expect(15, s.slices_in)

    arrived(12)
    s.first_all[core, chip] = s.first_piece[0] + jnp.sum(s.first_z_in[...], axis=0)

    over_chips(lambda to, j: start(
        s.first_all.at[core, chip], s.first_all.at[core, chip], 16, (to * 2 + core, z)))
    expect(16, s.first_all.at[0, pl.ds(0, chips - 1)])

    arrived(6)
    term = s.term[me] + jnp.sum(s.term_in[...], axis=0)
    arrived(15)
    mixed = s.slices[z] + jnp.sum(s.slices_in[...], axis=0)
    s.second_all[me] = (term - mixed) * scale

    over_row(lambda to, j: start(s.second_all.at[me], s.second_all.at[me], 17, (to, z)))
    expect(17, s.second_all.at[pl.ds(0, n_row - 1)])

    arrived(16)
    start(s.first_all.at[core], s.first_all.at[core], 18, sibling)
    expect(18, s.first_all.at[0])
    arrived(18)
    out_first[...] = s.first_all[...]
    arrived(17)
    out_second[...] = s.second_all[...]
    finish()


def place(geometry, first, second, out_first, out_second, wide):
    ny, nx, nz = geometry
    half, piece = out_first.shape[1] // 2, first.shape[2]
    quarter = half // 2
    for y in range(ny):
        for x in range(nx):
            chip = y * nx + x
            for c in range(2):
                out_first[chip * piece:(chip + 1) * piece, c * half:(c + 1) * half] = first[c, chip]
                upper = c * half + y * (quarter // ny) + x * 8
                lower = c * half + quarter + x * (quarter // nx) + y * 8
                v = second[2 * chip + c]
                wide[upper:upper + 8, :] = v
                wide[lower:lower + 8, :] = pltpu.roll(v, 64, axis=1)
    for k in range(wide.shape[0] // LANES):
        out_second[:, k * LANES:(k + 1) * LANES] = jnp.transpose(wide[k * LANES:(k + 1) * LANES, :])[0:64, :]


def shards(geometry, noise, w_first, w_second, history):
    ny, nx, nz = geometry
    chips = ny * nx
    n_row = 2 * chips
    gen, zdim = noise.shape
    hist, width = history.shape
    hid = w_first.shape[1]
    half, quarter = hid // 2, hid // 4
    piece = zdim // chips
    jr, ir = hist // LANES, gen // LANES
    shapes = dict(
        w_second=((hid, width), BF16), history=((hist, width), BF16),
        hidden=((gen, hid), BF16), hidden_t=((hid, gen), BF16), noise_t=((zdim, gen), BF16),
        surface=((gen, width), BF16), mult=((gen, hid), F32), surf_w=((gen, hid), F32),
        hist_w_hi=((hist, hid), BF16), hist_w_lo=((hist, hid), BF16),
        plan=((gen, hist), F32), weights=((gen, hist), BF16),
        surf_sq=((gen, LANES), F32), hist_sq=((jr, LANES), F32),
        row_a=((gen, LANES), F32), row_b=((gen, LANES), F32), col_b=((jr, LANES), F32),
        m_pair=((2, jr, LANES), F32), m_pair_in=((n_row - 1, 2, jr, LANES), F32),
        m_col0=((2, ir, LANES), F32), m_col0_in=((nz - 1, 2, ir, LANES), F32),
        m_row=((SWEEPS, jr, LANES), F32), m_row_in=((SWEEPS - 1, n_row - 1, jr, LANES), F32),
        m_col=((SWEEPS - 1, ir, LANES), F32), m_col_in=((SWEEPS - 1, nz - 1, ir, LANES), F32),
        acc=((hid, hist), F32), acc_in=((half, hist), F32),
        x_in=((ny, nx - 1, 8, hist), F32), y_in=((nx, ny - 1, 8, hist), F32),
        x_in2=((nx - 1, 8, hist), F32), y_in2=((ny - 1, 8, hist), F32), reduced=((16, hist), F32),
        first=((zdim, hid), F32), first_in=((zdim, half), F32), first_half=((zdim, half), F32),
        first_chip_in=((chips - 1, piece, half), F32), first_piece=((1, piece, half), F32),
        first_z_in=((nz - 1, piece, half), F32), first_all=((2, chips, piece, half), F32),
        term_a=((hid, LANES), F32), term_b=((hid, LANES), F32),
        term=((n_row, 8, LANES), F32), term_in=((n_row - 1, 8, LANES), F32),
        mix=((16, width), F32), slices=((nz, 8, LANES), F32), slices_in=((nz - 1, 8, LANES), F32),
        second_all=((n_row, 8, LANES), F32),
    )
    scratch = [pltpu.VMEM(*shape) for shape in shapes.values()] + [pltpu.SemaphoreType.DMA((80,))]
    vmem = pl.BlockSpec(memory_space=pltpu.VMEM)
    first, second = pl.pallas_call(
        functools.partial(kernel, geometry, tuple(shapes)),
        out_shape=(
            jax.ShapeDtypeStruct((2, chips, piece, half), F32),
            jax.ShapeDtypeStruct((n_row, 8, LANES), F32),
        ),
        in_specs=[vmem] * 2 + [pl.BlockSpec(memory_space=pl.ANY)] * 2,
        out_specs=(vmem, vmem),
        scratch_shapes=scratch,
        compiler_params=pltpu.CompilerParams(
            collective_id=0, has_side_effects=True, vmem_limit_bytes=56 * 1024 * 1024
        ),
        name="transport",
    )(noise, w_first, w_second, history)
    grad_first, turned = pl.pallas_call(
        functools.partial(place, geometry),
        out_shape=(
            jax.ShapeDtypeStruct((zdim, hid), F32),
            jax.ShapeDtypeStruct((width // nz, hid), F32),
        ),
        in_specs=[vmem] * 2,
        out_specs=(vmem, vmem),
        scratch_shapes=[pltpu.VMEM((hid, LANES), F32)],
        name="place",
    )(first, second)
    return grad_first, turned.T


def solution(mesh):
    chips = mesh.shape["row"] // 2
    nx = math.isqrt(chips)
    geometry = (chips // nx, nx, mesh.shape["col"])
    placed = (P("row", None), P(), P(), P("col", None))
    return jax.shard_map(
        functools.partial(shards, geometry), mesh=mesh, in_specs=placed,
        out_specs=(P(), P(None, "col")), check_vma=False,
    )
```

```python
import functools
import math
from types import SimpleNamespace

import jax
import jax.numpy as jnp
from jax import lax
from jax.experimental import pallas as pl
from jax.experimental.pallas import tpu as pltpu
from jax.sharding import PartitionSpec as P

SWEEPS = 3
EPSILON = 0.01
MESH = pl.DeviceIdType.MESH
F32 = jnp.float32
BF16 = jnp.bfloat16
LANES = 128


def kernel(geometry, names, noise, w_first, w_second_hbm, history_hbm, out_first, out_second, *scratch):
    ny, nx, nz = geometry
    chips = ny * nx
    n_row, n_col = 2 * chips, nz
    s = SimpleNamespace(**dict(zip(names, scratch)))
    sem = scratch[-1]
    w_second, history = s.w_second, s.history
    load_w = pltpu.make_async_copy(w_second_hbm, w_second, sem.at[78])
    load_h = pltpu.make_async_copy(history_hbm, history, sem.at[79])
    load_w.start()
    load_h.start()
    gen, zdim = noise.shape
    hist, width = history.shape
    hid = w_first.shape[1]
    half = hid // 2
    quarter = half // 2
    gen_total, hist_total = gen * n_row, hist * n_col
    scale = 1.0 / math.sqrt(gen_total)

    me = lax.axis_index("row")
    z = lax.axis_index("col")
    core = lax.rem(me, 2)
    other = 1 - core
    chip = me // 2
    x = lax.rem(chip, nx)
    y = chip // nx
    odd = lax.rem(z, 2) == 1

    barrier = pltpu.get_barrier_semaphore()

    def far(a, n):
        return lax.rem(n // 2 + n * n - a * (a + 1) // 2, n)

    def over_chips(send):
        def step(j, c):
            to_y, to_x = lax.rem(y + far(j // nx, ny), ny), lax.rem(x + far(lax.rem(j, nx), nx), nx)
            send(to_y * nx + to_x, j)
            return c
        lax.fori_loop(0, chips - 1, step, 0)

    def over_row(send):
        def step(j, c):
            k = j // 2
            to_y, to_x = lax.rem(y + far(k // nx, ny), ny), lax.rem(x + far(lax.rem(k, nx), nx), nx)
            send((to_y * nx + to_x) * 2 + lax.rem(core + 1 + j, 2), j)
            return c
        lax.fori_loop(0, n_row - 1, step, 0)

    def over_col(send):
        def step(j, c):
            send(lax.rem(z + n_col // 2 + (j + 1) // 2 * (1 - 2 * lax.rem(j, 2)), n_col), j)
            return c
        lax.fori_loop(0, n_col - 1, step, 0)

    over_col(lambda to, j: pl.semaphore_signal(barrier, inc=1, device_id=(me, to), device_id_type=MESH))
    over_row(lambda to, j: pl.semaphore_signal(barrier, inc=1, device_id=(to, z), device_id_type=MESH))

    def start(src, dst, number, device):
        pltpu.make_async_remote_copy(
            src_ref=src, dst_ref=dst, send_sem=sem.at[2 * number], recv_sem=sem.at[2 * number + 1],
            device_id=device, device_id_type=MESH,
        ).start()

    def wait_bytes(like, index):
        pltpu.make_async_copy(like, like, sem.at[index]).wait()

    flying, landed = {}, {}

    def expect(number, like):
        flying[number] = like

    def arrived(number):
        landed[number] = flying.pop(number)
        wait_bytes(landed[number], 2 * number + 1)

    def finish():
        for number in tuple(flying):
            arrived(number)
        for number, like in landed.items():
            wait_bytes(like, 2 * number)

    def to_row(src, dst, number):
        over_row(lambda to, j: start(src, dst.at[j], number, (to, z)))
        expect(number, dst)

    def to_col(src, dst, number):
        over_col(lambda to, j: start(src, dst.at[j], number, (me, to)))
        expect(number, dst)

    def at(offset, size, unit):
        return pl.ds(offset if isinstance(offset, int) else pl.multiple_of(offset, unit), size)

    def each(count, body):
        lax.fori_loop(0, count, lambda k, c: (body(k), c)[1], 0)

    tiles = [slice(k * LANES, (k + 1) * LANES) for k in range(max(hist, width) // LANES)]
    plan_tiles = tiles[:hist // LANES]
    blocks = gen // LANES

    def block(k):
        return at(k * LANES, LANES, LANES)

    def fold(v):
        return jnp.sum(v.reshape(LANES // 8, 8, LANES), axis=0)

    def squares(ref, rows, across):
        total = jnp.zeros((LANES, LANES), F32)
        for cols in across:
            v = ref[rows, cols].astype(F32)
            total = total + v * v
        return total

    def rows_from_column(column, dst, total):
        for k in range(dst.shape[0]):
            turned = jnp.transpose(column[tiles[k], :])
            dst[k:k + 1, :] = jnp.sum(turned, axis=0, keepdims=True) if total else turned[0:1, :]

    def column_from_rows(rows, column):
        for k in range(rows.shape[0]):
            column[tiles[k], :] = jnp.transpose(jnp.broadcast_to(rows[k:k + 1, :], (LANES, LANES)))

    def dot(a, b):
        return jnp.dot(a, b, preferred_element_type=F32)

    def dot_t(a, b):
        return lax.dot_general(a, b, (((1,), (1,)), ((), ())), preferred_element_type=F32)

    tile_h = min(256, hid)
    tile_g = min(256, width)
    tile_j = min(256, hist)

    for n in range(hid // tile_h):
        cols = slice(n * tile_h, (n + 1) * tile_h)
        preact = dot(noise[...], w_first[:, cols])
        s.mult[:, cols] = preact
        s.hidden[:, cols] = (preact / (1.0 + jnp.exp(-preact))).astype(BF16)

    load_w.wait()

    for n in range(width // tile_g):
        cols = slice(n * tile_g, (n + 1) * tile_g)
        s.surface[:, cols] = dot(s.hidden[...], w_second[:, cols]).astype(BF16)
        for k in range(blocks):
            total = squares(s.surface, tiles[k], tiles[n * tile_g // LANES:(n + 1) * tile_g // LANES])
            s.surf_sq[tiles[k], :] = total if n == 0 else s.surf_sq[tiles[k], :] + total
    s.surf_sq[...] = jnp.broadcast_to(jnp.sum(s.surf_sq[...], axis=1, keepdims=True), (gen, LANES))

    load_h.wait()
    for n in range(hist // tile_j):
        wide = slice(n * tile_j, (n + 1) * tile_j)
        s.plan[:, wide] = dot_t(s.surface[...], history[wide, :])
        for c in range(n * tile_j // LANES, (n + 1) * tile_j // LANES):
            top = None
            for k in range(blocks):
                cost = (s.surf_sq[tiles[k], :] - 2.0 * s.plan[tiles[k], tiles[c]]) * (1.0 / width)
                scores = cost * (-1.0 / EPSILON)
                s.plan[tiles[k], tiles[c]] = scores
                tall = jnp.max(scores.reshape(LANES // 8, 8, LANES), axis=0)
                top = tall if top is None else jnp.maximum(top, tall)
            top = jnp.max(top, axis=0, keepdims=True)
            total = jnp.zeros((8, LANES), F32)
            for k in range(blocks):
                total = total + fold(jnp.exp(s.plan[tiles[k], tiles[c]] - top))
            s.m_lse[c:c + 1, :] = top + jnp.log(jnp.sum(total, axis=0, keepdims=True))

    pl.semaphore_wait(barrier, n_row - 1 + n_col - 1)
    to_row(s.m_lse, s.m_lse_in, 0)

    def hist_w_tile(n):
        rows = at(n * 256, min(256, hist), min(256, hist))
        prod = dot_t(history[rows, :], w_second[...])
        hi = prod.astype(BF16)
        s.hist_w_hi[rows, :] = hi
        s.hist_w_lo[rows, :] = (prod - hi.astype(F32)).astype(BF16)
    each(hist // min(256, hist), hist_w_tile)

    def hist_squares(k):
        s.hist_sq[pl.ds(k, 1), :] = jnp.sum(
            jnp.transpose(squares(history, block(k), tiles[:width // LANES])), axis=0, keepdims=True)
    each(hist // LANES, hist_squares)
    hist_cost = s.hist_sq[...] * (1.0 / width) * (1.0 / EPSILON)

    arrived(0)
    top = jnp.maximum(jnp.max(s.m_lse_in[...], axis=0), s.m_lse[...])
    total = jnp.sum(jnp.exp(s.m_lse_in[...] - top[None]), axis=0) + jnp.exp(s.m_lse[...] - top)
    g_first = math.log(gen_total) - (top + jnp.log(total) - hist_cost)
    s.m_row[0] = g_first - hist_cost

    def row_tops(k):
        rows = block(k)
        top = s.plan[rows, plan_tiles[0]] + s.m_row[0, 0:1, :]
        for n, cols in enumerate(plan_tiles[1:], 1):
            top = jnp.maximum(top, s.plan[rows, cols] + s.m_row[0, n:n + 1, :])
        s.row_a[rows, :] = top
    for k in range(blocks):
        row_tops(k)
    s.row_a[...] = jnp.broadcast_to(jnp.max(s.row_a[...], axis=1, keepdims=True), (gen, LANES))

    def first_rows(k):
        rows = block(k)
        top, total = s.row_a[rows, :], jnp.zeros((LANES, LANES), F32)
        for n, cols in enumerate(plan_tiles):
            grown = jnp.exp(s.plan[rows, cols] + s.m_row[0, n:n + 1, :] - top)
            s.plan[rows, cols] = grown
            total = total + grown
        s.row_b[rows, :] = total
    for k in range(blocks):
        first_rows(k)
    rows_from_column(s.row_a, s.row_top, False)
    rows_from_column(s.row_b, s.row_lse, True)
    s.row_lse[...] = s.row_top[...] + jnp.log(s.row_lse[...])
    to_col(s.row_lse, s.row_lse_in, 1)

    def surf_w_tile(n):
        cols = at(n * tile_h, tile_h, tile_h)
        s.surf_w[:, cols] = dot_t(s.surface[...], w_second[cols, :])
    each(hid // tile_h, surf_w_tile)
    s.hidden_t[...] = jnp.transpose(s.hidden[...].astype(F32)).astype(BF16)

    pair = at(lax.div(z, 2) * LANES, LANES, LANES)
    prod = dot(s.hidden_t[...], s.surface[:, pair])
    turned = pltpu.roll(prod, 64, axis=1)
    s.term_a[...] = jnp.where(odd, turned, prod)
    s.term_b[...] = jnp.where(odd, prod, turned)
    low = lax.broadcasted_iota(jnp.int32, (8, LANES), 1) < 64

    def owner_term(o):
        oc, ox, oy = lax.rem(o, 2), lax.rem(o // 2, nx), o // (2 * nx)
        upper = oc * half + oy * (quarter // ny) + ox * 8
        lower = oc * half + quarter + ox * (quarter // nx) + oy * 8
        s.term[o] = jnp.where(low, s.term_a[at(upper, 8, 8), :], s.term_b[at(lower, 8, 8), :])
    each(n_row, owner_term)

    over_row(lambda to, j: start(s.term.at[to], s.term_in.at[j], 6, (to, z)))
    expect(6, s.term_in)

    arrived(1)
    top = jnp.maximum(jnp.max(s.row_lse_in[...], axis=0), s.row_lse[...])
    total = jnp.sum(jnp.exp(s.row_lse_in[...] - top[None]), axis=0) + jnp.exp(s.row_lse[...] - top)
    column_from_rows(jnp.exp(s.row_top[...] - top) / total, s.row_a)

    def column_sums(scaled, dst):
        def step(k, sums):
            rows, out = block(k), []
            own = s.row_a[rows, :]
            for cols, total in zip(plan_tiles, sums):
                v = s.plan[rows, cols] * own
                if scaled:
                    s.plan[rows, cols] = v
                out.append(total + fold(v))
            return tuple(out)
        sums = [jnp.zeros((8, LANES), F32) for _ in plan_tiles]
        for k in range(blocks):
            sums = step(k, sums)
        for k, total in enumerate(sums):
            dst[k:k + 1, :] = jnp.sum(total, axis=0, keepdims=True)

    def row_sums(k):
        rows = block(k)
        total = jnp.zeros((LANES, LANES), F32)
        for n, cols in enumerate(plan_tiles):
            total = total + s.plan[rows, cols] * s.col_b[n:n + 1, :]
        s.row_b[rows, :] = total

    def unscaled_rows(k):
        rows = block(k)
        for n, cols in enumerate(plan_tiles):
            v = s.plan[rows, cols] * s.col_b[n:n + 1, :]
            hi = v.astype(BF16)
            s.plan_hi[rows, cols] = hi
            s.plan_lo[rows, cols] = (v - hi.astype(F32)).astype(BF16)

    def value_tile(n):
        cols = at(n * tile_h, tile_h, tile_h)
        s.value[:, cols] = (dot(s.plan_hi[...], s.hist_w_hi[:, cols]) + dot(s.plan_hi[...], s.hist_w_lo[:, cols])
                            + dot(s.plan_lo[...], s.hist_w_hi[:, cols]))

    for sweep in range(1, SWEEPS):
        number = 2 * sweep
        mine, theirs = s.m_row.at[sweep], s.m_row_in.at[sweep - 1]
        column_sums(sweep == 1, mine)
        to_row(mine, theirs, number)
        if sweep == 1:
            preact = s.mult[...]
            sigma = 1.0 / (1.0 + jnp.exp(-preact))
            s.mult[...] = sigma * (1.0 + preact * (1.0 - sigma))
            s.noise_t[...] = jnp.transpose(noise[...].astype(F32)).astype(BF16)
        arrived(number)
        total = mine[...] + jnp.sum(theirs[...], axis=0)
        s.col_b[...] = (gen_total / hist_total) / total

        for k in range(blocks):
            row_sums(k)
        mine, theirs = s.m_col.at[sweep - 1], s.m_col_in.at[sweep - 1]
        rows_from_column(s.row_b, mine, True)
        to_col(mine, theirs, number + 1)
        if sweep == SWEEPS - 1:
            for k in range(blocks):
                unscaled_rows(k)
            each(hid // tile_h, value_tile)
        arrived(number + 1)
        total = mine[...] + jnp.sum(theirs[...], axis=0)
        column_from_rows(1.0 / total, s.row_a)

    def weight_rows(k):
        rows = block(k)
        own = s.row_a[rows, :]
        for n, cols in enumerate(plan_tiles):
            s.weights[rows, cols] = (s.plan[rows, cols] * own * s.col_b[n:n + 1, :]).astype(BF16)
    for k in range(blocks):
        weight_rows(k)

    def acc_tile(which):
        rows = at(which * half, half, half)

        def body(n):
            cols = at(n * tile_j, tile_j, tile_j)
            s.acc[rows, cols] = dot(s.hidden_t[rows, :], s.weights[:, cols])
        each(hist // tile_j, body)

    span_x, span_y = quarter // nx, quarter // ny
    base_u, base_l = core * half, core * half + quarter
    sibling = (me + 1 - 2 * core, z)
    acc_tile(other)
    order = [pair for k in range(1, nx) for pair in ((True, k), (False, k))] + [(True, 0), (False, 0)]

    def block_rows(upper, k):
        return lax.rem(y + k, ny) * span_y if upper else quarter + lax.rem(x + k, nx) * span_x

    for n, (upper, k) in enumerate(order):
        rows = block_rows(upper, k)
        start(s.acc.at[at(other * half + rows, span_x, 8), :], s.acc_in.at[at(rows, span_x, 8), :], 20 + n, sibling)
        expect(20 + n, s.acc_in.at[at(n * span_x, span_x, 8), :])

    def chip_at(upper, k, first):
        if upper == first:
            return (y * nx + lax.rem(x + k, nx)) * 2 + core, lax.rem(x + k, nx) * 8
        return (lax.rem(y + k, ny) * nx + x) * 2 + core, lax.rem(y + k, ny) * 8

    def pass_on(n):
        upper, k = order[n]
        rows = block_rows(upper, k)
        arrived(20 + n)
        mine = at(core * half + rows, span_x, 8)
        s.acc[mine, :] = s.acc[mine, :] + s.acc_in[at(rows, span_x, 8), :]
        into = s.x_in if upper else s.y_in
        for j in range(1, nx):
            device, offset = chip_at(upper, j, True)
            start(s.acc.at[at(core * half + rows + offset, 8, 8), :], into.at[k, j - 1], 30 + n, (device, z))
        expect(30 + n, into.at[k])

    def pass_second(n):
        upper, k = order[n]
        arrived(30 + n)
        rows = at(core * half + block_rows(upper, k) + chip_at(upper, 0, True)[1], 8, 8)
        total = s.acc[rows, :] + jnp.sum((s.x_in if upper else s.y_in)[k], axis=0)
        if k == 0:
            return total
        s.acc[rows, :] = total
        into = s.y_in2 if upper else s.x_in2
        start(s.acc.at[rows, :], into.at[k - 1], 13 if upper else 14, (chip_at(upper, k, False)[0], z))

    for k in range(blocks):
        for cols in tiles[:hid // LANES]:
            rows = tiles[k]
            d_hidden = (s.surf_w[rows, cols] * (1.0 / n_col) - s.value[rows, cols] * s.row_a[rows, :]) * scale
            d_preact = d_hidden * s.mult[rows, cols]
            hi = d_preact.astype(BF16)
            s.d_hi[rows, cols] = hi
            s.d_lo[rows, cols] = (d_preact - hi.astype(F32)).astype(BF16)
    s.first[...] = dot(s.noise_t[...], s.d_hi[...]) + dot(s.noise_t[...], s.d_lo[...])
    start(s.first.at[:, at(other * half, half, half)], s.first_in, 8, sibling)
    expect(8, s.first_in)
    acc_tile(core)

    for n in range(len(order)):
        pass_on(n)
    pass_second(0)
    pass_second(1)

    arrived(8)
    s.first_half[...] = s.first[:, at(core * half, half, half)] + s.first_in[...]
    piece = zdim // chips
    over_chips(lambda to, j: start(
        s.first_half.at[at(to * piece, piece, 8), :], s.first_chip_in.at[j], 11, (to * 2 + core, z)))
    expect(11, s.first_chip_in)
    for n in range(2, len(order) - 2):
        pass_second(n)
    expect(13, s.y_in2)
    expect(14, s.x_in2)
    own_u, own_l = pass_second(len(order) - 2), pass_second(len(order) - 1)
    arrived(11)
    s.first_piece[0] = s.first_half[at(chip * piece, piece, 8), :] + jnp.sum(s.first_chip_in[...], axis=0)
    to_col(s.first_piece.at[0], s.first_z_in, 12)
    arrived(13)
    arrived(14)
    s.reduced[0:8, :] = own_u + jnp.sum(s.y_in2[...], axis=0)
    s.reduced[8:16, :] = own_l + jnp.sum(s.x_in2[...], axis=0)

    hi = s.reduced[...].astype(BF16)
    lo = (s.reduced[...] - hi.astype(F32)).astype(BF16)
    both = jnp.concatenate([hi, lo], axis=0)

    def mix_tile(n):
        cols = at(n * tile_g, tile_g, tile_g)
        prod = dot(both, history[:, cols])
        s.mix[:, cols] = prod[0:16] + prod[16:32]
    each(width // tile_g, mix_tile)
    low = lax.broadcasted_iota(jnp.int32, (8, LANES), 1) < 64
    for k in range(nz):
        lanes = slice((k // 2) * LANES, (k // 2 + 1) * LANES)
        upper, lower = s.mix[0:8, lanes], s.mix[8:16, lanes]
        if k % 2 == 0:
            s.slices[k] = jnp.where(low, upper, pltpu.roll(lower, 64, axis=1))
        else:
            s.slices[k] = jnp.where(low, pltpu.roll(upper, 64, axis=1), lower)

    over_col(lambda to, j: start(s.slices.at[to], s.slices_in.at[j], 15, (me, to)))
    expect(15, s.slices_in)

    arrived(12)
    s.first_all[core, chip] = s.first_piece[0] + jnp.sum(s.first_z_in[...], axis=0)

    over_chips(lambda to, j: start(
        s.first_all.at[core, chip], s.first_all.at[core, chip], 16, (to * 2 + core, z)))
    expect(16, s.first_all.at[0, pl.ds(0, chips - 1)])

    arrived(6)
    term = s.term[me] + jnp.sum(s.term_in[...], axis=0)
    arrived(15)
    mixed = s.slices[z] + jnp.sum(s.slices_in[...], axis=0)
    s.second_all[me] = (term - mixed) * scale

    over_row(lambda to, j: start(s.second_all.at[me], s.second_all.at[me], 17, (to, z)))
    expect(17, s.second_all.at[pl.ds(0, n_row - 1)])

    arrived(16)
    start(s.first_all.at[core], s.first_all.at[core], 18, sibling)
    expect(18, s.first_all.at[0])
    arrived(18)
    out_first[...] = s.first_all[...]
    arrived(17)
    out_second[...] = s.second_all[...]
    finish()


def place(geometry, first, second, out_first, out_second, wide):
    ny, nx, nz = geometry
    half, piece = out_first.shape[1] // 2, first.shape[2]
    quarter = half // 2
    for y in range(ny):
        for x in range(nx):
            chip = y * nx + x
            for c in range(2):
                out_first[chip * piece:(chip + 1) * piece, c * half:(c + 1) * half] = first[c, chip]
                upper = c * half + y * (quarter // ny) + x * 8
                lower = c * half + quarter + x * (quarter // nx) + y * 8
                v = second[2 * chip + c]
                wide[upper:upper + 8, :] = v
                wide[lower:lower + 8, :] = pltpu.roll(v, 64, axis=1)
    for k in range(wide.shape[0] // LANES):
        out_second[:, k * LANES:(k + 1) * LANES] = jnp.transpose(wide[k * LANES:(k + 1) * LANES, :])[0:64, :]


def shards(geometry, noise, w_first, w_second, history):
    ny, nx, nz = geometry
    chips = ny * nx
    n_row = 2 * chips
    gen, zdim = noise.shape
    hist, width = history.shape
    hid = w_first.shape[1]
    half, quarter = hid // 2, hid // 4
    piece = zdim // chips
    jr, ir = hist // LANES, gen // LANES
    shapes = dict(
        w_second=((hid, width), BF16), history=((hist, width), BF16),
        hidden=((gen, hid), BF16), hidden_t=((hid, gen), BF16), noise_t=((zdim, gen), BF16),
        surface=((gen, width), BF16), mult=((gen, hid), F32), surf_w=((gen, hid), F32),
        hist_w_hi=((hist, hid), BF16), hist_w_lo=((hist, hid), BF16),
        plan=((gen, hist), F32), weights=((gen, hist), BF16),
        surf_sq=((gen, LANES), F32), hist_sq=((jr, LANES), F32),
        row_a=((gen, LANES), F32), row_b=((gen, LANES), F32), col_b=((jr, LANES), F32),
        m_lse=((jr, LANES), F32), m_lse_in=((n_row - 1, jr, LANES), F32),
        row_top=((ir, LANES), F32), row_lse=((ir, LANES), F32), row_lse_in=((nz - 1, ir, LANES), F32),
        plan_hi=((gen, hist), BF16), plan_lo=((gen, hist), BF16), value=((gen, hid), F32),
        d_hi=((gen, hid), BF16), d_lo=((gen, hid), BF16),
        m_row=((SWEEPS, jr, LANES), F32), m_row_in=((SWEEPS - 1, n_row - 1, jr, LANES), F32),
        m_col=((SWEEPS - 1, ir, LANES), F32), m_col_in=((SWEEPS - 1, nz - 1, ir, LANES), F32),
        acc=((hid, hist), F32), acc_in=((half, hist), F32),
        x_in=((ny, nx - 1, 8, hist), F32), y_in=((nx, ny - 1, 8, hist), F32),
        x_in2=((nx - 1, 8, hist), F32), y_in2=((ny - 1, 8, hist), F32), reduced=((16, hist), F32),
        first=((zdim, hid), F32), first_in=((zdim, half), F32), first_half=((zdim, half), F32),
        first_chip_in=((chips - 1, piece, half), F32), first_piece=((1, piece, half), F32),
        first_z_in=((nz - 1, piece, half), F32), first_all=((2, chips, piece, half), F32),
        term_a=((hid, LANES), F32), term_b=((hid, LANES), F32),
        term=((n_row, 8, LANES), F32), term_in=((n_row - 1, 8, LANES), F32),
        mix=((16, width), F32), slices=((nz, 8, LANES), F32), slices_in=((nz - 1, 8, LANES), F32),
        second_all=((n_row, 8, LANES), F32),
    )
    scratch = [pltpu.VMEM(*shape) for shape in shapes.values()] + [pltpu.SemaphoreType.DMA((80,))]
    vmem = pl.BlockSpec(memory_space=pltpu.VMEM)
    first, second = pl.pallas_call(
        functools.partial(kernel, geometry, tuple(shapes)),
        out_shape=(
            jax.ShapeDtypeStruct((2, chips, piece, half), F32),
            jax.ShapeDtypeStruct((n_row, 8, LANES), F32),
        ),
        in_specs=[vmem] * 2 + [pl.BlockSpec(memory_space=pl.ANY)] * 2,
        out_specs=(vmem, vmem),
        scratch_shapes=scratch,
        compiler_params=pltpu.CompilerParams(
            collective_id=0, has_side_effects=True, vmem_limit_bytes=56 * 1024 * 1024
        ),
        name="transport",
    )(noise, w_first, w_second, history)
    grad_first, turned = pl.pallas_call(
        functools.partial(place, geometry),
        out_shape=(
            jax.ShapeDtypeStruct((zdim, hid), F32),
            jax.ShapeDtypeStruct((width // nz, hid), F32),
        ),
        in_specs=[vmem] * 2,
        out_specs=(vmem, vmem),
        scratch_shapes=[pltpu.VMEM((hid, LANES), F32)],
        name="place",
    )(first, second)
    return grad_first, turned.T


def solution(mesh):
    chips = mesh.shape["row"] // 2
    nx = math.isqrt(chips)
    geometry = (chips // nx, nx, mesh.shape["col"])
    placed = (P("row", None), P(), P(), P("col", None))
    return jax.shard_map(
        functools.partial(shards, geometry), mesh=mesh, in_specs=placed,
        out_specs=(P(), P(None, "col")), check_vma=False,
    )
```

```python
import functools
import math
from types import SimpleNamespace

import jax
import jax.numpy as jnp
from jax import lax
from jax.experimental import pallas as pl
from jax.experimental.pallas import tpu as pltpu
from jax.sharding import PartitionSpec as P

SWEEPS = 3
EPSILON = 0.01
MESH = pl.DeviceIdType.MESH
F32 = jnp.float32
BF16 = jnp.bfloat16
LANES = 128


def kernel(geometry, names, noise, w_first, w_second_hbm, history_hbm, out_first, out_second, *scratch):
    ny, nx, nz = geometry
    chips = ny * nx
    n_row, n_col = 2 * chips, nz
    s = SimpleNamespace(**dict(zip(names, scratch)))
    sem = scratch[-1]
    w_second, history = s.w_second, s.history
    load_w = pltpu.make_async_copy(w_second_hbm, w_second, sem.at[78])
    load_h = pltpu.make_async_copy(history_hbm, history, sem.at[79])
    load_w.start()
    load_h.start()
    gen, zdim = noise.shape
    hist, width = history.shape
    hid = w_first.shape[1]
    half = hid // 2
    quarter = half // 2
    gen_total, hist_total = gen * n_row, hist * n_col
    scale = 1.0 / math.sqrt(gen_total)

    me = lax.axis_index("row")
    z = lax.axis_index("col")
    core = lax.rem(me, 2)
    other = 1 - core
    chip = me // 2
    x = lax.rem(chip, nx)
    y = chip // nx
    odd = lax.rem(z, 2) == 1

    barrier = pltpu.get_barrier_semaphore()

    def far(a, n):
        return lax.rem(n // 2 + n * n - a * (a + 1) // 2, n)

    def over_chips(send):
        def step(j, c):
            to_y, to_x = lax.rem(y + far(j // nx, ny), ny), lax.rem(x + far(lax.rem(j, nx), nx), nx)
            send(to_y * nx + to_x, j)
            return c
        lax.fori_loop(0, chips - 1, step, 0)

    def over_row(send):
        def step(j, c):
            k = j // 2
            to_y, to_x = lax.rem(y + far(k // nx, ny), ny), lax.rem(x + far(lax.rem(k, nx), nx), nx)
            send((to_y * nx + to_x) * 2 + lax.rem(core + 1 + j, 2), j)
            return c
        lax.fori_loop(0, n_row - 1, step, 0)

    def over_col(send):
        def step(j, c):
            send(lax.rem(z + n_col // 2 + (j + 1) // 2 * (1 - 2 * lax.rem(j, 2)), n_col), j)
            return c
        lax.fori_loop(0, n_col - 1, step, 0)

    over_col(lambda to, j: pl.semaphore_signal(barrier, inc=1, device_id=(me, to), device_id_type=MESH))
    over_row(lambda to, j: pl.semaphore_signal(barrier, inc=1, device_id=(to, z), device_id_type=MESH))

    def start(src, dst, number, device):
        pltpu.make_async_remote_copy(
            src_ref=src, dst_ref=dst, send_sem=sem.at[2 * number], recv_sem=sem.at[2 * number + 1],
            device_id=device, device_id_type=MESH,
        ).start()

    def wait_bytes(like, index):
        pltpu.make_async_copy(like, like, sem.at[index]).wait()

    flying, landed = {}, {}

    def expect(number, like):
        flying[number] = like

    def arrived(number):
        landed[number] = flying.pop(number)
        wait_bytes(landed[number], 2 * number + 1)

    def finish():
        for number in tuple(flying):
            arrived(number)
        for number, like in landed.items():
            wait_bytes(like, 2 * number)

    def to_row(src, dst, number):
        over_row(lambda to, j: start(src, dst.at[j], number, (to, z)))
        expect(number, dst)

    def to_col(src, dst, number):
        over_col(lambda to, j: start(src, dst.at[j], number, (me, to)))
        expect(number, dst)

    def at(offset, size, unit):
        return pl.ds(offset if isinstance(offset, int) else pl.multiple_of(offset, unit), size)

    def each(count, body):
        lax.fori_loop(0, count, lambda k, c: (body(k), c)[1], 0)

    tiles = [slice(k * LANES, (k + 1) * LANES) for k in range(max(hist, width) // LANES)]
    plan_tiles = tiles[:hist // LANES]
    blocks = gen // LANES

    def block(k):
        return at(k * LANES, LANES, LANES)

    def fold(v):
        return jnp.sum(v.reshape(LANES // 8, 8, LANES), axis=0)

    def squares(ref, rows, across):
        total = jnp.zeros((LANES, LANES), F32)
        for cols in across:
            v = ref[rows, cols].astype(F32)
            total = total + v * v
        return total

    def rows_from_column(column, dst, total):
        for k in range(dst.shape[0]):
            turned = jnp.transpose(column[tiles[k], :])
            dst[k:k + 1, :] = jnp.sum(turned, axis=0, keepdims=True) if total else turned[0:1, :]

    def column_from_rows(rows, column):
        for k in range(rows.shape[0]):
            column[tiles[k], :] = jnp.transpose(jnp.broadcast_to(rows[k:k + 1, :], (LANES, LANES)))

    def dot(a, b):
        return jnp.dot(a, b, preferred_element_type=F32)

    def dot_t(a, b):
        return lax.dot_general(a, b, (((1,), (1,)), ((), ())), preferred_element_type=F32)

    tile_h = min(256, hid)
    tile_g = min(256, width)
    tile_j = min(256, hist)

    for n in range(hid // tile_h):
        cols = slice(n * tile_h, (n + 1) * tile_h)
        preact = dot(noise[...], w_first[:, cols])
        s.mult[:, cols] = preact
        s.hidden[:, cols] = (preact / (1.0 + jnp.exp(-preact))).astype(BF16)

    load_w.wait()

    for n in range(width // tile_g):
        cols = slice(n * tile_g, (n + 1) * tile_g)
        s.surface[:, cols] = dot(s.hidden[...], w_second[:, cols]).astype(BF16)
        for k in range(blocks):
            total = squares(s.surface, tiles[k], tiles[n * tile_g // LANES:(n + 1) * tile_g // LANES])
            s.surf_sq[tiles[k], :] = total if n == 0 else s.surf_sq[tiles[k], :] + total
    s.surf_sq[...] = jnp.broadcast_to(jnp.sum(s.surf_sq[...], axis=1, keepdims=True), (gen, LANES))

    load_h.wait()
    for n in range(hist // tile_j):
        wide = slice(n * tile_j, (n + 1) * tile_j)
        s.plan[:, wide] = dot_t(s.surface[...], history[wide, :])
        for c in range(n * tile_j // LANES, (n + 1) * tile_j // LANES):
            top = None
            for k in range(blocks):
                cost = (s.surf_sq[tiles[k], :] - 2.0 * s.plan[tiles[k], tiles[c]]) * (1.0 / width)
                scores = cost * (-1.0 / EPSILON)
                s.plan[tiles[k], tiles[c]] = scores
                tall = jnp.max(scores.reshape(LANES // 8, 8, LANES), axis=0)
                top = tall if top is None else jnp.maximum(top, tall)
            top = jnp.max(top, axis=0, keepdims=True)
            total = jnp.zeros((8, LANES), F32)
            for k in range(blocks):
                total = total + fold(jnp.exp(s.plan[tiles[k], tiles[c]] - top))
            s.m_lse[c:c + 1, :] = top + jnp.log(jnp.sum(total, axis=0, keepdims=True))

    pl.semaphore_wait(barrier, n_row - 1 + n_col - 1)
    to_row(s.m_lse, s.m_lse_in, 0)

    def hist_w_tile(n):
        rows = at(n * 256, min(256, hist), min(256, hist))
        prod = dot_t(history[rows, :], w_second[...])
        hi = prod.astype(BF16)
        s.hist_w_hi[rows, :] = hi
        s.hist_w_lo[rows, :] = (prod - hi.astype(F32)).astype(BF16)
    each(hist // min(256, hist), hist_w_tile)

    def hist_squares(k):
        s.hist_sq[pl.ds(k, 1), :] = jnp.sum(
            jnp.transpose(squares(history, block(k), tiles[:width // LANES])), axis=0, keepdims=True)
    each(hist // LANES, hist_squares)
    hist_cost = s.hist_sq[...] * (1.0 / width) * (1.0 / EPSILON)

    arrived(0)
    top = jnp.maximum(jnp.max(s.m_lse_in[...], axis=0), s.m_lse[...])
    total = jnp.sum(jnp.exp(s.m_lse_in[...] - top[None]), axis=0) + jnp.exp(s.m_lse[...] - top)
    g_first = math.log(gen_total) - (top + jnp.log(total) - hist_cost)
    s.m_row[0] = g_first - hist_cost

    def row_tops(k):
        rows = block(k)
        top = s.plan[rows, plan_tiles[0]] + s.m_row[0, 0:1, :]
        for n, cols in enumerate(plan_tiles[1:], 1):
            top = jnp.maximum(top, s.plan[rows, cols] + s.m_row[0, n:n + 1, :])
        s.row_a[rows, :] = top
    for k in range(blocks):
        row_tops(k)
    s.row_a[...] = jnp.broadcast_to(jnp.max(s.row_a[...], axis=1, keepdims=True), (gen, LANES))

    def first_rows(k):
        rows = block(k)
        top, total = s.row_a[rows, :], jnp.zeros((LANES, LANES), F32)
        for n, cols in enumerate(plan_tiles):
            grown = jnp.exp(s.plan[rows, cols] + s.m_row[0, n:n + 1, :] - top)
            s.plan[rows, cols] = grown
            total = total + grown
        s.row_b[rows, :] = total
    for k in range(blocks):
        first_rows(k)
    rows_from_column(s.row_a, s.row_top, False)
    rows_from_column(s.row_b, s.row_lse, True)
    s.row_lse[...] = s.row_top[...] + jnp.log(s.row_lse[...])
    to_col(s.row_lse, s.row_lse_in, 1)

    def surf_w_tile(n):
        cols = at(n * tile_h, tile_h, tile_h)
        s.surf_w[:, cols] = dot_t(s.surface[...], w_second[cols, :])
    each(hid // tile_h, surf_w_tile)
    s.hidden_t[...] = jnp.transpose(s.hidden[...].astype(F32)).astype(BF16)

    pair = at(lax.div(z, 2) * LANES, LANES, LANES)
    prod = dot(s.hidden_t[...], s.surface[:, pair])
    turned = pltpu.roll(prod, 64, axis=1)
    s.term_a[...] = jnp.where(odd, turned, prod)
    s.term_b[...] = jnp.where(odd, prod, turned)
    low = lax.broadcasted_iota(jnp.int32, (8, LANES), 1) < 64

    def owner_term(o):
        oc, ox, oy = lax.rem(o, 2), lax.rem(o // 2, nx), o // (2 * nx)
        upper = oc * half + oy * (quarter // ny) + ox * 8
        lower = oc * half + quarter + ox * (quarter // nx) + oy * 8
        s.term[o] = jnp.where(low, s.term_a[at(upper, 8, 8), :], s.term_b[at(lower, 8, 8), :])
    each(n_row, owner_term)

    over_row(lambda to, j: start(s.term.at[to], s.term_in.at[j], 6, (to, z)))
    expect(6, s.term_in)

    arrived(1)
    top = jnp.maximum(jnp.max(s.row_lse_in[...], axis=0), s.row_lse[...])
    total = jnp.sum(jnp.exp(s.row_lse_in[...] - top[None]), axis=0) + jnp.exp(s.row_lse[...] - top)
    column_from_rows(jnp.exp(s.row_top[...] - top) / total, s.row_a)

    def column_sums(scaled, dst):
        def step(k, sums):
            rows, out = block(k), []
            own = s.row_a[rows, :]
            for cols, total in zip(plan_tiles, sums):
                v = s.plan[rows, cols] * own
                if scaled:
                    s.plan[rows, cols] = v
                out.append(total + fold(v))
            return tuple(out)
        sums = [jnp.zeros((8, LANES), F32) for _ in plan_tiles]
        for k in range(blocks):
            sums = step(k, sums)
        for k, total in enumerate(sums):
            dst[k:k + 1, :] = jnp.sum(total, axis=0, keepdims=True)

    def row_sums(k):
        rows = block(k)
        total = jnp.zeros((LANES, LANES), F32)
        for n, cols in enumerate(plan_tiles):
            total = total + s.plan[rows, cols] * s.col_b[n:n + 1, :]
        s.row_b[rows, :] = total

    def unscaled_rows(k):
        rows = block(k)
        for n, cols in enumerate(plan_tiles):
            v = s.plan[rows, cols] * s.col_b[n:n + 1, :]
            hi = v.astype(BF16)
            s.plan_hi[rows, cols] = hi
            s.plan_lo[rows, cols] = (v - hi.astype(F32)).astype(BF16)

    def value_tile(n):
        cols = at(n * tile_h, tile_h, tile_h)
        s.value[:, cols] = (dot(s.plan_hi[...], s.hist_w_hi[:, cols]) + dot(s.plan_hi[...], s.hist_w_lo[:, cols])
                            + dot(s.plan_lo[...], s.hist_w_hi[:, cols]))

    for sweep in range(1, SWEEPS):
        number = 2 * sweep
        mine, theirs = s.m_row.at[sweep], s.m_row_in.at[sweep - 1]
        column_sums(sweep == 1, mine)
        to_row(mine, theirs, number)
        if sweep == 1:
            preact = s.mult[...]
            sigma = 1.0 / (1.0 + jnp.exp(-preact))
            s.mult[...] = sigma * (1.0 + preact * (1.0 - sigma))
            s.noise_t[...] = jnp.transpose(noise[...].astype(F32)).astype(BF16)
        arrived(number)
        total = mine[...] + jnp.sum(theirs[...], axis=0)
        s.col_b[...] = (gen_total / hist_total) / total

        for k in range(blocks):
            row_sums(k)
        mine, theirs = s.m_col.at[sweep - 1], s.m_col_in.at[sweep - 1]
        rows_from_column(s.row_b, mine, True)
        to_col(mine, theirs, number + 1)
        if sweep == SWEEPS - 1:
            for k in range(blocks):
                unscaled_rows(k)
            each(hid // tile_h, value_tile)
        arrived(number + 1)
        total = mine[...] + jnp.sum(theirs[...], axis=0)
        column_from_rows(1.0 / total, s.row_a)

    def weight_rows(k):
        rows = block(k)
        own = s.row_a[rows, :]
        for n, cols in enumerate(plan_tiles):
            s.weights[rows, cols] = (s.plan[rows, cols] * own * s.col_b[n:n + 1, :]).astype(BF16)
    for k in range(blocks):
        weight_rows(k)

    def acc_tile(which):
        rows = at(which * half, half, half)

        def body(n):
            cols = at(n * tile_j, tile_j, tile_j)
            s.acc[rows, cols] = dot(s.hidden_t[rows, :], s.weights[:, cols])
        each(hist // tile_j, body)

    span_x, span_y = quarter // nx, quarter // ny
    base_u, base_l = core * half, core * half + quarter
    sibling = (me + 1 - 2 * core, z)
    acc_tile(other)
    order = [pair for k in range(1, nx) for pair in ((True, k), (False, k))] + [(True, 0), (False, 0)]

    def block_rows(upper, k):
        return lax.rem(y + k, ny) * span_y if upper else quarter + lax.rem(x + k, nx) * span_x

    for n, (upper, k) in enumerate(order):
        rows = block_rows(upper, k)
        start(s.acc.at[at(other * half + rows, span_x, 8), :], s.acc_in.at[at(rows, span_x, 8), :], 20 + n, sibling)
        expect(20 + n, s.acc_in.at[at(n * span_x, span_x, 8), :])

    def chip_at(upper, k, first):
        if upper == first:
            return (y * nx + lax.rem(x + k, nx)) * 2 + core, lax.rem(x + k, nx) * 8
        return (lax.rem(y + k, ny) * nx + x) * 2 + core, lax.rem(y + k, ny) * 8

    def pass_on(n):
        upper, k = order[n]
        rows = block_rows(upper, k)
        arrived(20 + n)
        mine = at(core * half + rows, span_x, 8)
        s.acc[mine, :] = s.acc[mine, :] + s.acc_in[at(rows, span_x, 8), :]
        into = s.x_in if upper else s.y_in
        for j in range(1, nx):
            device, offset = chip_at(upper, j, True)
            start(s.acc.at[at(core * half + rows + offset, 8, 8), :], into.at[k, j - 1], 30 + n, (device, z))
        expect(30 + n, into.at[k])

    def pass_second(n):
        upper, k = order[n]
        arrived(30 + n)
        rows = at(core * half + block_rows(upper, k) + chip_at(upper, 0, True)[1], 8, 8)
        total = s.acc[rows, :] + jnp.sum((s.x_in if upper else s.y_in)[k], axis=0)
        if k == 0:
            return total
        s.acc[rows, :] = total
        into = s.y_in2 if upper else s.x_in2
        start(s.acc.at[rows, :], into.at[k - 1], 13 if upper else 14, (chip_at(upper, k, False)[0], z))

    for k in range(blocks):
        for cols in tiles[:hid // LANES]:
            rows = tiles[k]
            d_hidden = (s.surf_w[rows, cols] * (1.0 / n_col) - s.value[rows, cols] * s.row_a[rows, :]) * scale
            d_preact = d_hidden * s.mult[rows, cols]
            hi = d_preact.astype(BF16)
            s.d_hi[rows, cols] = hi
            s.d_lo[rows, cols] = (d_preact - hi.astype(F32)).astype(BF16)
    s.first[...] = dot(s.noise_t[...], s.d_hi[...]) + dot(s.noise_t[...], s.d_lo[...])
    start(s.first.at[:, at(other * half, half, half)], s.first_in, 8, sibling)
    expect(8, s.first_in)
    acc_tile(core)

    for n in range(len(order)):
        pass_on(n)

    arrived(8)
    s.first_half[...] = s.first[:, at(core * half, half, half)] + s.first_in[...]
    piece = zdim // chips
    over_chips(lambda to, j: start(
        s.first_half.at[at(to * piece, piece, 8), :], s.first_chip_in.at[j], 11, (to * 2 + core, z)))
    expect(11, s.first_chip_in)
    for n in range(len(order) - 2):
        pass_second(n)
    expect(13, s.y_in2)
    expect(14, s.x_in2)
    arrived(11)
    s.first_piece[0] = s.first_half[at(chip * piece, piece, 8), :] + jnp.sum(s.first_chip_in[...], axis=0)
    to_col(s.first_piece.at[0], s.first_z_in, 12)
    own_u, own_l = pass_second(len(order) - 2), pass_second(len(order) - 1)
    arrived(13)
    arrived(14)
    s.reduced[0:8, :] = own_u + jnp.sum(s.y_in2[...], axis=0)
    s.reduced[8:16, :] = own_l + jnp.sum(s.x_in2[...], axis=0)

    hi = s.reduced[...].astype(BF16)
    lo = (s.reduced[...] - hi.astype(F32)).astype(BF16)
    both = jnp.concatenate([hi, lo], axis=0)

    low = lax.broadcasted_iota(jnp.int32, (8, LANES), 1) < 64
    for n in range(width // tile_g):
        prod = dot(both, history[:, n * tile_g:(n + 1) * tile_g])
        prod = prod[0:16] + prod[16:32]
        for c in range(tile_g // LANES):
            upper, lower = prod[0:8, tiles[c]], prod[8:16, tiles[c]]
            k = 2 * (n * tile_g // LANES + c)
            s.slices[k] = jnp.where(low, upper, pltpu.roll(lower, 64, axis=1))
            s.slices[k + 1] = jnp.where(low, pltpu.roll(upper, 64, axis=1), lower)

    over_col(lambda to, j: start(s.slices.at[to], s.slices_in.at[j], 15, (me, to)))
    expect(15, s.slices_in)

    arrived(12)
    s.first_all[me] = s.first_piece[0] + jnp.sum(s.first_z_in[...], axis=0)
    over_row(lambda to, j: start(s.first_all.at[me], s.first_all.at[me], 16, (to, z)))
    expect(16, s.first_all.at[pl.ds(0, n_row - 1)])

    arrived(6)
    term = s.term[me] + jnp.sum(s.term_in[...], axis=0)
    arrived(15)
    mixed = s.slices[z] + jnp.sum(s.slices_in[...], axis=0)
    s.second_all[me] = (term - mixed) * scale

    over_row(lambda to, j: start(s.second_all.at[me], s.second_all.at[me], 17, (to, z)))
    expect(17, s.second_all.at[pl.ds(0, n_row - 1)])

    arrived(16)
    out_first[...] = s.first_all[...]
    arrived(17)
    out_second[...] = s.second_all[...]
    finish()


def place(geometry, first, second, out_first, out_second, wide):
    ny, nx, nz = geometry
    half, piece = out_first.shape[1] // 2, first.shape[1]
    quarter = half // 2
    for y in range(ny):
        for x in range(nx):
            chip = y * nx + x
            for c in range(2):
                out_first[chip * piece:(chip + 1) * piece, c * half:(c + 1) * half] = first[2 * chip + c]
                upper = c * half + y * (quarter // ny) + x * 8
                lower = c * half + quarter + x * (quarter // nx) + y * 8
                v = second[2 * chip + c]
                wide[upper:upper + 8, :] = v
                wide[lower:lower + 8, :] = pltpu.roll(v, 64, axis=1)
    for k in range(wide.shape[0] // LANES):
        out_second[:, k * LANES:(k + 1) * LANES] = jnp.transpose(wide[k * LANES:(k + 1) * LANES, :])[0:64, :]


def shards(geometry, noise, w_first, w_second, history):
    ny, nx, nz = geometry
    chips = ny * nx
    n_row = 2 * chips
    gen, zdim = noise.shape
    hist, width = history.shape
    hid = w_first.shape[1]
    half, quarter = hid // 2, hid // 4
    piece = zdim // chips
    jr, ir = hist // LANES, gen // LANES
    shapes = dict(
        w_second=((hid, width), BF16), history=((hist, width), BF16),
        hidden=((gen, hid), BF16), hidden_t=((hid, gen), BF16), noise_t=((zdim, gen), BF16),
        surface=((gen, width), BF16), mult=((gen, hid), F32), surf_w=((gen, hid), F32),
        hist_w_hi=((hist, hid), BF16), hist_w_lo=((hist, hid), BF16),
        plan=((gen, hist), F32), weights=((gen, hist), BF16),
        surf_sq=((gen, LANES), F32), hist_sq=((jr, LANES), F32),
        row_a=((gen, LANES), F32), row_b=((gen, LANES), F32), col_b=((jr, LANES), F32),
        m_lse=((jr, LANES), F32), m_lse_in=((n_row - 1, jr, LANES), F32),
        row_top=((ir, LANES), F32), row_lse=((ir, LANES), F32), row_lse_in=((nz - 1, ir, LANES), F32),
        plan_hi=((gen, hist), BF16), plan_lo=((gen, hist), BF16), value=((gen, hid), F32),
        d_hi=((gen, hid), BF16), d_lo=((gen, hid), BF16),
        m_row=((SWEEPS, jr, LANES), F32), m_row_in=((SWEEPS - 1, n_row - 1, jr, LANES), F32),
        m_col=((SWEEPS - 1, ir, LANES), F32), m_col_in=((SWEEPS - 1, nz - 1, ir, LANES), F32),
        acc=((hid, hist), F32), acc_in=((half, hist), F32),
        x_in=((ny, nx - 1, 8, hist), F32), y_in=((nx, ny - 1, 8, hist), F32),
        x_in2=((nx - 1, 8, hist), F32), y_in2=((ny - 1, 8, hist), F32), reduced=((16, hist), F32),
        first=((zdim, hid), F32), first_in=((zdim, half), F32), first_half=((zdim, half), F32),
        first_chip_in=((chips - 1, piece, half), F32), first_piece=((1, piece, half), F32),
        first_z_in=((nz - 1, piece, half), F32), first_all=((n_row, piece, half), F32),
        term_a=((hid, LANES), F32), term_b=((hid, LANES), F32),
        term=((n_row, 8, LANES), F32), term_in=((n_row - 1, 8, LANES), F32),
        slices=((nz, 8, LANES), F32), slices_in=((nz - 1, 8, LANES), F32),
        second_all=((n_row, 8, LANES), F32),
    )
    scratch = [pltpu.VMEM(*shape) for shape in shapes.values()] + [pltpu.SemaphoreType.DMA((80,))]
    vmem = pl.BlockSpec(memory_space=pltpu.VMEM)
    first, second = pl.pallas_call(
        functools.partial(kernel, geometry, tuple(shapes)),
        out_shape=(
            jax.ShapeDtypeStruct((n_row, piece, half), F32),
            jax.ShapeDtypeStruct((n_row, 8, LANES), F32),
        ),
        in_specs=[vmem] * 2 + [pl.BlockSpec(memory_space=pl.ANY)] * 2,
        out_specs=(vmem, vmem),
        scratch_shapes=scratch,
        compiler_params=pltpu.CompilerParams(
            collective_id=0, has_side_effects=True, vmem_limit_bytes=56 * 1024 * 1024
        ),
        name="transport",
    )(noise, w_first, w_second, history)
    grad_first, turned = pl.pallas_call(
        functools.partial(place, geometry),
        out_shape=(
            jax.ShapeDtypeStruct((zdim, hid), F32),
            jax.ShapeDtypeStruct((width // nz, hid), F32),
        ),
        in_specs=[vmem] * 2,
        out_specs=(vmem, vmem),
        scratch_shapes=[pltpu.VMEM((hid, LANES), F32)],
        name="place",
    )(first, second)
    return grad_first, turned.T


def solution(mesh):
    chips = mesh.shape["row"] // 2
    nx = math.isqrt(chips)
    geometry = (chips // nx, nx, mesh.shape["col"])
    placed = (P("row", None), P(), P(), P("col", None))
    return jax.shard_map(
        functools.partial(shards, geometry), mesh=mesh, in_specs=placed,
        out_specs=(P(), P(None, "col")), check_vma=False,
    )
```

```python
import functools
import math
from types import SimpleNamespace

import jax
import jax.numpy as jnp
from jax import lax
from jax.experimental import pallas as pl
from jax.experimental.pallas import tpu as pltpu
from jax.sharding import PartitionSpec as P

SWEEPS = 3
EPSILON = 0.01
MESH = pl.DeviceIdType.MESH
F32 = jnp.float32
BF16 = jnp.bfloat16
LANES = 128


def kernel(geometry, names, noise_hbm, w_first_hbm, w_second_hbm, history_hbm, out_first, out_second, *scratch):
    ny, nx, nz = geometry
    chips = ny * nx
    n_row, n_col = 2 * chips, nz
    s = SimpleNamespace(**dict(zip(names, scratch)))
    sem = scratch[-1]
    noise, w_first, w_second, history = s.noise, s.w_first, s.w_second, s.history
    load_n = pltpu.make_async_copy(noise_hbm, noise, sem.at[76])
    load_f = pltpu.make_async_copy(w_first_hbm, w_first, sem.at[77])
    load_w = pltpu.make_async_copy(w_second_hbm, w_second, sem.at[78])
    load_h = pltpu.make_async_copy(history_hbm, history, sem.at[79])
    load_n.start()
    load_f.start()
    load_w.start()
    load_h.start()
    gen, zdim = noise.shape
    hist, width = history.shape
    hid = w_first.shape[1]
    half = hid // 2
    quarter = half // 2
    gen_total, hist_total = gen * n_row, hist * n_col
    scale = 1.0 / math.sqrt(gen_total)

    me = lax.axis_index("row")
    z = lax.axis_index("col")
    core = lax.rem(me, 2)
    other = 1 - core
    chip = me // 2
    x = lax.rem(chip, nx)
    y = chip // nx
    odd = lax.rem(z, 2) == 1
    sibling = (me + 1 - 2 * core, z)

    barrier = pltpu.get_barrier_semaphore()

    def far(a, n):
        return lax.rem(n // 2 + n * n - a * (a + 1) // 2, n)

    def over_chips(send):
        def step(j, c):
            to_y, to_x = lax.rem(y + far(j // nx, ny), ny), lax.rem(x + far(lax.rem(j, nx), nx), nx)
            send(to_y * nx + to_x, j)
            return c
        lax.fori_loop(0, chips - 1, step, 0)

    def over_row(send):
        def step(j, c):
            k = j // 2
            to_y, to_x = lax.rem(y + far(k // nx, ny), ny), lax.rem(x + far(lax.rem(k, nx), nx), nx)
            send((to_y * nx + to_x) * 2 + lax.rem(core + 1 + j, 2), j)
            return c
        lax.fori_loop(0, n_row - 1, step, 0)

    def over_col(send):
        def step(j, c):
            send(lax.rem(z + n_col // 2 + (j + 1) // 2 * (1 - 2 * lax.rem(j, 2)), n_col), j)
            return c
        lax.fori_loop(0, n_col - 1, step, 0)

    over_col(lambda to, j: pl.semaphore_signal(barrier, inc=1, device_id=(me, to), device_id_type=MESH))
    over_row(lambda to, j: pl.semaphore_signal(barrier, inc=1, device_id=(to, z), device_id_type=MESH))

    def start(src, dst, number, device):
        pltpu.make_async_remote_copy(
            src_ref=src, dst_ref=dst, send_sem=sem.at[2 * number], recv_sem=sem.at[2 * number + 1],
            device_id=device, device_id_type=MESH,
        ).start()

    def wait_bytes(like, index):
        pltpu.make_async_copy(like, like, sem.at[index]).wait()

    flying, landed = {}, {}

    def expect(number, like):
        flying[number] = like

    def arrived(number):
        landed[number] = flying.pop(number)
        wait_bytes(landed[number], 2 * number + 1)

    def finish():
        for number in tuple(flying):
            arrived(number)
        for number, like in landed.items():
            wait_bytes(like, 2 * number)

    def to_row(src, dst, number):
        over_row(lambda to, j: start(src, dst.at[j], number, (to, z)))
        expect(number, dst)

    def to_col(src, dst, number):
        over_col(lambda to, j: start(src, dst.at[j], number, (me, to)))
        expect(number, dst)

    def at(offset, size, unit):
        return pl.ds(offset if isinstance(offset, int) else pl.multiple_of(offset, unit), size)

    def each(count, body):
        lax.fori_loop(0, count, lambda k, c: (body(k), c)[1], 0)

    tiles = [slice(k * LANES, (k + 1) * LANES) for k in range(max(hist, width) // LANES)]
    plan_tiles = tiles[:hist // LANES]
    blocks = gen // LANES

    def block(k):
        return at(k * LANES, LANES, LANES)

    def fold(v):
        return jnp.sum(v.reshape(LANES // 8, 8, LANES), axis=0)

    def squares(ref, rows, across):
        total = jnp.zeros((LANES, LANES), F32)
        for cols in across:
            v = ref[rows, cols].astype(F32)
            total = total + v * v
        return total

    def rows_from_column(column, dst, total):
        for k in range(dst.shape[0]):
            turned = jnp.transpose(column[tiles[k], :])
            dst[k:k + 1, :] = jnp.sum(turned, axis=0, keepdims=True) if total else turned[0:1, :]

    def column_from_rows(rows, column):
        for k in range(rows.shape[0]):
            column[tiles[k], :] = jnp.transpose(jnp.broadcast_to(rows[k:k + 1, :], (LANES, LANES)))

    def dot(a, b):
        return jnp.dot(a, b, preferred_element_type=F32)

    def dot_t(a, b):
        return lax.dot_general(a, b, (((1,), (1,)), ((), ())), preferred_element_type=F32)

    tile_h = min(256, hid)
    tile_g = min(256, width)
    tile_j = min(256, hist)

    load_n.wait()
    load_f.wait()

    for n in range(hid // tile_h):
        cols = slice(n * tile_h, (n + 1) * tile_h)
        preact = dot(noise[...], w_first[:, cols])
        s.mult[:, cols] = preact
        s.hidden[:, cols] = (preact / (1.0 + jnp.exp(-preact))).astype(BF16)

    load_w.wait()

    for n in range(width // tile_g):
        cols = slice(n * tile_g, (n + 1) * tile_g)
        s.surface[:, cols] = dot(s.hidden[...], w_second[:, cols]).astype(BF16)
        for k in range(blocks):
            total = squares(s.surface, tiles[k], tiles[n * tile_g // LANES:(n + 1) * tile_g // LANES])
            s.surf_sq[tiles[k], :] = total if n == 0 else s.surf_sq[tiles[k], :] + total
    s.surf_sq[...] = jnp.broadcast_to(jnp.sum(s.surf_sq[...], axis=1, keepdims=True), (gen, LANES))

    load_h.wait()
    for n in range(hist // tile_j):
        wide = slice(n * tile_j, (n + 1) * tile_j)
        s.plan[:, wide] = dot_t(s.surface[...], history[wide, :])
        for c in range(n * tile_j // LANES, (n + 1) * tile_j // LANES):
            top = None
            for k in range(blocks):
                cost = (s.surf_sq[tiles[k], :] - 2.0 * s.plan[tiles[k], tiles[c]]) * (1.0 / width)
                scores = cost * (-1.0 / EPSILON)
                s.plan[tiles[k], tiles[c]] = scores
                tall = jnp.max(scores.reshape(LANES // 8, 8, LANES), axis=0)
                top = tall if top is None else jnp.maximum(top, tall)
            top = jnp.max(top, axis=0, keepdims=True)
            total = jnp.zeros((8, LANES), F32)
            for k in range(blocks):
                total = total + fold(jnp.exp(s.plan[tiles[k], tiles[c]] - top))
            s.m_lse[c:c + 1, :] = top + jnp.log(jnp.sum(total, axis=0, keepdims=True))

    pl.semaphore_wait(barrier, n_row - 1 + n_col - 1)
    to_row(s.m_lse, s.m_lse_in, 0)

    def hist_w_tile(n):
        rows = at(n * 256, min(256, hist), min(256, hist))
        prod = dot_t(history[rows, :], w_second[...])
        hi = prod.astype(BF16)
        s.hist_w_hi[rows, :] = hi
        s.hist_w_lo[rows, :] = (prod - hi.astype(F32)).astype(BF16)
    each(hist // min(256, hist), hist_w_tile)

    def hist_squares(k):
        s.hist_sq[pl.ds(k, 1), :] = jnp.sum(
            jnp.transpose(squares(history, block(k), tiles[:width // LANES])), axis=0, keepdims=True)
    each(hist // LANES, hist_squares)
    hist_cost = s.hist_sq[...] * (1.0 / width) * (1.0 / EPSILON)

    arrived(0)
    top = jnp.maximum(jnp.max(s.m_lse_in[...], axis=0), s.m_lse[...])
    total = jnp.sum(jnp.exp(s.m_lse_in[...] - top[None]), axis=0) + jnp.exp(s.m_lse[...] - top)
    g_first = math.log(gen_total) - (top + jnp.log(total) - hist_cost)
    s.m_row[0] = g_first - hist_cost

    def row_tops(k):
        rows = block(k)
        top = s.plan[rows, plan_tiles[0]] + s.m_row[0, 0:1, :]
        for n, cols in enumerate(plan_tiles[1:], 1):
            top = jnp.maximum(top, s.plan[rows, cols] + s.m_row[0, n:n + 1, :])
        s.row_a[rows, :] = top
    for k in range(blocks):
        row_tops(k)
    s.row_a[...] = jnp.broadcast_to(jnp.max(s.row_a[...], axis=1, keepdims=True), (gen, LANES))

    def first_rows(k):
        rows = block(k)
        top, total = s.row_a[rows, :], jnp.zeros((LANES, LANES), F32)
        for n, cols in enumerate(plan_tiles):
            grown = jnp.exp(s.plan[rows, cols] + s.m_row[0, n:n + 1, :] - top)
            s.plan[rows, cols] = grown
            total = total + grown
        s.row_b[rows, :] = total
    for k in range(blocks):
        first_rows(k)
    rows_from_column(s.row_a, s.row_top, False)
    rows_from_column(s.row_b, s.row_lse, True)
    s.row_lse[...] = s.row_top[...] + jnp.log(s.row_lse[...])
    to_col(s.row_lse, s.row_lse_in, 1)

    def surf_w_tile(n):
        cols = at(n * tile_h, tile_h, tile_h)
        s.surf_w[:, cols] = dot_t(s.surface[...], w_second[cols, :])
    each(hid // tile_h, surf_w_tile)
    s.hidden_t[...] = jnp.transpose(s.hidden[...].astype(F32)).astype(BF16)

    pair = at(lax.div(z, 2) * LANES, LANES, LANES)
    prod = dot(s.hidden_t[...], s.surface[:, pair])
    turned = pltpu.roll(prod, 64, axis=1)
    s.term_a[...] = jnp.where(odd, turned, prod)
    s.term_b[...] = jnp.where(odd, prod, turned)
    low = lax.broadcasted_iota(jnp.int32, (8, LANES), 1) < 64

    def owner_term(o):
        oc, ox, oy = lax.rem(o, 2), lax.rem(o // 2, nx), o // (2 * nx)
        upper = oc * half + oy * (quarter // ny) + ox * 8
        lower = oc * half + quarter + ox * (quarter // nx) + oy * 8
        s.term[o] = jnp.where(low, s.term_a[at(upper, 8, 8), :], s.term_b[at(lower, 8, 8), :])
    each(n_row, owner_term)

    over_row(lambda to, j: start(s.term.at[to], s.term_in.at[j], 6, (to, z)))
    expect(6, s.term_in)

    arrived(1)
    top = jnp.maximum(jnp.max(s.row_lse_in[...], axis=0), s.row_lse[...])
    total = jnp.sum(jnp.exp(s.row_lse_in[...] - top[None]), axis=0) + jnp.exp(s.row_lse[...] - top)
    column_from_rows(jnp.exp(s.row_top[...] - top) / total, s.row_a)

    def column_sums(scaled, dst):
        def step(k, sums):
            rows, out = block(k), []
            own = s.row_a[rows, :]
            for cols, total in zip(plan_tiles, sums):
                v = s.plan[rows, cols] * own
                if scaled:
                    s.plan[rows, cols] = v
                out.append(total + fold(v))
            return tuple(out)
        sums = [jnp.zeros((8, LANES), F32) for _ in plan_tiles]
        for k in range(blocks):
            sums = step(k, sums)
        for k, total in enumerate(sums):
            dst[k:k + 1, :] = jnp.sum(total, axis=0, keepdims=True)

    def row_sums(k):
        rows = block(k)
        total = jnp.zeros((LANES, LANES), F32)
        for n, cols in enumerate(plan_tiles):
            total = total + s.plan[rows, cols] * s.col_b[n:n + 1, :]
        s.row_b[rows, :] = total

    def unscaled_rows(k):
        rows = block(k)
        for n, cols in enumerate(plan_tiles):
            v = s.plan[rows, cols] * s.col_b[n:n + 1, :]
            s.plan[rows, cols] = v
            hi = v.astype(BF16)
            s.plan_hi[rows, cols] = hi
            s.plan_lo[rows, cols] = (v - hi.astype(F32)).astype(BF16)

    def value_tile(n):
        cols = at(n * tile_h, tile_h, tile_h)
        s.value[:, cols] = (dot(s.plan_hi[...], s.hist_w_hi[:, cols]) + dot(s.plan_hi[...], s.hist_w_lo[:, cols])
                            + dot(s.plan_lo[...], s.hist_w_hi[:, cols]))

    for sweep in range(1, SWEEPS):
        number = 2 * sweep
        mine, theirs = s.m_row.at[sweep], s.m_row_in.at[sweep - 1]
        column_sums(sweep == 1, mine)
        to_row(mine, theirs, number)
        if sweep == 1:
            preact = s.mult[...]
            sigma = 1.0 / (1.0 + jnp.exp(-preact))
            s.mult[...] = sigma * (1.0 + preact * (1.0 - sigma))
            s.noise_t[...] = jnp.transpose(noise[...].astype(F32)).astype(BF16)
        arrived(number)
        total = mine[...] + jnp.sum(theirs[...], axis=0)
        s.col_b[...] = (gen_total / hist_total) / total

        for k in range(blocks):
            row_sums(k)
        mine, theirs = s.m_col.at[sweep - 1], s.m_col_in.at[sweep - 1]
        rows_from_column(s.row_b, mine, True)
        to_col(mine, theirs, number + 1)
        if sweep == SWEEPS - 1:
            for k in range(blocks):
                unscaled_rows(k)
            each(hid // tile_h, value_tile)
        arrived(number + 1)
        total = mine[...] + jnp.sum(theirs[...], axis=0)
        column_from_rows(1.0 / total, s.row_a)

    for k in range(blocks):
        for cols in tiles[:hid // LANES]:
            rows = tiles[k]
            d_hidden = (s.surf_w[rows, cols] * (1.0 / n_col) - s.value[rows, cols] * s.row_a[rows, :]) * scale
            d_preact = d_hidden * s.mult[rows, cols]
            hi = d_preact.astype(BF16)
            s.d_hi[rows, cols] = hi
            s.d_lo[rows, cols] = (d_preact - hi.astype(F32)).astype(BF16)
    s.first[...] = dot(s.noise_t[...], s.d_hi[...]) + dot(s.noise_t[...], s.d_lo[...])
    start(s.first.at[:, at(other * half, half, half)], s.first_in, 8, sibling)
    expect(8, s.first_in)
    piece = zdim // chips

    def send_pieces():
        arrived(8)
        s.first_half[...] = s.first[:, at(core * half, half, half)] + s.first_in[...]
        over_chips(lambda to, j: start(
            s.first_half.at[at(to * piece, piece, 8), :], s.first_chip_in.at[j], 11, (to * 2 + core, z)))
        expect(11, s.first_chip_in)

    def weight_rows(k):
        rows = block(k)
        own = s.row_a[rows, :]
        for cols in plan_tiles:
            s.weights[rows, cols] = (s.plan[rows, cols] * own).astype(BF16)
    for k in range(blocks):
        weight_rows(k)

    def acc_tile(which):
        rows = at(which * half, half, half)

        def body(n):
            cols = at(n * tile_j, tile_j, tile_j)
            s.acc[rows, cols] = dot(s.hidden_t[rows, :], s.weights[:, cols])
        each(hist // tile_j, body)

    span_x, span_y = quarter // nx, quarter // ny
    base_u, base_l = core * half, core * half + quarter
    acc_tile(other)
    order = [pair for k in range(1, nx) for pair in ((True, k), (False, k))] + [(True, 0), (False, 0)]

    def block_rows(upper, k):
        return lax.rem(y + k, ny) * span_y if upper else quarter + lax.rem(x + k, nx) * span_x

    for n, (upper, k) in enumerate(order):
        rows = block_rows(upper, k)
        start(s.acc.at[at(other * half + rows, span_x, 8), :], s.acc_in.at[at(rows, span_x, 8), :], 20 + n, sibling)
        expect(20 + n, s.acc_in.at[at(n * span_x, span_x, 8), :])

    def chip_at(upper, k, first):
        if upper == first:
            return (y * nx + lax.rem(x + k, nx)) * 2 + core, lax.rem(x + k, nx) * 8
        return (lax.rem(y + k, ny) * nx + x) * 2 + core, lax.rem(y + k, ny) * 8

    def pass_on(n):
        upper, k = order[n]
        rows = block_rows(upper, k)
        arrived(20 + n)
        mine = at(core * half + rows, span_x, 8)
        s.acc[mine, :] = s.acc[mine, :] + s.acc_in[at(rows, span_x, 8), :]
        into = s.x_in if upper else s.y_in
        for j in range(1, nx):
            device, offset = chip_at(upper, j, True)
            start(s.acc.at[at(core * half + rows + offset, 8, 8), :], into.at[k, j - 1], 30 + n, (device, z))
        expect(30 + n, into.at[k])

    def pass_second(n):
        upper, k = order[n]
        arrived(30 + n)
        rows = at(core * half + block_rows(upper, k) + chip_at(upper, 0, True)[1], 8, 8)
        total = s.acc[rows, :] + jnp.sum((s.x_in if upper else s.y_in)[k], axis=0)
        if k == 0:
            return total
        s.acc[rows, :] = total
        into = s.y_in2 if upper else s.x_in2
        start(s.acc.at[rows, :], into.at[k - 1], 13 if upper else 14, (chip_at(upper, k, False)[0], z))

    send_pieces()
    acc_tile(core)

    for n in range(len(order)):
        pass_on(n)

    for n in range(len(order) - 2):
        pass_second(n)
    expect(13, s.y_in2)
    expect(14, s.x_in2)
    arrived(11)
    s.first_piece[0] = s.first_half[at(chip * piece, piece, 8), :] + jnp.sum(s.first_chip_in[...], axis=0)
    to_col(s.first_piece.at[0], s.first_z_in, 12)
    own_u, own_l = pass_second(len(order) - 2), pass_second(len(order) - 1)
    arrived(13)
    arrived(14)
    s.reduced[0:8, :] = own_u + jnp.sum(s.y_in2[...], axis=0)
    s.reduced[8:16, :] = own_l + jnp.sum(s.x_in2[...], axis=0)

    hi = s.reduced[...].astype(BF16)
    lo = (s.reduced[...] - hi.astype(F32)).astype(BF16)
    both = jnp.concatenate([hi, lo], axis=0)

    low = lax.broadcasted_iota(jnp.int32, (8, LANES), 1) < 64
    for n in range(width // tile_g):
        prod = dot(both, history[:, n * tile_g:(n + 1) * tile_g])
        prod = prod[0:16] + prod[16:32]
        for c in range(tile_g // LANES):
            upper, lower = prod[0:8, tiles[c]], prod[8:16, tiles[c]]
            k = 2 * (n * tile_g // LANES + c)
            s.slices[k] = jnp.where(low, upper, pltpu.roll(lower, 64, axis=1))
            s.slices[k + 1] = jnp.where(low, pltpu.roll(upper, 64, axis=1), lower)

    over_col(lambda to, j: start(s.slices.at[to], s.slices_in.at[j], 15, (me, to)))
    expect(15, s.slices_in)

    arrived(12)
    s.first_all[me] = s.first_piece[0] + jnp.sum(s.first_z_in[...], axis=0)
    over_row(lambda to, j: start(s.first_all.at[me], s.first_all.at[me], 16, (to, z)))
    expect(16, s.first_all.at[pl.ds(0, n_row - 1)])

    arrived(6)
    term = s.term[me] + jnp.sum(s.term_in[...], axis=0)
    arrived(15)
    mixed = s.slices[z] + jnp.sum(s.slices_in[...], axis=0)
    s.second_all[me] = (term - mixed) * scale

    over_row(lambda to, j: start(s.second_all.at[me], s.second_all.at[me], 17, (to, z)))
    expect(17, s.second_all.at[pl.ds(0, n_row - 1)])

    arrived(16)
    out_first[...] = s.first_all[...]
    arrived(17)
    out_second[...] = s.second_all[...]
    finish()


def place(geometry, first, second, out_first, out_second, wide):
    ny, nx, nz = geometry
    half, piece = out_first.shape[1] // 2, first.shape[1]
    quarter = half // 2
    for y in range(ny):
        for x in range(nx):
            chip = y * nx + x
            for c in range(2):
                out_first[chip * piece:(chip + 1) * piece, c * half:(c + 1) * half] = first[2 * chip + c]
                upper = c * half + y * (quarter // ny) + x * 8
                lower = c * half + quarter + x * (quarter // nx) + y * 8
                v = second[2 * chip + c]
                wide[upper:upper + 8, :] = v
                wide[lower:lower + 8, :] = pltpu.roll(v, 64, axis=1)
    for k in range(wide.shape[0] // LANES):
        out_second[:, k * LANES:(k + 1) * LANES] = jnp.transpose(wide[k * LANES:(k + 1) * LANES, :])[0:64, :]


def shards(geometry, noise, w_first, w_second, history):
    ny, nx, nz = geometry
    chips = ny * nx
    n_row = 2 * chips
    gen, zdim = noise.shape
    hist, width = history.shape
    hid = w_first.shape[1]
    half, quarter = hid // 2, hid // 4
    piece = zdim // chips
    jr, ir = hist // LANES, gen // LANES
    shapes = dict(
        noise=((gen, zdim), BF16), w_first=((zdim, hid), BF16), w_second=((hid, width), BF16), history=((hist, width), BF16),
        hidden=((gen, hid), BF16), hidden_t=((hid, gen), BF16), noise_t=((zdim, gen), BF16),
        surface=((gen, width), BF16), mult=((gen, hid), F32), surf_w=((gen, hid), F32),
        hist_w_hi=((hist, hid), BF16), hist_w_lo=((hist, hid), BF16),
        plan=((gen, hist), F32), weights=((gen, hist), BF16),
        surf_sq=((gen, LANES), F32), hist_sq=((jr, LANES), F32),
        row_a=((gen, LANES), F32), row_b=((gen, LANES), F32), col_b=((jr, LANES), F32),
        m_lse=((jr, LANES), F32), m_lse_in=((n_row - 1, jr, LANES), F32),
        row_top=((ir, LANES), F32), row_lse=((ir, LANES), F32), row_lse_in=((nz - 1, ir, LANES), F32),
        plan_hi=((gen, hist), BF16), plan_lo=((gen, hist), BF16), value=((gen, hid), F32),
        d_hi=((gen, hid), BF16), d_lo=((gen, hid), BF16),
        m_row=((SWEEPS, jr, LANES), F32), m_row_in=((SWEEPS - 1, n_row - 1, jr, LANES), F32),
        m_col=((SWEEPS - 1, ir, LANES), F32), m_col_in=((SWEEPS - 1, nz - 1, ir, LANES), F32),
        acc=((hid, hist), F32), acc_in=((half, hist), F32),
        x_in=((ny, nx - 1, 8, hist), F32), y_in=((nx, ny - 1, 8, hist), F32),
        x_in2=((nx - 1, 8, hist), F32), y_in2=((ny - 1, 8, hist), F32), reduced=((16, hist), F32),
        first=((zdim, hid), F32), first_in=((zdim, half), F32), first_half=((zdim, half), F32),
        first_chip_in=((chips - 1, piece, half), F32), first_piece=((1, piece, half), F32),
        first_z_in=((nz - 1, piece, half), F32), first_all=((n_row, piece, half), F32),
        term_a=((hid, LANES), F32), term_b=((hid, LANES), F32),
        term=((n_row, 8, LANES), F32), term_in=((n_row - 1, 8, LANES), F32),
        slices=((nz, 8, LANES), F32), slices_in=((nz - 1, 8, LANES), F32),
        second_all=((n_row, 8, LANES), F32),
    )
    scratch = [pltpu.VMEM(*shape) for shape in shapes.values()] + [pltpu.SemaphoreType.DMA((80,))]
    vmem = pl.BlockSpec(memory_space=pltpu.VMEM)
    first, second = pl.pallas_call(
        functools.partial(kernel, geometry, tuple(shapes)),
        out_shape=(
            jax.ShapeDtypeStruct((n_row, piece, half), F32),
            jax.ShapeDtypeStruct((n_row, 8, LANES), F32),
        ),
        in_specs=[pl.BlockSpec(memory_space=pl.ANY)] * 4,
        out_specs=(vmem, vmem),
        scratch_shapes=scratch,
        compiler_params=pltpu.CompilerParams(
            collective_id=0, has_side_effects=True, vmem_limit_bytes=56 * 1024 * 1024
        ),
        name="transport",
    )(noise, w_first, w_second, history)
    grad_first, turned = pl.pallas_call(
        functools.partial(place, geometry),
        out_shape=(
            jax.ShapeDtypeStruct((zdim, hid), F32),
            jax.ShapeDtypeStruct((width // nz, hid), F32),
        ),
        in_specs=[vmem] * 2,
        out_specs=(vmem, vmem),
        scratch_shapes=[pltpu.VMEM((hid, LANES), F32)],
        name="place",
    )(first, second)
    return grad_first, turned.T


def solution(mesh):
    chips = mesh.shape["row"] // 2
    nx = math.isqrt(chips)
    geometry = (chips // nx, nx, mesh.shape["col"])
    placed = (P("row", None), P(), P(), P("col", None))
    return jax.shard_map(
        functools.partial(shards, geometry), mesh=mesh, in_specs=placed,
        out_specs=(P(), P(None, "col")), check_vma=False,
    )
```

```python
import functools
import math
from types import SimpleNamespace

import jax
import jax.numpy as jnp
from jax import lax
from jax.experimental import pallas as pl
from jax.experimental.pallas import tpu as pltpu
from jax.sharding import PartitionSpec as P

SWEEPS = 3
EPSILON = 0.01
MESH = pl.DeviceIdType.MESH
F32 = jnp.float32
BF16 = jnp.bfloat16
LANES = 128


def kernel(geometry, names, noise_hbm, w_first_hbm, w_second_hbm, history_hbm, out_first, out_second, *scratch):
    ny, nx, nz = geometry
    chips = ny * nx
    n_row, n_col = 2 * chips, nz
    s = SimpleNamespace(**dict(zip(names, scratch)))
    sem = scratch[-1]
    noise, w_first, w_second, history = s.noise, s.w_first, s.w_second, s.history
    load_n = pltpu.make_async_copy(noise_hbm, noise, sem.at[76])
    load_f = pltpu.make_async_copy(w_first_hbm, w_first, sem.at[77])
    load_w = pltpu.make_async_copy(w_second_hbm, w_second, sem.at[78])
    load_h = pltpu.make_async_copy(history_hbm, history, sem.at[79])
    load_n.start()
    load_f.start()
    load_w.start()
    load_h.start()
    gen, zdim = noise.shape
    hist, width = history.shape
    hid = w_first.shape[1]
    half = hid // 2
    quarter = half // 2
    gen_total, hist_total = gen * n_row, hist * n_col
    scale = 1.0 / math.sqrt(gen_total)

    me = lax.axis_index("row")
    z = lax.axis_index("col")
    core = lax.rem(me, 2)
    other = 1 - core
    chip = me // 2
    x = lax.rem(chip, nx)
    y = chip // nx
    odd = lax.rem(z, 2) == 1
    sibling = (me + 1 - 2 * core, z)

    barrier = pltpu.get_barrier_semaphore()

    def far(a, n):
        return lax.rem(n // 2 + n * n - a * (a + 1) // 2, n)

    def over_chips(send):
        def step(j, c):
            to_y, to_x = lax.rem(y + far(j // nx, ny), ny), lax.rem(x + far(lax.rem(j, nx), nx), nx)
            send(to_y * nx + to_x, j)
            return c
        lax.fori_loop(0, chips - 1, step, 0)

    def over_row(send):
        def step(j, c):
            k = j // 2
            to_y, to_x = lax.rem(y + far(k // nx, ny), ny), lax.rem(x + far(lax.rem(k, nx), nx), nx)
            send((to_y * nx + to_x) * 2 + lax.rem(core + 1 + j, 2), j)
            return c
        lax.fori_loop(0, n_row - 1, step, 0)

    def over_col(send):
        def step(j, c):
            send(lax.rem(z + n_col // 2 + (j + 1) // 2 * (1 - 2 * lax.rem(j, 2)), n_col), j)
            return c
        lax.fori_loop(0, n_col - 1, step, 0)

    over_col(lambda to, j: pl.semaphore_signal(barrier, inc=1, device_id=(me, to), device_id_type=MESH))
    over_row(lambda to, j: pl.semaphore_signal(barrier, inc=1, device_id=(to, z), device_id_type=MESH))

    def start(src, dst, number, device):
        pltpu.make_async_remote_copy(
            src_ref=src, dst_ref=dst, send_sem=sem.at[2 * number], recv_sem=sem.at[2 * number + 1],
            device_id=device, device_id_type=MESH,
        ).start()

    def wait_bytes(like, index):
        pltpu.make_async_copy(like, like, sem.at[index]).wait()

    flying, landed = {}, {}

    def expect(number, like):
        flying[number] = like

    def arrived(number):
        landed[number] = flying.pop(number)
        wait_bytes(landed[number], 2 * number + 1)

    def finish():
        for number in tuple(flying):
            arrived(number)
        for number, like in landed.items():
            wait_bytes(like, 2 * number)

    def to_row(src, dst, number):
        over_row(lambda to, j: start(src, dst.at[j], number, (to, z)))
        expect(number, dst)

    def to_col(src, dst, number):
        over_col(lambda to, j: start(src, dst.at[j], number, (me, to)))
        expect(number, dst)

    def at(offset, size, unit):
        return pl.ds(offset if isinstance(offset, int) else pl.multiple_of(offset, unit), size)

    def each(count, body):
        lax.fori_loop(0, count, lambda k, c: (body(k), c)[1], 0)

    tiles = [slice(k * LANES, (k + 1) * LANES) for k in range(max(hist, width) // LANES)]
    plan_tiles = tiles[:hist // LANES]
    blocks = gen // LANES

    def block(k):
        return at(k * LANES, LANES, LANES)

    def fold(v):
        return jnp.sum(v.reshape(LANES // 8, 8, LANES), axis=0)

    def squares(ref, rows, across):
        total = jnp.zeros((LANES, LANES), F32)
        for cols in across:
            v = ref[rows, cols].astype(F32)
            total = total + v * v
        return total

    def rows_from_column(column, dst, total):
        for k in range(dst.shape[0]):
            turned = jnp.transpose(column[tiles[k], :])
            dst[k:k + 1, :] = jnp.sum(turned, axis=0, keepdims=True) if total else turned[0:1, :]

    def column_from_rows(rows, column):
        for k in range(rows.shape[0]):
            column[tiles[k], :] = jnp.transpose(jnp.broadcast_to(rows[k:k + 1, :], (LANES, LANES)))

    def dot(a, b):
        return jnp.dot(a, b, preferred_element_type=F32)

    def dot_t(a, b):
        return lax.dot_general(a, b, (((1,), (1,)), ((), ())), preferred_element_type=F32)

    tile_h = min(256, hid)
    tile_g = min(256, width)
    tile_j = min(256, hist)

    load_n.wait()
    load_f.wait()

    for n in range(hid // tile_h):
        cols = slice(n * tile_h, (n + 1) * tile_h)
        preact = dot(noise[...], w_first[:, cols])
        s.mult[:, cols] = preact
        s.hidden[:, cols] = (preact / (1.0 + jnp.exp(-preact))).astype(BF16)

    load_w.wait()

    for n in range(width // tile_g):
        cols = slice(n * tile_g, (n + 1) * tile_g)
        s.surface[:, cols] = dot(s.hidden[...], w_second[:, cols]).astype(BF16)
        for k in range(blocks):
            total = squares(s.surface, tiles[k], tiles[n * tile_g // LANES:(n + 1) * tile_g // LANES])
            s.surf_sq[tiles[k], :] = total if n == 0 else s.surf_sq[tiles[k], :] + total
    s.surf_sq[...] = jnp.broadcast_to(jnp.sum(s.surf_sq[...], axis=1, keepdims=True), (gen, LANES))

    load_h.wait()
    for n in range(hist // tile_j):
        wide = slice(n * tile_j, (n + 1) * tile_j)
        s.plan[:, wide] = dot_t(s.surface[...], history[wide, :])
        for c in range(n * tile_j // LANES, (n + 1) * tile_j // LANES):
            top = None
            for k in range(blocks):
                cost = (s.surf_sq[tiles[k], :] - 2.0 * s.plan[tiles[k], tiles[c]]) * (1.0 / width)
                scores = cost * (-1.0 / EPSILON)
                s.plan[tiles[k], tiles[c]] = scores
                tall = jnp.max(scores.reshape(LANES // 8, 8, LANES), axis=0)
                top = tall if top is None else jnp.maximum(top, tall)
            top = jnp.max(top, axis=0, keepdims=True)
            total = jnp.zeros((8, LANES), F32)
            for k in range(blocks):
                total = total + fold(jnp.exp(s.plan[tiles[k], tiles[c]] - top))
            s.m_lse[c:c + 1, :] = top + jnp.log(jnp.sum(total, axis=0, keepdims=True))

    pl.semaphore_wait(barrier, n_row - 1 + n_col - 1)
    to_row(s.m_lse, s.m_lse_in, 0)

    def hist_w_tile(n):
        rows = at(n * 256, min(256, hist), min(256, hist))
        prod = dot_t(history[rows, :], w_second[...])
        hi = prod.astype(BF16)
        s.hist_w_hi[rows, :] = hi
        s.hist_w_lo[rows, :] = (prod - hi.astype(F32)).astype(BF16)
    each(hist // min(256, hist), hist_w_tile)

    def hist_squares(k):
        s.hist_sq[pl.ds(k, 1), :] = jnp.sum(
            jnp.transpose(squares(history, block(k), tiles[:width // LANES])), axis=0, keepdims=True)
    each(hist // LANES, hist_squares)
    hist_cost = s.hist_sq[...] * (1.0 / width) * (1.0 / EPSILON)

    arrived(0)
    top = jnp.maximum(jnp.max(s.m_lse_in[...], axis=0), s.m_lse[...])
    total = jnp.sum(jnp.exp(s.m_lse_in[...] - top[None]), axis=0) + jnp.exp(s.m_lse[...] - top)
    g_first = math.log(gen_total) - (top + jnp.log(total) - hist_cost)
    s.m_row[0] = g_first - hist_cost

    def row_tops(k):
        rows = block(k)
        top = s.plan[rows, plan_tiles[0]] + s.m_row[0, 0:1, :]
        for n, cols in enumerate(plan_tiles[1:], 1):
            top = jnp.maximum(top, s.plan[rows, cols] + s.m_row[0, n:n + 1, :])
        s.row_a[rows, :] = top
    for k in range(blocks):
        row_tops(k)
    s.row_a[...] = jnp.broadcast_to(jnp.max(s.row_a[...], axis=1, keepdims=True), (gen, LANES))

    def first_rows(k):
        rows = block(k)
        top, total = s.row_a[rows, :], jnp.zeros((LANES, LANES), F32)
        for n, cols in enumerate(plan_tiles):
            grown = jnp.exp(s.plan[rows, cols] + s.m_row[0, n:n + 1, :] - top)
            s.plan[rows, cols] = grown
            total = total + grown
        s.row_b[rows, :] = total
    for k in range(blocks):
        first_rows(k)
    rows_from_column(s.row_a, s.row_top, False)
    rows_from_column(s.row_b, s.row_lse, True)
    s.row_lse[...] = s.row_top[...] + jnp.log(s.row_lse[...])
    to_col(s.row_lse, s.row_lse_in, 1)

    def surf_w_tile(n):
        cols = at(n * tile_h, tile_h, tile_h)
        s.surf_w[:, cols] = dot_t(s.surface[...], w_second[cols, :])
    each(hid // tile_h, surf_w_tile)
    s.hidden_t[...] = jnp.transpose(s.hidden[...].astype(F32)).astype(BF16)

    pair = at(lax.div(z, 2) * LANES, LANES, LANES)
    prod = dot(s.hidden_t[...], s.surface[:, pair])
    turned = pltpu.roll(prod, 64, axis=1)
    s.term_a[...] = jnp.where(odd, turned, prod)
    s.term_b[...] = jnp.where(odd, prod, turned)
    low = lax.broadcasted_iota(jnp.int32, (8, LANES), 1) < 64

    def owner_term(o):
        oc, ox, oy = lax.rem(o, 2), lax.rem(o // 2, nx), o // (2 * nx)
        upper = oc * half + oy * (quarter // ny) + ox * 8
        lower = oc * half + quarter + ox * (quarter // nx) + oy * 8
        s.term[o] = jnp.where(low, s.term_a[at(upper, 8, 8), :], s.term_b[at(lower, 8, 8), :])
    each(n_row, owner_term)

    over_row(lambda to, j: start(s.term.at[to], s.term_in.at[j], 6, (to, z)))
    expect(6, s.term_in)

    arrived(1)
    top = jnp.maximum(jnp.max(s.row_lse_in[...], axis=0), s.row_lse[...])
    total = jnp.sum(jnp.exp(s.row_lse_in[...] - top[None]), axis=0) + jnp.exp(s.row_lse[...] - top)
    column_from_rows(jnp.exp(s.row_top[...] - top) / total, s.row_a)

    def column_sums(scaled, dst):
        def step(k, sums):
            rows, out = block(k), []
            own = s.row_a[rows, :]
            for cols, total in zip(plan_tiles, sums):
                v = s.plan[rows, cols] * own
                if scaled:
                    s.plan[rows, cols] = v
                out.append(total + fold(v))
            return tuple(out)
        sums = [jnp.zeros((8, LANES), F32) for _ in plan_tiles]
        for k in range(blocks):
            sums = step(k, sums)
        for k, total in enumerate(sums):
            dst[k:k + 1, :] = jnp.sum(total, axis=0, keepdims=True)

    def row_sums(k):
        rows = block(k)
        total = jnp.zeros((LANES, LANES), F32)
        for n, cols in enumerate(plan_tiles):
            total = total + s.plan[rows, cols] * s.col_b[n:n + 1, :]
        s.row_b[rows, :] = total

    def unscaled_rows(k):
        rows = block(k)
        for n, cols in enumerate(plan_tiles):
            v = s.plan[rows, cols] * s.col_b[n:n + 1, :]
            s.plan[rows, cols] = v
            hi = v.astype(BF16)
            s.plan_hi[rows, cols] = hi
            s.plan_lo[rows, cols] = (v - hi.astype(F32)).astype(BF16)

    def value_tile(n):
        cols = at(n * tile_h, tile_h, tile_h)
        s.value[:, cols] = (dot(s.plan_hi[...], s.hist_w_hi[:, cols]) + dot(s.plan_hi[...], s.hist_w_lo[:, cols])
                            + dot(s.plan_lo[...], s.hist_w_hi[:, cols]))

    for sweep in range(1, SWEEPS):
        number = 2 * sweep
        mine, theirs = s.m_row.at[sweep], s.m_row_in.at[sweep - 1]
        column_sums(sweep == 1, mine)
        to_row(mine, theirs, number)
        if sweep == 1:
            preact = s.mult[...]
            sigma = 1.0 / (1.0 + jnp.exp(-preact))
            s.mult[...] = sigma * (1.0 + preact * (1.0 - sigma))
            s.noise_t[...] = jnp.transpose(noise[...].astype(F32)).astype(BF16)
        arrived(number)
        total = mine[...] + jnp.sum(theirs[...], axis=0)
        s.col_b[...] = (gen_total / hist_total) / total

        for k in range(blocks):
            row_sums(k)
        mine, theirs = s.m_col.at[sweep - 1], s.m_col_in.at[sweep - 1]
        rows_from_column(s.row_b, mine, True)
        to_col(mine, theirs, number + 1)
        if sweep == SWEEPS - 1:
            for k in range(blocks):
                unscaled_rows(k)
            each(hid // tile_h, value_tile)
        arrived(number + 1)
        total = mine[...] + jnp.sum(theirs[...], axis=0)
        column_from_rows(1.0 / total, s.row_a)

    for k in range(blocks):
        for cols in tiles[:hid // LANES]:
            rows = tiles[k]
            d_hidden = (s.surf_w[rows, cols] * (1.0 / n_col) - s.value[rows, cols] * s.row_a[rows, :]) * scale
            d_preact = d_hidden * s.mult[rows, cols]
            hi = d_preact.astype(BF16)
            s.d_hi[rows, cols] = hi
            s.d_lo[rows, cols] = (d_preact - hi.astype(F32)).astype(BF16)
    s.first[...] = dot(s.noise_t[...], s.d_hi[...]) + dot(s.noise_t[...], s.d_lo[...])
    start(s.first.at[:, at(other * half, half, half)], s.first_in, 8, sibling)
    expect(8, s.first_in)
    piece = zdim // chips

    def send_pieces():
        arrived(8)
        s.first_half[...] = s.first[:, at(core * half, half, half)] + s.first_in[...]
        over_chips(lambda to, j: start(
            s.first_half.at[at(to * piece, piece, 8), :], s.first_chip_in.at[j], 11, (to * 2 + core, z)))
        expect(11, s.first_chip_in)

    def weight_rows(k):
        rows = block(k)
        own = s.row_a[rows, :]
        for cols in plan_tiles:
            s.weights[rows, cols] = (s.plan[rows, cols] * own).astype(BF16)
    for k in range(blocks):
        weight_rows(k)

    def acc_tile(which):
        rows = at(which * half, half, half)

        def body(n):
            cols = at(n * tile_j, tile_j, tile_j)
            s.acc[rows, cols] = dot(s.hidden_t[rows, :], s.weights[:, cols])
        each(hist // tile_j, body)

    span_x, span_y = quarter // nx, quarter // ny
    base_u, base_l = core * half, core * half + quarter
    acc_tile(other)
    order = [pair for k in range(1, nx) for pair in ((True, k), (False, k))] + [(True, 0), (False, 0)]

    def block_rows(upper, k):
        return lax.rem(y + k, ny) * span_y if upper else quarter + lax.rem(x + k, nx) * span_x

    for n, (upper, k) in enumerate(order):
        rows = block_rows(upper, k)
        start(s.acc.at[at(other * half + rows, span_x, 8), :], s.acc_in.at[at(rows, span_x, 8), :], 20 + n, sibling)
        expect(20 + n, s.acc_in.at[at(n * span_x, span_x, 8), :])

    def chip_at(upper, k, first):
        if upper == first:
            return (y * nx + lax.rem(x + k, nx)) * 2 + core, lax.rem(x + k, nx) * 8
        return (lax.rem(y + k, ny) * nx + x) * 2 + core, lax.rem(y + k, ny) * 8

    def pass_on(n):
        upper, k = order[n]
        rows = block_rows(upper, k)
        arrived(20 + n)
        mine = at(core * half + rows, span_x, 8)
        s.acc[mine, :] = s.acc[mine, :] + s.acc_in[at(rows, span_x, 8), :]
        into = s.x_in if upper else s.y_in
        for j in range(1, nx):
            device, offset = chip_at(upper, j, True)
            start(s.acc.at[at(core * half + rows + offset, 8, 8), :], into.at[k, j - 1], 30 + n, (device, z))
        expect(30 + n, into.at[k])

    def pass_second(n):
        upper, k = order[n]
        arrived(30 + n)
        rows = at(core * half + block_rows(upper, k) + chip_at(upper, 0, True)[1], 8, 8)
        total = s.acc[rows, :] + jnp.sum((s.x_in if upper else s.y_in)[k], axis=0)
        if k == 0:
            return total
        s.acc[rows, :] = total
        into = s.y_in2 if upper else s.x_in2
        start(s.acc.at[rows, :], into.at[k - 1], 13 if upper else 14, (chip_at(upper, k, False)[0], z))

    send_pieces()
    acc_tile(core)

    for n in range(len(order)):
        pass_on(n)

    pass_second(0)
    pass_second(1)
    arrived(11)
    s.first_piece[0] = s.first_half[at(chip * piece, piece, 8), :] + jnp.sum(s.first_chip_in[...], axis=0)
    to_col(s.first_piece.at[0], s.first_z_in, 12)
    for n in range(2, len(order) - 2):
        pass_second(n)
    expect(13, s.y_in2)
    expect(14, s.x_in2)
    own_u, own_l = pass_second(len(order) - 2), pass_second(len(order) - 1)
    arrived(13)
    arrived(14)
    s.reduced[0:8, :] = own_u + jnp.sum(s.y_in2[...], axis=0)
    s.reduced[8:16, :] = own_l + jnp.sum(s.x_in2[...], axis=0)

    hi = s.reduced[...].astype(BF16)
    lo = (s.reduced[...] - hi.astype(F32)).astype(BF16)
    both = jnp.concatenate([hi, lo], axis=0)

    low = lax.broadcasted_iota(jnp.int32, (8, LANES), 1) < 64
    for n in range(width // tile_g):
        prod = dot(both, history[:, n * tile_g:(n + 1) * tile_g])
        prod = prod[0:16] + prod[16:32]
        for c in range(tile_g // LANES):
            upper, lower = prod[0:8, tiles[c]], prod[8:16, tiles[c]]
            k = 2 * (n * tile_g // LANES + c)
            s.slices[k] = jnp.where(low, upper, pltpu.roll(lower, 64, axis=1))
            s.slices[k + 1] = jnp.where(low, pltpu.roll(upper, 64, axis=1), lower)

    over_col(lambda to, j: start(s.slices.at[to], s.slices_in.at[j], 15, (me, to)))
    expect(15, s.slices_in)

    arrived(12)
    s.first_all[me] = s.first_piece[0] + jnp.sum(s.first_z_in[...], axis=0)
    over_row(lambda to, j: start(s.first_all.at[me], s.first_all.at[me], 16, (to, z)))
    expect(16, s.first_all.at[pl.ds(0, n_row - 1)])

    arrived(6)
    term = s.term[me] + jnp.sum(s.term_in[...], axis=0)
    arrived(15)
    mixed = s.slices[z] + jnp.sum(s.slices_in[...], axis=0)
    s.second_all[me] = (term - mixed) * scale

    over_row(lambda to, j: start(s.second_all.at[me], s.second_all.at[me], 17, (to, z)))
    expect(17, s.second_all.at[pl.ds(0, n_row - 1)])

    arrived(16)
    for k in range(chips):
        for c in range(2):
            out_first[k * piece:(k + 1) * piece, c * half:(c + 1) * half] = s.first_all[2 * k + c]
    arrived(17)
    out_second[...] = s.second_all[...]
    finish()


def place(geometry, first, second, out_first, out_second, wide, done):
    hand_on = pltpu.make_async_copy(first, out_first, done)
    hand_on.start()
    ny, nx, nz = geometry
    half = wide.shape[0] // 2
    quarter = half // 2
    for y in range(ny):
        for x in range(nx):
            chip = y * nx + x
            for c in range(2):
                upper = c * half + y * (quarter // ny) + x * 8
                lower = c * half + quarter + x * (quarter // nx) + y * 8
                v = second[2 * chip + c]
                wide[upper:upper + 8, :] = v
                wide[lower:lower + 8, :] = pltpu.roll(v, 64, axis=1)
    for k in range(wide.shape[0] // LANES):
        out_second[:, k * LANES:(k + 1) * LANES] = jnp.transpose(wide[k * LANES:(k + 1) * LANES, :])[0:64, :]
    hand_on.wait()


def shards(geometry, noise, w_first, w_second, history):
    ny, nx, nz = geometry
    chips = ny * nx
    n_row = 2 * chips
    gen, zdim = noise.shape
    hist, width = history.shape
    hid = w_first.shape[1]
    half, quarter = hid // 2, hid // 4
    piece = zdim // chips
    jr, ir = hist // LANES, gen // LANES
    shapes = dict(
        noise=((gen, zdim), BF16), w_first=((zdim, hid), BF16), w_second=((hid, width), BF16), history=((hist, width), BF16),
        hidden=((gen, hid), BF16), hidden_t=((hid, gen), BF16), noise_t=((zdim, gen), BF16),
        surface=((gen, width), BF16), mult=((gen, hid), F32), surf_w=((gen, hid), F32),
        hist_w_hi=((hist, hid), BF16), hist_w_lo=((hist, hid), BF16),
        plan=((gen, hist), F32), weights=((gen, hist), BF16),
        surf_sq=((gen, LANES), F32), hist_sq=((jr, LANES), F32),
        row_a=((gen, LANES), F32), row_b=((gen, LANES), F32), col_b=((jr, LANES), F32),
        m_lse=((jr, LANES), F32), m_lse_in=((n_row - 1, jr, LANES), F32),
        row_top=((ir, LANES), F32), row_lse=((ir, LANES), F32), row_lse_in=((nz - 1, ir, LANES), F32),
        plan_hi=((gen, hist), BF16), plan_lo=((gen, hist), BF16), value=((gen, hid), F32),
        d_hi=((gen, hid), BF16), d_lo=((gen, hid), BF16),
        m_row=((SWEEPS, jr, LANES), F32), m_row_in=((SWEEPS - 1, n_row - 1, jr, LANES), F32),
        m_col=((SWEEPS - 1, ir, LANES), F32), m_col_in=((SWEEPS - 1, nz - 1, ir, LANES), F32),
        acc=((hid, hist), F32), acc_in=((half, hist), F32),
        x_in=((ny, nx - 1, 8, hist), F32), y_in=((nx, ny - 1, 8, hist), F32),
        x_in2=((nx - 1, 8, hist), F32), y_in2=((ny - 1, 8, hist), F32), reduced=((16, hist), F32),
        first=((zdim, hid), F32), first_in=((zdim, half), F32), first_half=((zdim, half), F32),
        first_chip_in=((chips - 1, piece, half), F32), first_piece=((1, piece, half), F32),
        first_z_in=((nz - 1, piece, half), F32), first_all=((n_row, piece, half), F32),
        term_a=((hid, LANES), F32), term_b=((hid, LANES), F32),
        term=((n_row, 8, LANES), F32), term_in=((n_row - 1, 8, LANES), F32),
        slices=((nz, 8, LANES), F32), slices_in=((nz - 1, 8, LANES), F32),
        second_all=((n_row, 8, LANES), F32),
    )
    scratch = [pltpu.VMEM(*shape) for shape in shapes.values()] + [pltpu.SemaphoreType.DMA((80,))]
    vmem = pl.BlockSpec(memory_space=pltpu.VMEM)
    first, second = pl.pallas_call(
        functools.partial(kernel, geometry, tuple(shapes)),
        out_shape=(
            jax.ShapeDtypeStruct((zdim, hid), F32),
            jax.ShapeDtypeStruct((n_row, 8, LANES), F32),
        ),
        in_specs=[pl.BlockSpec(memory_space=pl.ANY)] * 4,
        out_specs=(vmem, vmem),
        scratch_shapes=scratch,
        compiler_params=pltpu.CompilerParams(
            collective_id=0, has_side_effects=True, vmem_limit_bytes=56 * 1024 * 1024
        ),
        name="transport",
    )(noise, w_first, w_second, history)
    grad_first, turned = pl.pallas_call(
        functools.partial(place, geometry),
        out_shape=(
            jax.ShapeDtypeStruct((zdim, hid), F32),
            jax.ShapeDtypeStruct((width // nz, hid), F32),
        ),
        in_specs=[pl.BlockSpec(memory_space=pl.ANY), vmem],
        out_specs=(pl.BlockSpec(memory_space=pl.ANY), vmem),
        scratch_shapes=[pltpu.VMEM((hid, LANES), F32), pltpu.SemaphoreType.DMA],
        name="place",
    )(first, second)
    return grad_first, turned.T


def solution(mesh):
    chips = mesh.shape["row"] // 2
    nx = math.isqrt(chips)
    geometry = (chips // nx, nx, mesh.shape["col"])
    placed = (P("row", None), P(), P(), P("col", None))
    return jax.shard_map(
        functools.partial(shards, geometry), mesh=mesh, in_specs=placed,
        out_specs=(P(), P(None, "col")), check_vma=False,
    )
```

```python
import functools
import math
from types import SimpleNamespace

import jax
import jax.numpy as jnp
from jax import lax
from jax.experimental import pallas as pl
from jax.experimental.pallas import tpu as pltpu
from jax.sharding import PartitionSpec as P

SWEEPS = 3
EPSILON = 0.01
MESH = pl.DeviceIdType.MESH
F32 = jnp.float32
BF16 = jnp.bfloat16
LANES = 128


def kernel(geometry, names, noise_hbm, w_first_hbm, w_second_hbm, history_hbm, out_first, out_second, *scratch):
    ny, nx, nz = geometry
    chips = ny * nx
    n_row, n_col = 2 * chips, nz
    s = SimpleNamespace(**dict(zip(names, scratch)))
    sem = scratch[-1]
    noise, w_first, w_second, history = s.noise, s.w_first, s.w_second, s.history
    load_n = pltpu.make_async_copy(noise_hbm, noise, sem.at[76])
    load_f = pltpu.make_async_copy(w_first_hbm, w_first, sem.at[77])
    load_w = pltpu.make_async_copy(w_second_hbm, w_second, sem.at[78])
    load_h = pltpu.make_async_copy(history_hbm, history, sem.at[79])
    load_n.start()
    load_f.start()
    load_w.start()
    load_h.start()
    gen, zdim = noise.shape
    hist, width = history.shape
    hid = w_first.shape[1]
    half = hid // 2
    quarter = half // 2
    gen_total, hist_total = gen * n_row, hist * n_col
    scale = 1.0 / math.sqrt(gen_total)

    me = lax.axis_index("row")
    z = lax.axis_index("col")
    core = lax.rem(me, 2)
    other = 1 - core
    chip = me // 2
    x = lax.rem(chip, nx)
    y = chip // nx
    odd = lax.rem(z, 2) == 1
    sibling = (me + 1 - 2 * core, z)

    barrier = pltpu.get_barrier_semaphore()

    def far(a, n):
        return lax.rem(n // 2 + n * n - a * (a + 1) // 2, n)

    def over_chips(send):
        def step(j, c):
            to_y, to_x = lax.rem(y + far(j // nx, ny), ny), lax.rem(x + far(lax.rem(j, nx), nx), nx)
            send(to_y * nx + to_x, j)
            return c
        lax.fori_loop(0, chips - 1, step, 0)

    def over_row(send):
        def step(j, c):
            k = j // 2
            to_y, to_x = lax.rem(y + far(k // nx, ny), ny), lax.rem(x + far(lax.rem(k, nx), nx), nx)
            send((to_y * nx + to_x) * 2 + lax.rem(core + 1 + j, 2), j)
            return c
        lax.fori_loop(0, n_row - 1, step, 0)

    def over_col(send):
        def step(j, c):
            send(lax.rem(z + n_col // 2 + (j + 1) // 2 * (1 - 2 * lax.rem(j, 2)), n_col), j)
            return c
        lax.fori_loop(0, n_col - 1, step, 0)

    over_col(lambda to, j: pl.semaphore_signal(barrier, inc=1, device_id=(me, to), device_id_type=MESH))
    over_row(lambda to, j: pl.semaphore_signal(barrier, inc=1, device_id=(to, z), device_id_type=MESH))

    def start(src, dst, number, device):
        pltpu.make_async_remote_copy(
            src_ref=src, dst_ref=dst, send_sem=sem.at[2 * number], recv_sem=sem.at[2 * number + 1],
            device_id=device, device_id_type=MESH,
        ).start()

    def wait_bytes(like, index):
        pltpu.make_async_copy(like, like, sem.at[index]).wait()

    flying, landed = {}, {}

    def expect(number, like):
        flying[number] = like

    def arrived(number):
        landed[number] = flying.pop(number)
        wait_bytes(landed[number], 2 * number + 1)

    def finish():
        for number in tuple(flying):
            arrived(number)
        for number, like in landed.items():
            wait_bytes(like, 2 * number)

    def to_row(src, dst, number):
        over_row(lambda to, j: start(src, dst.at[j], number, (to, z)))
        expect(number, dst)

    def to_col(src, dst, number):
        over_col(lambda to, j: start(src, dst.at[j], number, (me, to)))
        expect(number, dst)

    def at(offset, size, unit):
        return pl.ds(offset if isinstance(offset, int) else pl.multiple_of(offset, unit), size)

    def each(count, body):
        lax.fori_loop(0, count, lambda k, c: (body(k), c)[1], 0)

    tiles = [slice(k * LANES, (k + 1) * LANES) for k in range(max(hist, width) // LANES)]
    plan_tiles = tiles[:hist // LANES]
    blocks = gen // LANES

    def block(k):
        return at(k * LANES, LANES, LANES)

    def fold(v):
        return jnp.sum(v.reshape(LANES // 8, 8, LANES), axis=0)

    def squares(ref, rows, across):
        total = jnp.zeros((LANES, LANES), F32)
        for cols in across:
            v = ref[rows, cols].astype(F32)
            total = total + v * v
        return total

    def rows_from_column(column, dst, total):
        for k in range(dst.shape[0]):
            turned = jnp.transpose(column[tiles[k], :])
            dst[k:k + 1, :] = jnp.sum(turned, axis=0, keepdims=True) if total else turned[0:1, :]

    def column_from_rows(rows, column):
        for k in range(rows.shape[0]):
            column[tiles[k], :] = jnp.transpose(jnp.broadcast_to(rows[k:k + 1, :], (LANES, LANES)))

    def dot(a, b):
        return jnp.dot(a, b, preferred_element_type=F32)

    def dot_t(a, b):
        return lax.dot_general(a, b, (((1,), (1,)), ((), ())), preferred_element_type=F32)

    tile_h = min(256, hid)
    tile_g = min(256, width)
    tile_j = min(256, hist)

    load_n.wait()
    load_f.wait()

    for n in range(hid // tile_h):
        cols = slice(n * tile_h, (n + 1) * tile_h)
        preact = dot(noise[...], w_first[:, cols])
        s.mult[:, cols] = preact
        s.hidden[:, cols] = (preact / (1.0 + jnp.exp(-preact))).astype(BF16)

    load_w.wait()

    for n in range(width // tile_g):
        cols = slice(n * tile_g, (n + 1) * tile_g)
        s.surface[:, cols] = dot(s.hidden[...], w_second[:, cols]).astype(BF16)
        for k in range(blocks):
            total = squares(s.surface, tiles[k], tiles[n * tile_g // LANES:(n + 1) * tile_g // LANES])
            s.surf_sq[tiles[k], :] = total if n == 0 else s.surf_sq[tiles[k], :] + total
    s.surf_sq[...] = jnp.broadcast_to(jnp.sum(s.surf_sq[...], axis=1, keepdims=True), (gen, LANES))

    load_h.wait()
    for n in range(hist // tile_j):
        wide = slice(n * tile_j, (n + 1) * tile_j)
        s.plan[:, wide] = dot_t(s.surface[...], history[wide, :])
        for c in range(n * tile_j // LANES, (n + 1) * tile_j // LANES):
            top = None
            for k in range(blocks):
                cost = (s.surf_sq[tiles[k], :] - 2.0 * s.plan[tiles[k], tiles[c]]) * (1.0 / width)
                scores = cost * (-1.0 / EPSILON)
                s.plan[tiles[k], tiles[c]] = scores
                tall = jnp.max(scores.reshape(LANES // 8, 8, LANES), axis=0)
                top = tall if top is None else jnp.maximum(top, tall)
            top = jnp.max(top, axis=0, keepdims=True)
            total = jnp.zeros((8, LANES), F32)
            for k in range(blocks):
                total = total + fold(jnp.exp(s.plan[tiles[k], tiles[c]] - top))
            s.m_lse[c:c + 1, :] = top + jnp.log(jnp.sum(total, axis=0, keepdims=True))

    pl.semaphore_wait(barrier, n_row - 1 + n_col - 1)
    to_row(s.m_lse, s.m_lse_in, 0)

    def hist_w_tile(n):
        rows = at(n * 256, min(256, hist), min(256, hist))
        prod = dot_t(history[rows, :], w_second[...])
        hi = prod.astype(BF16)
        s.hist_w_hi[rows, :] = hi
        s.hist_w_lo[rows, :] = (prod - hi.astype(F32)).astype(BF16)
    each(hist // min(256, hist), hist_w_tile)

    def hist_squares(k):
        s.hist_sq[pl.ds(k, 1), :] = jnp.sum(
            jnp.transpose(squares(history, block(k), tiles[:width // LANES])), axis=0, keepdims=True)
    each(hist // LANES, hist_squares)
    hist_cost = s.hist_sq[...] * (1.0 / width) * (1.0 / EPSILON)

    arrived(0)
    top = jnp.maximum(jnp.max(s.m_lse_in[...], axis=0), s.m_lse[...])
    total = jnp.sum(jnp.exp(s.m_lse_in[...] - top[None]), axis=0) + jnp.exp(s.m_lse[...] - top)
    g_first = math.log(gen_total) - (top + jnp.log(total) - hist_cost)
    s.m_row[0] = g_first - hist_cost

    def row_tops(k):
        rows = block(k)
        top = s.plan[rows, plan_tiles[0]] + s.m_row[0, 0:1, :]
        for n, cols in enumerate(plan_tiles[1:], 1):
            top = jnp.maximum(top, s.plan[rows, cols] + s.m_row[0, n:n + 1, :])
        s.row_a[rows, :] = top
    for k in range(blocks):
        row_tops(k)
    s.row_a[...] = jnp.broadcast_to(jnp.max(s.row_a[...], axis=1, keepdims=True), (gen, LANES))

    def first_rows(k):
        rows = block(k)
        top, total = s.row_a[rows, :], jnp.zeros((LANES, LANES), F32)
        for n, cols in enumerate(plan_tiles):
            grown = jnp.exp(s.plan[rows, cols] + s.m_row[0, n:n + 1, :] - top)
            s.plan[rows, cols] = grown
            total = total + grown
        s.row_b[rows, :] = total
    for k in range(blocks):
        first_rows(k)
    rows_from_column(s.row_a, s.row_top, False)
    rows_from_column(s.row_b, s.row_lse, True)
    s.row_lse[...] = s.row_top[...] + jnp.log(s.row_lse[...])
    to_col(s.row_lse, s.row_lse_in, 1)

    def surf_w_tile(n):
        cols = at(n * tile_h, tile_h, tile_h)
        s.surf_w[:, cols] = dot_t(s.surface[...], w_second[cols, :])
    each(hid // tile_h, surf_w_tile)
    s.hidden_t[...] = jnp.transpose(s.hidden[...].astype(F32)).astype(BF16)

    pair = at(lax.div(z, 2) * LANES, LANES, LANES)
    prod = dot(s.hidden_t[...], s.surface[:, pair])
    turned = pltpu.roll(prod, 64, axis=1)
    s.term_a[...] = jnp.where(odd, turned, prod)
    s.term_b[...] = jnp.where(odd, prod, turned)
    low = lax.broadcasted_iota(jnp.int32, (8, LANES), 1) < 64

    def owner_term(o):
        oc, ox, oy = lax.rem(o, 2), lax.rem(o // 2, nx), o // (2 * nx)
        upper = oc * half + oy * (quarter // ny) + ox * 8
        lower = oc * half + quarter + ox * (quarter // nx) + oy * 8
        s.term[o] = jnp.where(low, s.term_a[at(upper, 8, 8), :], s.term_b[at(lower, 8, 8), :])
    each(n_row, owner_term)

    over_row(lambda to, j: start(s.term.at[to], s.term_in.at[j], 6, (to, z)))
    expect(6, s.term_in)

    arrived(1)
    top = jnp.maximum(jnp.max(s.row_lse_in[...], axis=0), s.row_lse[...])
    total = jnp.sum(jnp.exp(s.row_lse_in[...] - top[None]), axis=0) + jnp.exp(s.row_lse[...] - top)
    column_from_rows(jnp.exp(s.row_top[...] - top) / total, s.row_a)

    def column_sums(scaled, dst):
        def step(k, sums):
            rows, out = block(k), []
            own = s.row_a[rows, :]
            for cols, total in zip(plan_tiles, sums):
                v = s.plan[rows, cols] * own
                if scaled:
                    s.plan[rows, cols] = v
                out.append(total + fold(v))
            return tuple(out)
        sums = [jnp.zeros((8, LANES), F32) for _ in plan_tiles]
        for k in range(blocks):
            sums = step(k, sums)
        for k, total in enumerate(sums):
            dst[k:k + 1, :] = jnp.sum(total, axis=0, keepdims=True)

    def row_sums(k):
        rows = block(k)
        total = jnp.zeros((LANES, LANES), F32)
        for n, cols in enumerate(plan_tiles):
            total = total + s.plan[rows, cols] * s.col_b[n:n + 1, :]
        s.row_b[rows, :] = total

    def unscaled_rows(k):
        rows = block(k)
        for n, cols in enumerate(plan_tiles):
            v = s.plan[rows, cols] * s.col_b[n:n + 1, :]
            s.plan[rows, cols] = v
            hi = v.astype(BF16)
            s.plan_hi[rows, cols] = hi
            s.plan_lo[rows, cols] = (v - hi.astype(F32)).astype(BF16)

    def value_tile(n):
        cols = at(n * tile_h, tile_h, tile_h)
        s.value[:, cols] = (dot(s.plan_hi[...], s.hist_w_hi[:, cols]) + dot(s.plan_hi[...], s.hist_w_lo[:, cols])
                            + dot(s.plan_lo[...], s.hist_w_hi[:, cols]))

    for sweep in range(1, SWEEPS):
        number = 2 * sweep
        mine, theirs = s.m_row.at[sweep], s.m_row_in.at[sweep - 1]
        column_sums(sweep == 1, mine)
        to_row(mine, theirs, number)
        if sweep == 1:
            preact = s.mult[...]
            sigma = 1.0 / (1.0 + jnp.exp(-preact))
            s.mult[...] = sigma * (1.0 + preact * (1.0 - sigma))
            s.noise_t[...] = jnp.transpose(noise[...].astype(F32)).astype(BF16)
        arrived(number)
        total = mine[...] + jnp.sum(theirs[...], axis=0)
        s.col_b[...] = (gen_total / hist_total) / total

        for k in range(blocks):
            row_sums(k)
        mine, theirs = s.m_col.at[sweep - 1], s.m_col_in.at[sweep - 1]
        rows_from_column(s.row_b, mine, True)
        to_col(mine, theirs, number + 1)
        if sweep == SWEEPS - 1:
            for k in range(blocks):
                unscaled_rows(k)
            each(hid // tile_h, value_tile)
        arrived(number + 1)
        total = mine[...] + jnp.sum(theirs[...], axis=0)
        column_from_rows(1.0 / total, s.row_a)

    for k in range(blocks):
        for cols in tiles[:hid // LANES]:
            rows = tiles[k]
            d_hidden = (s.surf_w[rows, cols] * (1.0 / n_col) - s.value[rows, cols] * s.row_a[rows, :]) * scale
            d_preact = d_hidden * s.mult[rows, cols]
            hi = d_preact.astype(BF16)
            s.d_hi[rows, cols] = hi
            s.d_lo[rows, cols] = (d_preact - hi.astype(F32)).astype(BF16)
    s.first[...] = dot(s.noise_t[...], s.d_hi[...]) + dot(s.noise_t[...], s.d_lo[...])
    start(s.first.at[:, at(other * half, half, half)], s.first_in, 8, sibling)
    expect(8, s.first_in)
    piece = zdim // chips

    def send_pieces():
        arrived(8)
        s.first_half[...] = s.first[:, at(core * half, half, half)] + s.first_in[...]
        over_chips(lambda to, j: start(
            s.first_half.at[at(to * piece, piece, 8), :], s.first_chip_in.at[j], 11, (to * 2 + core, z)))
        expect(11, s.first_chip_in)

    def weight_rows(k):
        rows = block(k)
        own = s.row_a[rows, :]
        for cols in plan_tiles:
            s.weights[rows, cols] = (s.plan[rows, cols] * own).astype(BF16)
    for k in range(blocks):
        weight_rows(k)

    def acc_tile(which):
        rows = at(which * half, half, half)

        def body(n):
            cols = at(n * tile_j, tile_j, tile_j)
            s.acc[rows, cols] = dot(s.hidden_t[rows, :], s.weights[:, cols])
        each(hist // tile_j, body)

    span_x, span_y = quarter // nx, quarter // ny
    base_u, base_l = core * half, core * half + quarter
    acc_tile(other)
    order = [pair for k in range(1, nx) for pair in ((True, k), (False, k))] + [(True, 0), (False, 0)]

    def block_rows(upper, k):
        return lax.rem(y + k, ny) * span_y if upper else quarter + lax.rem(x + k, nx) * span_x

    for n, (upper, k) in enumerate(order):
        rows = block_rows(upper, k)
        start(s.acc.at[at(other * half + rows, span_x, 8), :], s.acc_in.at[at(rows, span_x, 8), :], 20 + n, sibling)
        expect(20 + n, s.acc_in.at[at(n * span_x, span_x, 8), :])

    def chip_at(upper, k, first):
        if upper == first:
            return (y * nx + lax.rem(x + k, nx)) * 2 + core, lax.rem(x + k, nx) * 8
        return (lax.rem(y + k, ny) * nx + x) * 2 + core, lax.rem(y + k, ny) * 8

    def pass_on(n):
        upper, k = order[n]
        rows = block_rows(upper, k)
        arrived(20 + n)
        mine = at(core * half + rows, span_x, 8)
        s.acc[mine, :] = s.acc[mine, :] + s.acc_in[at(rows, span_x, 8), :]
        into = s.x_in if upper else s.y_in
        for j in range(1, nx):
            device, offset = chip_at(upper, j, True)
            start(s.acc.at[at(core * half + rows + offset, 8, 8), :], into.at[k, j - 1], 30 + n, (device, z))
        expect(30 + n, into.at[k])

    def pass_second(n):
        upper, k = order[n]
        arrived(30 + n)
        rows = at(core * half + block_rows(upper, k) + chip_at(upper, 0, True)[1], 8, 8)
        total = s.acc[rows, :] + jnp.sum((s.x_in if upper else s.y_in)[k], axis=0)
        if k == 0:
            return total
        s.acc[rows, :] = total
        into = s.y_in2 if upper else s.x_in2
        start(s.acc.at[rows, :], into.at[k - 1], 13 if upper else 14, (chip_at(upper, k, False)[0], z))

    send_pieces()
    acc_tile(core)

    for n in range(len(order)):
        pass_on(n)

    pass_second(0)
    pass_second(1)
    arrived(11)
    s.first_piece[0] = s.first_half[at(chip * piece, piece, 8), :] + jnp.sum(s.first_chip_in[...], axis=0)
    to_col(s.first_piece.at[0], s.first_z_in, 12)
    for n in range(2, len(order) - 2):
        pass_second(n)
    expect(13, s.y_in2)
    expect(14, s.x_in2)
    own_u, own_l = pass_second(len(order) - 2), pass_second(len(order) - 1)
    arrived(13)
    arrived(14)
    s.reduced[0:8, :] = own_u + jnp.sum(s.y_in2[...], axis=0)
    s.reduced[8:16, :] = own_l + jnp.sum(s.x_in2[...], axis=0)

    hi = s.reduced[...].astype(BF16)
    lo = (s.reduced[...] - hi.astype(F32)).astype(BF16)
    both = jnp.concatenate([hi, lo], axis=0)

    low = lax.broadcasted_iota(jnp.int32, (8, LANES), 1) < 64
    for n in range(width // tile_g):
        prod = dot(both, history[:, n * tile_g:(n + 1) * tile_g])
        prod = prod[0:16] + prod[16:32]
        for c in range(tile_g // LANES):
            upper, lower = prod[0:8, tiles[c]], prod[8:16, tiles[c]]
            k = 2 * (n * tile_g // LANES + c)
            s.slices[k] = jnp.where(low, upper, pltpu.roll(lower, 64, axis=1))
            s.slices[k + 1] = jnp.where(low, pltpu.roll(upper, 64, axis=1), lower)

    over_col(lambda to, j: start(s.slices.at[to], s.slices_in.at[j], 15, (me, to)))
    expect(15, s.slices_in)

    arrived(12)
    s.first_all[me] = s.first_piece[0] + jnp.sum(s.first_z_in[...], axis=0)
    over_row(lambda to, j: start(s.first_all.at[me], s.first_all.at[me], 16, (to, z)))
    expect(16, s.first_all.at[pl.ds(0, n_row - 1)])

    arrived(6)
    term = s.term[me] + jnp.sum(s.term_in[...], axis=0)
    arrived(15)
    mixed = s.slices[z] + jnp.sum(s.slices_in[...], axis=0)
    s.second_all[me] = (term - mixed) * scale

    over_row(lambda to, j: start(s.second_all.at[me], s.second_all.at[me], 17, (to, z)))
    expect(17, s.second_all.at[pl.ds(0, n_row - 1)])

    arrived(16)
    for k in range(chips):
        for c in range(2):
            out_first[k * piece:(k + 1) * piece, c * half:(c + 1) * half] = s.first_all[2 * k + c]
    arrived(17)
    out_second[...] = s.second_all[...]
    finish()


def place(geometry, first, second, out_first, out_second, wide):
    out_first[...] = first[...]
    ny, nx, nz = geometry
    half = wide.shape[0] // 2
    quarter = half // 2
    for y in range(ny):
        for x in range(nx):
            chip = y * nx + x
            for c in range(2):
                upper = c * half + y * (quarter // ny) + x * 8
                lower = c * half + quarter + x * (quarter // nx) + y * 8
                v = second[2 * chip + c]
                wide[upper:upper + 8, :] = v
                wide[lower:lower + 8, :] = pltpu.roll(v, 64, axis=1)
    for k in range(wide.shape[0] // LANES):
        out_second[:, k * LANES:(k + 1) * LANES] = jnp.transpose(wide[k * LANES:(k + 1) * LANES, :])[0:64, :]


def shards(geometry, noise, w_first, w_second, history):
    ny, nx, nz = geometry
    chips = ny * nx
    n_row = 2 * chips
    gen, zdim = noise.shape
    hist, width = history.shape
    hid = w_first.shape[1]
    half, quarter = hid // 2, hid // 4
    piece = zdim // chips
    jr, ir = hist // LANES, gen // LANES
    shapes = dict(
        noise=((gen, zdim), BF16), w_first=((zdim, hid), BF16), w_second=((hid, width), BF16), history=((hist, width), BF16),
        hidden=((gen, hid), BF16), hidden_t=((hid, gen), BF16), noise_t=((zdim, gen), BF16),
        surface=((gen, width), BF16), mult=((gen, hid), F32), surf_w=((gen, hid), F32),
        hist_w_hi=((hist, hid), BF16), hist_w_lo=((hist, hid), BF16),
        plan=((gen, hist), F32), weights=((gen, hist), BF16),
        surf_sq=((gen, LANES), F32), hist_sq=((jr, LANES), F32),
        row_a=((gen, LANES), F32), row_b=((gen, LANES), F32), col_b=((jr, LANES), F32),
        m_lse=((jr, LANES), F32), m_lse_in=((n_row - 1, jr, LANES), F32),
        row_top=((ir, LANES), F32), row_lse=((ir, LANES), F32), row_lse_in=((nz - 1, ir, LANES), F32),
        plan_hi=((gen, hist), BF16), plan_lo=((gen, hist), BF16), value=((gen, hid), F32),
        d_hi=((gen, hid), BF16), d_lo=((gen, hid), BF16),
        m_row=((SWEEPS, jr, LANES), F32), m_row_in=((SWEEPS - 1, n_row - 1, jr, LANES), F32),
        m_col=((SWEEPS - 1, ir, LANES), F32), m_col_in=((SWEEPS - 1, nz - 1, ir, LANES), F32),
        acc=((hid, hist), F32), acc_in=((half, hist), F32),
        x_in=((ny, nx - 1, 8, hist), F32), y_in=((nx, ny - 1, 8, hist), F32),
        x_in2=((nx - 1, 8, hist), F32), y_in2=((ny - 1, 8, hist), F32), reduced=((16, hist), F32),
        first=((zdim, hid), F32), first_in=((zdim, half), F32), first_half=((zdim, half), F32),
        first_chip_in=((chips - 1, piece, half), F32), first_piece=((1, piece, half), F32),
        first_z_in=((nz - 1, piece, half), F32), first_all=((n_row, piece, half), F32),
        term_a=((hid, LANES), F32), term_b=((hid, LANES), F32),
        term=((n_row, 8, LANES), F32), term_in=((n_row - 1, 8, LANES), F32),
        slices=((nz, 8, LANES), F32), slices_in=((nz - 1, 8, LANES), F32),
        second_all=((n_row, 8, LANES), F32),
    )
    scratch = [pltpu.VMEM(*shape) for shape in shapes.values()] + [pltpu.SemaphoreType.DMA((80,))]
    vmem = pl.BlockSpec(memory_space=pltpu.VMEM)
    first, second = pl.pallas_call(
        functools.partial(kernel, geometry, tuple(shapes)),
        out_shape=(
            jax.ShapeDtypeStruct((zdim, hid), F32),
            jax.ShapeDtypeStruct((n_row, 8, LANES), F32),
        ),
        in_specs=[pl.BlockSpec(memory_space=pl.ANY)] * 4,
        out_specs=(vmem, vmem),
        scratch_shapes=scratch,
        compiler_params=pltpu.CompilerParams(
            collective_id=0, has_side_effects=True, vmem_limit_bytes=56 * 1024 * 1024
        ),
        name="transport",
    )(noise, w_first, w_second, history)
    grad_first, turned = pl.pallas_call(
        functools.partial(place, geometry),
        out_shape=(
            jax.ShapeDtypeStruct((zdim, hid), F32),
            jax.ShapeDtypeStruct((width // nz, hid), F32),
        ),
        in_specs=[vmem] * 2,
        out_specs=(vmem, vmem),
        scratch_shapes=[pltpu.VMEM((hid, LANES), F32)],
        name="place",
    )(first, second)
    return grad_first, turned.T


def solution(mesh):
    chips = mesh.shape["row"] // 2
    nx = math.isqrt(chips)
    geometry = (chips // nx, nx, mesh.shape["col"])
    placed = (P("row", None), P(), P(), P("col", None))
    return jax.shard_map(
        functools.partial(shards, geometry), mesh=mesh, in_specs=placed,
        out_specs=(P(), P(None, "col")), check_vma=False,
    )
```

```python
import functools
import math
from types import SimpleNamespace

import jax
import jax.numpy as jnp
from jax import lax
from jax.experimental import pallas as pl
from jax.experimental.pallas import tpu as pltpu
from jax.sharding import PartitionSpec as P

SWEEPS = 3
EPSILON = 0.01
MESH = pl.DeviceIdType.MESH
F32 = jnp.float32
BF16 = jnp.bfloat16
LANES = 128


def kernel(geometry, names, noise_hbm, w_first_hbm, w_second_hbm, history_hbm, out_first, out_second, *scratch):
    ny, nx, nz = geometry
    chips = ny * nx
    n_row, n_col = 2 * chips, nz
    s = SimpleNamespace(**dict(zip(names, scratch)))
    sem = scratch[-1]
    noise, w_first, w_second, history = s.noise, s.w_first, s.w_second, s.history
    load_n = pltpu.make_async_copy(noise_hbm, noise, sem.at[76])
    load_f = pltpu.make_async_copy(w_first_hbm, w_first, sem.at[77])
    load_w = pltpu.make_async_copy(w_second_hbm, w_second, sem.at[78])
    load_h = pltpu.make_async_copy(history_hbm, history, sem.at[79])
    load_n.start()
    load_f.start()
    load_w.start()
    load_h.start()
    gen, zdim = noise.shape
    hist, width = history.shape
    hid = w_first.shape[1]
    half = hid // 2
    quarter = half // 2
    gen_total, hist_total = gen * n_row, hist * n_col
    scale = 1.0 / math.sqrt(gen_total)

    me = lax.axis_index("row")
    z = lax.axis_index("col")
    core = lax.rem(me, 2)
    other = 1 - core
    chip = me // 2
    x = lax.rem(chip, nx)
    y = chip // nx
    odd = lax.rem(z, 2) == 1
    sibling = (me + 1 - 2 * core, z)

    barrier = pltpu.get_barrier_semaphore()

    def far(a, n):
        return lax.rem(n // 2 + n * n - a * (a + 1) // 2, n)

    def over_chips(send):
        def step(j, c):
            to_y, to_x = lax.rem(y + far(j // nx, ny), ny), lax.rem(x + far(lax.rem(j, nx), nx), nx)
            send(to_y * nx + to_x, j)
            return c
        lax.fori_loop(0, chips - 1, step, 0)

    def over_row(send):
        def step(j, c):
            k = j // 2
            to_y, to_x = lax.rem(y + far(k // nx, ny), ny), lax.rem(x + far(lax.rem(k, nx), nx), nx)
            send((to_y * nx + to_x) * 2 + lax.rem(core + 1 + j, 2), j)
            return c
        lax.fori_loop(0, n_row - 1, step, 0)

    def over_col(send):
        def step(j, c):
            send(lax.rem(z + n_col // 2 + (j + 1) // 2 * (1 - 2 * lax.rem(j, 2)), n_col), j)
            return c
        lax.fori_loop(0, n_col - 1, step, 0)

    over_col(lambda to, j: pl.semaphore_signal(barrier, inc=1, device_id=(me, to), device_id_type=MESH))
    over_row(lambda to, j: pl.semaphore_signal(barrier, inc=1, device_id=(to, z), device_id_type=MESH))

    def start(src, dst, number, device):
        pltpu.make_async_remote_copy(
            src_ref=src, dst_ref=dst, send_sem=sem.at[2 * number], recv_sem=sem.at[2 * number + 1],
            device_id=device, device_id_type=MESH,
        ).start()

    def wait_bytes(like, index):
        pltpu.make_async_copy(like, like, sem.at[index]).wait()

    flying, landed = {}, {}

    def expect(number, like):
        flying[number] = like

    def arrived(number):
        landed[number] = flying.pop(number)
        wait_bytes(landed[number], 2 * number + 1)

    def finish():
        for number in tuple(flying):
            arrived(number)
        for number, like in landed.items():
            wait_bytes(like, 2 * number)

    def to_row(src, dst, number):
        over_row(lambda to, j: start(src, dst.at[j], number, (to, z)))
        expect(number, dst)

    def to_col(src, dst, number):
        over_col(lambda to, j: start(src, dst.at[j], number, (me, to)))
        expect(number, dst)

    def at(offset, size, unit):
        return pl.ds(offset if isinstance(offset, int) else pl.multiple_of(offset, unit), size)

    def each(count, body):
        lax.fori_loop(0, count, lambda k, c: (body(k), c)[1], 0)

    tiles = [slice(k * LANES, (k + 1) * LANES) for k in range(max(hist, width) // LANES)]
    plan_tiles = tiles[:hist // LANES]
    blocks = gen // LANES

    def block(k):
        return at(k * LANES, LANES, LANES)

    def fold(v):
        return jnp.sum(v.reshape(LANES // 8, 8, LANES), axis=0)

    def squares(ref, rows, across):
        total = jnp.zeros((LANES, LANES), F32)
        for cols in across:
            v = ref[rows, cols].astype(F32)
            total = total + v * v
        return total

    def rows_from_column(column, dst, total):
        for k in range(dst.shape[0]):
            turned = jnp.transpose(column[tiles[k], :])
            dst[k:k + 1, :] = jnp.sum(turned, axis=0, keepdims=True) if total else turned[0:1, :]

    def column_from_rows(rows, column):
        for k in range(rows.shape[0]):
            column[tiles[k], :] = jnp.transpose(jnp.broadcast_to(rows[k:k + 1, :], (LANES, LANES)))

    def dot(a, b):
        return jnp.dot(a, b, preferred_element_type=F32)

    def dot_t(a, b):
        return lax.dot_general(a, b, (((1,), (1,)), ((), ())), preferred_element_type=F32)

    tile_h = min(256, hid)
    tile_g = min(256, width)
    tile_j = min(256, hist)

    load_n.wait()
    load_f.wait()

    for n in range(hid // tile_h):
        cols = slice(n * tile_h, (n + 1) * tile_h)
        preact = dot(noise[...], w_first[:, cols])
        s.mult[:, cols] = preact
        s.hidden[:, cols] = (preact / (1.0 + jnp.exp(-preact))).astype(BF16)

    load_w.wait()

    for n in range(width // tile_g):
        cols = slice(n * tile_g, (n + 1) * tile_g)
        s.surface[:, cols] = dot(s.hidden[...], w_second[:, cols]).astype(BF16)
        for k in range(blocks):
            total = squares(s.surface, tiles[k], tiles[n * tile_g // LANES:(n + 1) * tile_g // LANES])
            s.surf_sq[tiles[k], :] = total if n == 0 else s.surf_sq[tiles[k], :] + total
    s.surf_sq[...] = jnp.broadcast_to(jnp.sum(s.surf_sq[...], axis=1, keepdims=True), (gen, LANES))

    load_h.wait()
    for n in range(hist // tile_j):
        wide = slice(n * tile_j, (n + 1) * tile_j)
        s.plan[:, wide] = dot_t(s.surface[...], history[wide, :])
        for c in range(n * tile_j // LANES, (n + 1) * tile_j // LANES):
            top = None
            for k in range(blocks):
                cost = (s.surf_sq[tiles[k], :] - 2.0 * s.plan[tiles[k], tiles[c]]) * (1.0 / width)
                scores = cost * (-1.0 / EPSILON)
                s.plan[tiles[k], tiles[c]] = scores
                tall = jnp.max(scores.reshape(LANES // 8, 8, LANES), axis=0)
                top = tall if top is None else jnp.maximum(top, tall)
            top = jnp.max(top, axis=0, keepdims=True)
            total = jnp.zeros((8, LANES), F32)
            for k in range(blocks):
                total = total + fold(jnp.exp(s.plan[tiles[k], tiles[c]] - top))
            s.m_lse[c:c + 1, :] = top + jnp.log(jnp.sum(total, axis=0, keepdims=True))

    pl.semaphore_wait(barrier, n_row - 1 + n_col - 1)
    to_row(s.m_lse, s.m_lse_in, 0)

    def hist_w_tile(n):
        rows = at(n * 256, min(256, hist), min(256, hist))
        prod = dot_t(history[rows, :], w_second[...])
        hi = prod.astype(BF16)
        s.hist_w_hi[rows, :] = hi
        s.hist_w_lo[rows, :] = (prod - hi.astype(F32)).astype(BF16)
    each(hist // min(256, hist), hist_w_tile)

    def hist_squares(k):
        s.hist_sq[pl.ds(k, 1), :] = jnp.sum(
            jnp.transpose(squares(history, block(k), tiles[:width // LANES])), axis=0, keepdims=True)
    each(hist // LANES, hist_squares)
    hist_cost = s.hist_sq[...] * (1.0 / width) * (1.0 / EPSILON)

    arrived(0)
    top = jnp.maximum(jnp.max(s.m_lse_in[...], axis=0), s.m_lse[...])
    total = jnp.sum(jnp.exp(s.m_lse_in[...] - top[None]), axis=0) + jnp.exp(s.m_lse[...] - top)
    g_first = math.log(gen_total) - (top + jnp.log(total) - hist_cost)
    s.m_row[0] = g_first - hist_cost

    def row_tops(k):
        rows = block(k)
        top = s.plan[rows, plan_tiles[0]] + s.m_row[0, 0:1, :]
        for n, cols in enumerate(plan_tiles[1:], 1):
            top = jnp.maximum(top, s.plan[rows, cols] + s.m_row[0, n:n + 1, :])
        s.row_a[rows, :] = top
    for k in range(blocks):
        row_tops(k)
    s.row_a[...] = jnp.broadcast_to(jnp.max(s.row_a[...], axis=1, keepdims=True), (gen, LANES))

    def first_rows(k):
        rows = block(k)
        top, total = s.row_a[rows, :], jnp.zeros((LANES, LANES), F32)
        for n, cols in enumerate(plan_tiles):
            grown = jnp.exp(s.plan[rows, cols] + s.m_row[0, n:n + 1, :] - top)
            s.plan[rows, cols] = grown
            total = total + grown
        s.row_b[rows, :] = total
    for k in range(blocks):
        first_rows(k)
    rows_from_column(s.row_a, s.row_top, False)
    rows_from_column(s.row_b, s.row_lse, True)
    s.row_lse[...] = s.row_top[...] + jnp.log(s.row_lse[...])
    to_col(s.row_lse, s.row_lse_in, 1)

    def surf_w_tile(n):
        cols = at(n * tile_h, tile_h, tile_h)
        s.surf_w[:, cols] = dot_t(s.surface[...], w_second[cols, :])
    each(hid // tile_h, surf_w_tile)
    s.hidden_t[...] = jnp.transpose(s.hidden[...].astype(F32)).astype(BF16)

    pair = at(lax.div(z, 2) * LANES, LANES, LANES)
    prod = dot(s.hidden_t[...], s.surface[:, pair])
    turned = pltpu.roll(prod, 64, axis=1)
    s.term_a[...] = jnp.where(odd, turned, prod)
    s.term_b[...] = jnp.where(odd, prod, turned)
    low = lax.broadcasted_iota(jnp.int32, (8, LANES), 1) < 64

    def owner_term(o):
        oc, ox, oy = lax.rem(o, 2), lax.rem(o // 2, nx), o // (2 * nx)
        upper = oc * half + oy * (quarter // ny) + ox * 8
        lower = oc * half + quarter + ox * (quarter // nx) + oy * 8
        s.term[o] = jnp.where(low, s.term_a[at(upper, 8, 8), :], s.term_b[at(lower, 8, 8), :])
    each(n_row, owner_term)

    over_row(lambda to, j: start(s.term.at[to], s.term_in.at[j], 6, (to, z)))
    expect(6, s.term_in)

    arrived(1)
    top = jnp.maximum(jnp.max(s.row_lse_in[...], axis=0), s.row_lse[...])
    total = jnp.sum(jnp.exp(s.row_lse_in[...] - top[None]), axis=0) + jnp.exp(s.row_lse[...] - top)
    column_from_rows(jnp.exp(s.row_top[...] - top) / total, s.row_a)

    def column_sums(scaled, dst):
        def step(k, sums):
            rows, out = block(k), []
            own = s.row_a[rows, :]
            for cols, total in zip(plan_tiles, sums):
                v = s.plan[rows, cols] * own
                if scaled:
                    s.plan[rows, cols] = v
                out.append(total + fold(v))
            return tuple(out)
        sums = [jnp.zeros((8, LANES), F32) for _ in plan_tiles]
        for k in range(blocks):
            sums = step(k, sums)
        for k, total in enumerate(sums):
            dst[k:k + 1, :] = jnp.sum(total, axis=0, keepdims=True)

    def row_sums(k):
        rows = block(k)
        total = jnp.zeros((LANES, LANES), F32)
        for n, cols in enumerate(plan_tiles):
            total = total + s.plan[rows, cols] * s.col_b[n:n + 1, :]
        s.row_b[rows, :] = total

    def unscaled_rows(k):
        rows = block(k)
        for n, cols in enumerate(plan_tiles):
            v = s.plan[rows, cols] * s.col_b[n:n + 1, :]
            s.plan[rows, cols] = v
            hi = v.astype(BF16)
            s.plan_hi[rows, cols] = hi
            s.plan_lo[rows, cols] = (v - hi.astype(F32)).astype(BF16)

    def value_tile(n):
        cols = at(n * tile_h, tile_h, tile_h)
        s.value[:, cols] = (dot(s.plan_hi[...], s.hist_w_hi[:, cols]) + dot(s.plan_hi[...], s.hist_w_lo[:, cols])
                            + dot(s.plan_lo[...], s.hist_w_hi[:, cols]))

    for sweep in range(1, SWEEPS):
        number = 2 * sweep
        mine, theirs = s.m_row.at[sweep], s.m_row_in.at[sweep - 1]
        column_sums(sweep == 1, mine)
        to_row(mine, theirs, number)
        if sweep == 1:
            preact = s.mult[...]
            sigma = 1.0 / (1.0 + jnp.exp(-preact))
            s.mult[...] = sigma * (1.0 + preact * (1.0 - sigma))
            s.noise_t[...] = jnp.transpose(noise[...].astype(F32)).astype(BF16)
        arrived(number)
        total = mine[...] + jnp.sum(theirs[...], axis=0)
        s.col_b[...] = (gen_total / hist_total) / total

        for k in range(blocks):
            row_sums(k)
        mine, theirs = s.m_col.at[sweep - 1], s.m_col_in.at[sweep - 1]
        rows_from_column(s.row_b, mine, True)
        to_col(mine, theirs, number + 1)
        if sweep == SWEEPS - 1:
            for k in range(blocks):
                unscaled_rows(k)
            each(hid // tile_h, value_tile)
        arrived(number + 1)
        total = mine[...] + jnp.sum(theirs[...], axis=0)
        column_from_rows(1.0 / total, s.row_a)

    for k in range(blocks):
        for cols in tiles[:hid // LANES]:
            rows = tiles[k]
            d_hidden = (s.surf_w[rows, cols] * (1.0 / n_col) - s.value[rows, cols] * s.row_a[rows, :]) * scale
            d_preact = d_hidden * s.mult[rows, cols]
            hi = d_preact.astype(BF16)
            s.d_hi[rows, cols] = hi
            s.d_lo[rows, cols] = (d_preact - hi.astype(F32)).astype(BF16)
    s.first[...] = dot(s.noise_t[...], s.d_hi[...]) + dot(s.noise_t[...], s.d_lo[...])
    start(s.first.at[:, at(other * half, half, half)], s.first_in, 8, sibling)
    expect(8, s.first_in)
    piece = zdim // chips

    def send_pieces():
        arrived(8)
        s.first_half[...] = s.first[:, at(core * half, half, half)] + s.first_in[...]
        over_chips(lambda to, j: start(
            s.first_half.at[at(to * piece, piece, 8), :], s.first_chip_in.at[j], 11, (to * 2 + core, z)))
        expect(11, s.first_chip_in)

    def weight_rows(k):
        rows = block(k)
        own = s.row_a[rows, :]
        for cols in plan_tiles:
            s.weights[rows, cols] = (s.plan[rows, cols] * own).astype(BF16)
    for k in range(blocks):
        weight_rows(k)

    def acc_tile(which):
        rows = at(which * half, half, half)

        def body(n):
            cols = at(n * tile_j, tile_j, tile_j)
            s.acc[rows, cols] = dot(s.hidden_t[rows, :], s.weights[:, cols])
        each(hist // tile_j, body)

    span_x, span_y = quarter // nx, quarter // ny
    base_u, base_l = core * half, core * half + quarter
    acc_tile(other)
    order = [pair for k in range(1, nx) for pair in ((True, k), (False, k))] + [(True, 0), (False, 0)]

    def block_rows(upper, k):
        return lax.rem(y + k, ny) * span_y if upper else quarter + lax.rem(x + k, nx) * span_x

    for n, (upper, k) in enumerate(order):
        rows = block_rows(upper, k)
        start(s.acc.at[at(other * half + rows, span_x, 8), :], s.acc_in.at[at(rows, span_x, 8), :], 20 + n, sibling)
        expect(20 + n, s.acc_in.at[at(n * span_x, span_x, 8), :])

    def chip_at(upper, k, first):
        if upper == first:
            return (y * nx + lax.rem(x + k, nx)) * 2 + core, lax.rem(x + k, nx) * 8
        return (lax.rem(y + k, ny) * nx + x) * 2 + core, lax.rem(y + k, ny) * 8

    def pass_on(n):
        upper, k = order[n]
        rows = block_rows(upper, k)
        arrived(20 + n)
        mine = at(core * half + rows, span_x, 8)
        s.acc[mine, :] = s.acc[mine, :] + s.acc_in[at(rows, span_x, 8), :]
        into = s.x_in if upper else s.y_in
        for j in range(1, nx):
            device, offset = chip_at(upper, j, True)
            start(s.acc.at[at(core * half + rows + offset, 8, 8), :], into.at[k, j - 1], 30 + n, (device, z))
        expect(30 + n, into.at[k])

    def pass_second(n):
        upper, k = order[n]
        arrived(30 + n)
        rows = at(core * half + block_rows(upper, k) + chip_at(upper, 0, True)[1], 8, 8)
        total = s.acc[rows, :] + jnp.sum((s.x_in if upper else s.y_in)[k], axis=0)
        if k == 0:
            return total
        s.acc[rows, :] = total
        into = s.y_in2 if upper else s.x_in2
        start(s.acc.at[rows, :], into.at[k - 1], 13 if upper else 14, (chip_at(upper, k, False)[0], z))

    send_pieces()
    acc_tile(core)

    for n in range(len(order)):
        pass_on(n)

    arrived(11)
    s.first_piece[0] = s.first_half[at(chip * piece, piece, 8), :] + jnp.sum(s.first_chip_in[...], axis=0)
    to_col(s.first_piece.at[0], s.first_z_in, 12)
    for n in range(len(order) - 2):
        pass_second(n)
    expect(13, s.y_in2)
    expect(14, s.x_in2)
    own_u, own_l = pass_second(len(order) - 2), pass_second(len(order) - 1)
    arrived(13)
    arrived(14)
    s.reduced[0:8, :] = own_u + jnp.sum(s.y_in2[...], axis=0)
    s.reduced[8:16, :] = own_l + jnp.sum(s.x_in2[...], axis=0)

    hi = s.reduced[...].astype(BF16)
    lo = (s.reduced[...] - hi.astype(F32)).astype(BF16)
    both = jnp.concatenate([hi, lo], axis=0)

    low = lax.broadcasted_iota(jnp.int32, (8, LANES), 1) < 64
    for n in range(width // tile_g):
        prod = dot(both, history[:, n * tile_g:(n + 1) * tile_g])
        prod = prod[0:16] + prod[16:32]
        for c in range(tile_g // LANES):
            upper, lower = prod[0:8, tiles[c]], prod[8:16, tiles[c]]
            k = 2 * (n * tile_g // LANES + c)
            s.slices[k] = jnp.where(low, upper, pltpu.roll(lower, 64, axis=1))
            s.slices[k + 1] = jnp.where(low, pltpu.roll(upper, 64, axis=1), lower)

    over_col(lambda to, j: start(s.slices.at[to], s.slices_in.at[j], 15, (me, to)))
    expect(15, s.slices_in)

    arrived(12)
    s.first_all[me] = s.first_piece[0] + jnp.sum(s.first_z_in[...], axis=0)
    over_row(lambda to, j: start(s.first_all.at[me], s.first_all.at[me], 16, (to, z)))
    expect(16, s.first_all.at[pl.ds(0, n_row - 1)])

    arrived(6)
    term = s.term[me] + jnp.sum(s.term_in[...], axis=0)
    arrived(15)
    mixed = s.slices[z] + jnp.sum(s.slices_in[...], axis=0)
    s.second_all[me] = (term - mixed) * scale

    over_row(lambda to, j: start(s.second_all.at[me], s.second_all.at[me], 17, (to, z)))
    expect(17, s.second_all.at[pl.ds(0, n_row - 1)])

    arrived(16)
    for k in range(chips):
        for c in range(2):
            out_first[k * piece:(k + 1) * piece, c * half:(c + 1) * half] = s.first_all[2 * k + c]
    arrived(17)
    out_second[...] = s.second_all[...]
    finish()


def place(geometry, first, second, out_first, out_second, wide):
    out_first[...] = first[...]
    ny, nx, nz = geometry
    half = wide.shape[0] // 2
    quarter = half // 2
    for y in range(ny):
        for x in range(nx):
            chip = y * nx + x
            for c in range(2):
                upper = c * half + y * (quarter // ny) + x * 8
                lower = c * half + quarter + x * (quarter // nx) + y * 8
                v = second[2 * chip + c]
                wide[upper:upper + 8, :] = v
                wide[lower:lower + 8, :] = pltpu.roll(v, 64, axis=1)
    for k in range(wide.shape[0] // LANES):
        out_second[:, k * LANES:(k + 1) * LANES] = jnp.transpose(wide[k * LANES:(k + 1) * LANES, :])[0:64, :]


def shards(geometry, noise, w_first, w_second, history):
    ny, nx, nz = geometry
    chips = ny * nx
    n_row = 2 * chips
    gen, zdim = noise.shape
    hist, width = history.shape
    hid = w_first.shape[1]
    half, quarter = hid // 2, hid // 4
    piece = zdim // chips
    jr, ir = hist // LANES, gen // LANES
    shapes = dict(
        noise=((gen, zdim), BF16), w_first=((zdim, hid), BF16), w_second=((hid, width), BF16), history=((hist, width), BF16),
        hidden=((gen, hid), BF16), hidden_t=((hid, gen), BF16), noise_t=((zdim, gen), BF16),
        surface=((gen, width), BF16), mult=((gen, hid), F32), surf_w=((gen, hid), F32),
        hist_w_hi=((hist, hid), BF16), hist_w_lo=((hist, hid), BF16),
        plan=((gen, hist), F32), weights=((gen, hist), BF16),
        surf_sq=((gen, LANES), F32), hist_sq=((jr, LANES), F32),
        row_a=((gen, LANES), F32), row_b=((gen, LANES), F32), col_b=((jr, LANES), F32),
        m_lse=((jr, LANES), F32), m_lse_in=((n_row - 1, jr, LANES), F32),
        row_top=((ir, LANES), F32), row_lse=((ir, LANES), F32), row_lse_in=((nz - 1, ir, LANES), F32),
        plan_hi=((gen, hist), BF16), plan_lo=((gen, hist), BF16), value=((gen, hid), F32),
        d_hi=((gen, hid), BF16), d_lo=((gen, hid), BF16),
        m_row=((SWEEPS, jr, LANES), F32), m_row_in=((SWEEPS - 1, n_row - 1, jr, LANES), F32),
        m_col=((SWEEPS - 1, ir, LANES), F32), m_col_in=((SWEEPS - 1, nz - 1, ir, LANES), F32),
        acc=((hid, hist), F32), acc_in=((half, hist), F32),
        x_in=((ny, nx - 1, 8, hist), F32), y_in=((nx, ny - 1, 8, hist), F32),
        x_in2=((nx - 1, 8, hist), F32), y_in2=((ny - 1, 8, hist), F32), reduced=((16, hist), F32),
        first=((zdim, hid), F32), first_in=((zdim, half), F32), first_half=((zdim, half), F32),
        first_chip_in=((chips - 1, piece, half), F32), first_piece=((1, piece, half), F32),
        first_z_in=((nz - 1, piece, half), F32), first_all=((n_row, piece, half), F32),
        term_a=((hid, LANES), F32), term_b=((hid, LANES), F32),
        term=((n_row, 8, LANES), F32), term_in=((n_row - 1, 8, LANES), F32),
        slices=((nz, 8, LANES), F32), slices_in=((nz - 1, 8, LANES), F32),
        second_all=((n_row, 8, LANES), F32),
    )
    scratch = [pltpu.VMEM(*shape) for shape in shapes.values()] + [pltpu.SemaphoreType.DMA((80,))]
    vmem = pl.BlockSpec(memory_space=pltpu.VMEM)
    first, second = pl.pallas_call(
        functools.partial(kernel, geometry, tuple(shapes)),
        out_shape=(
            jax.ShapeDtypeStruct((zdim, hid), F32),
            jax.ShapeDtypeStruct((n_row, 8, LANES), F32),
        ),
        in_specs=[pl.BlockSpec(memory_space=pl.ANY)] * 4,
        out_specs=(vmem, vmem),
        scratch_shapes=scratch,
        compiler_params=pltpu.CompilerParams(
            collective_id=0, has_side_effects=True, vmem_limit_bytes=56 * 1024 * 1024
        ),
        name="transport",
    )(noise, w_first, w_second, history)
    grad_first, turned = pl.pallas_call(
        functools.partial(place, geometry),
        out_shape=(
            jax.ShapeDtypeStruct((zdim, hid), F32),
            jax.ShapeDtypeStruct((width // nz, hid), F32),
        ),
        in_specs=[vmem] * 2,
        out_specs=(vmem, vmem),
        scratch_shapes=[pltpu.VMEM((hid, LANES), F32)],
        name="place",
    )(first, second)
    return grad_first, turned.T


def solution(mesh):
    chips = mesh.shape["row"] // 2
    nx = math.isqrt(chips)
    geometry = (chips // nx, nx, mesh.shape["col"])
    placed = (P("row", None), P(), P(), P("col", None))
    return jax.shard_map(
        functools.partial(shards, geometry), mesh=mesh, in_specs=placed,
        out_specs=(P(), P(None, "col")), check_vma=False,
    )
```
